256 devices in a mesh: dp: 8 (over y, z_hi), tile: 32 (over x, z_lo, core).
Axes of the slice: x: 4, y: 4, z: 8 (z_hi: 2, z_lo: 4; z = z_hi * 4 + z_lo), core: 2. Of those that a mesh axis runs over, the one named last changes fastest.
Arguments:
- videos: bfloat16 [8, 32, 32, 64, 512], P('dp', 'tile'), may hold values from -6 to 6
- spatial_filter: bfloat16 [9, 512, 512], P(None, 'dp'), may hold values from -0.09375 to 0.09375
- temporal_filter: bfloat16 [3, 512, 512], P(None, 'dp'), may hold values from -0.15625 to 0.15625
- spatial_bias: float32 [512], replicated, may hold values from -3 to 3
- temporal_bias: float32 [512], replicated, may hold values from -3 to 3
Outputs:
- output: bfloat16 [8, 32, 32, 64, 512], P('dp', 'tile')
The draws below stay inside these ranges and needn't reach their ends.
All inputs are finite; a program needn't handle non-finite values.
Results may differ from the reference program's by a relative error of at most 0.0044.
Values may be sent and summed in bfloat16 or wider, within the bound.
A program may use at most 128 MiB of HBM per device.

```python
import jax
import jax.numpy as jnp
from jax import lax

C = 512
HH = 32
WW = 64
SAMPLES = 8
FRAMES = 32


def block_levels(own_key, shape, split, smallest, largest):
    factor_of, own = 1.0, jax.random.fold_in(own_key, 6)
    for axis_at, blocks in split:
        steps = jnp.exp(jax.random.uniform(jax.random.fold_in(own, axis_at), (blocks,), jnp.float32, smallest / len(split), largest / len(split)))
        factor_of = factor_of * jnp.repeat(steps, shape[axis_at] // blocks).reshape([-1 if axis == axis_at else 1 for axis in range(len(shape))])
    return factor_of


def bell_draw(key, extent, spread, most, pieces=(), dtype=jnp.bfloat16):
    gain = block_levels(key, extent, pieces, -0.22, 0.18) if pieces else 1.0
    entries = jax.random.normal(key, extent, jnp.float32) * spread * gain
    return jnp.minimum(jnp.maximum(entries, -most), most).astype(dtype)


def setup_inputs(seed: int = 0) -> dict:
    key_list = jax.random.split(jax.random.key(seed), 6)
    return {
        "videos": bell_draw(key_list[0], (SAMPLES, FRAMES, HH, WW, C), 1.0, 6.0, ((0, 8), (1, 32))),
        "spatial_filter": bell_draw(key_list[1], (9, C, C), (9 * C) ** -0.5, 0.09375, ((1, 8),)),
        "temporal_filter": bell_draw(key_list[2], (3, C, C), (3 * C) ** -0.5, 0.15625, ((1, 8),)),
        "spatial_bias": bell_draw(key_list[3], (C,), 0.5, 3.0, (), jnp.float32),
        "temporal_bias": bell_draw(key_list[4], (C,), 0.5, 3.0, (), jnp.float32),
    }


def reference(videos, spatial_filter, temporal_filter, spatial_bias, temporal_bias):
    def one_sample(video):
        frames, height, breadth, channels = video.shape
        padded = jnp.pad(video, ((0, 0), (1, 1), (1, 1), (0, 0)))
        summed = jnp.zeros((frames * height * breadth, channels), jnp.float32)
        for row_off in range(3):
            for col_off in range(3):
                window = padded[:, row_off:row_off + height, col_off:col_off + breadth, :].reshape(-1, channels)
                summed = summed + jnp.dot(window, spatial_filter[3 * row_off + col_off], preferred_element_type=jnp.float32)
        hidden = jax.nn.silu(summed + spatial_bias).astype(jnp.bfloat16).reshape(frames, height, breadth, channels)
        framed = jnp.pad(hidden, ((1, 1), (0, 0), (0, 0), (0, 0)))
        result = jnp.zeros((frames * height * breadth, channels), jnp.float32)
        for lag in range(3):
            window = framed[lag:lag + frames].reshape(-1, channels)
            result = result + jnp.dot(window, temporal_filter[lag], preferred_element_type=jnp.float32)
        return (result + temporal_bias).astype(jnp.bfloat16).reshape(video.shape)

    return lax.map(one_sample, videos)
```

```python
import functools

import jax
import jax.numpy as jnp
from jax import lax
from jax.experimental import pallas as pl
from jax.experimental.pallas import tpu as pltpu
from jax.sharding import PartitionSpec as P

WIDTHS = (128, 128, 256)
ROWS = 256
TAPS_S, TAPS_T = 9, 3


def kernel(dims, vid_hbm, ws_hbm, wt_hbm, sb_ref, tb_ref, out_hbm, xcat, *rest):
    nb = len(WIDTHS)
    height, breadth, chans, shard = dims
    pixels = height * breadth
    chunks = pixels // ROWS
    wbuf = rest[:nb]
    wt = rest[nb]
    own = rest[nb + 1 : 2 * nb + 1]
    before = rest[2 * nb + 1 : 3 * nb + 1]
    after = rest[3 * nb + 1 : 4 * nb + 1]
    acc, outv, local_sem, wsend, wrecv, hsend, hrecv, osem = rest[4 * nb + 1 :]
    offs = [sum(WIDTHS[:b]) for b in range(nb)]
    half = shard // 2
    quarter = half // 2

    dp, t = lax.axis_index("dp"), lax.axis_index("tile")
    tiles = lax.axis_size("tile")
    y, zh = dp // 2, dp % 2
    core = t % 2
    zl = (t // 2) % 4
    partner = t + 1 - 2 * core
    y_up, y_dn, y_far = (y + 1) % 4, (y + 3) % 4, (y + 2) % 4
    up, dn = y_up * 2 + zh, y_dn * 2 + zh
    other = y * 2 + 1 - zh
    first, last = zl == 0, zl == 3
    edge = jnp.logical_or(first, last)
    base = t - zl * 2
    cross_tile = base + jnp.where(first, 6, 0)
    inward_tile = base + jnp.where(first, 2, 4)
    inward_back = base + jnp.where(zl == 1, 0, 6)
    has_before, has_after = t > 0, t < tiles - 1

    def remote(src, dst, ssem, rsem, to_dp, to_tile):
        return pltpu.make_async_remote_copy(
            src_ref=src, dst_ref=dst, send_sem=ssem, recv_sem=rsem,
            device_id={"dp": to_dp, "tile": to_tile}, device_id_type=pl.DeviceIdType.MESH,
        )

    vid_copy = pltpu.make_async_copy(
        vid_hbm, xcat.at[pl.ds(breadth, pixels), pl.ds(chans, chans)], local_sem.at[0]
    )
    groups = [(ws_hbm, wbuf[b], offs[b], WIDTHS[b]) for b in range(nb)] + [(wt_hbm, wt, 0, chans)]
    loads = []
    for g, (src, buf, off, width) in enumerate(groups):
        mine = pl.multiple_of(dp * shard, shard)
        loads.append(
            pltpu.make_async_copy(
                src.at[:, :, pl.ds(off, width)], buf.at[:, pl.ds(mine, shard), :], local_sem.at[1 + g]
            )
        )
    loads[0].start()
    vid_copy.start()
    for c in loads[1:]:
        c.start()

    barrier = pltpu.get_barrier_semaphore()

    def greet(to_dp, to_tile):
        pl.semaphore_signal(
            barrier, inc=1, device_id={"dp": to_dp, "tile": to_tile}, device_id_type=pl.DeviceIdType.MESH
        )

    greet(dp, partner)
    greet(up, t)
    greet(dn, t)

    @pl.when(edge)
    def _():
        greet(other, cross_tile)
        greet(dp, inward_tile)

    @pl.when(jnp.logical_not(edge))
    def _():
        greet(dp, inward_back)

    @pl.when(has_before)
    def _():
        greet(dp, t - 1)

    @pl.when(has_after)
    def _():
        greet(dp, t + 1)

    one = lambda flag: jnp.where(flag, 1, 0)
    pl.semaphore_wait(barrier, 4 + one(edge) + one(has_before) + one(has_after))

    def piece(g, shard_id, low, count):
        start = pl.multiple_of(shard_id * shard + low, quarter)
        return groups[g][1].at[:, pl.ds(start, count), :]

    def wcopy(g, slot, shard_id, low, count, to_dp, to_tile):
        ref = piece(g, shard_id, low, count)
        return remote(ref, ref, wsend.at[g, slot], wrecv.at[g, slot], to_dp, to_tile)

    my_low = core * half
    def far(y_at, zh_at):
        return y_at * 2 + zh_at

    def sends_y(g, first_slot, shard_id, dst_zh):
        wcopy(g, first_slot, shard_id, my_low, half, up, t).start()
        wcopy(g, first_slot + 1, shard_id, my_low, half, dn, t).start()

    def to_partner(g, k, shard_id):
        wcopy(g, 9 + k, shard_id, my_low, half, dp, partner).start()

    def stage_start(g):
        loads[g].wait()

        @pl.when(edge)
        def _():
            wcopy(g, 0, dp, my_low, half, other, cross_tile).start()

        sends_y(g, 1, dp, zh)

    def stage_z(g):
        wcopy(g, 0, other, my_low, half, dp, t).wait_recv()

        @pl.when(edge)
        def _():
            ref = piece(g, other, my_low, half)
            remote(ref, ref, wsend.at[g, 16], wrecv.at[g, 0], dp, inward_tile).start()

        sends_y(g, 3, other, 1 - zh)
        to_partner(g, 0, other)

    def stage_y(g, which):
        z_at = zh if which == 0 else 1 - zh
        slot = 1 + 2 * which
        from_dn, from_up = far(y_dn, z_at), far(y_up, z_at)
        wcopy(g, slot, from_dn, my_low, half, dp, t).wait_recv()
        wcopy(g, 5 + 2 * which, from_dn, my_low, quarter, up, t).start()
        to_partner(g, 1 + 2 * which, from_dn)
        wcopy(g, slot + 1, from_up, my_low, half, dp, t).wait_recv()
        wcopy(g, 6 + 2 * which, from_up, my_low + quarter, quarter, dn, t).start()
        to_partner(g, 2 + 2 * which, from_up)

    def stage_far(g):
        for which in range(2):
            shard_id = far(y_far, zh if which == 0 else 1 - zh)
            wcopy(g, 5 + 2 * which, shard_id, my_low, quarter, dp, t).wait_recv()
            wcopy(g, 6 + 2 * which, shard_id, my_low + quarter, quarter, dp, t).wait_recv()
            to_partner(g, 5 + which, shard_id)

    def partner_ids():
        return [
            other, far(y_dn, zh), far(y_up, zh), far(y_dn, 1 - zh), far(y_up, 1 - zh),
            far(y_far, zh), far(y_far, 1 - zh),
        ]

    def stage_done(g):
        for k, shard_id in enumerate(partner_ids()):
            wcopy(g, 9 + k, shard_id, (1 - core) * half, half, dp, t).wait_recv()

    def wait_sends(g):
        @pl.when(edge)
        def _():
            wcopy(g, 0, dp, my_low, half, other, cross_tile).wait_send()
            wcopy(g, 16, other, my_low, half, dp, inward_tile).wait_send()

        for slot in range(1, 5):
            wcopy(g, slot, dp, my_low, half, up, t).wait_send()
        for slot in range(5, 9):
            wcopy(g, slot, dp, my_low, quarter, up, t).wait_send()
        for k in range(7):
            wcopy(g, 9 + k, dp, my_low, half, dp, partner).wait_send()

    def hcopy(b, i, side):
        rows = pl.ds(pl.multiple_of(i * ROWS, ROWS), ROWS)
        slot = b * chunks + i
        if side == 0:
            return remote(own[b].at[rows], after[b].at[rows], hsend.at[0, slot], hrecv.at[0, slot], dp, t - 1)
        return remote(own[b].at[rows], before[b].at[rows], hsend.at[1, slot], hrecv.at[1, slot], dp, t + 1)

    def send_hidden(b, i):
        @pl.when(has_before)
        def _():
            hcopy(b, i, 0).start()

        @pl.when(has_after)
        def _():
            hcopy(b, i, 1).start()

    def spatial(b, i):
        width = WIDTHS[b]
        total = None
        for dy in range(3):
            start = pl.multiple_of(i * ROWS + dy * breadth, breadth)
            lhs = xcat[pl.ds(start, ROWS), :]
            rhs = wbuf[b][3 * dy : 3 * dy + 3].reshape(3 * chans, width)
            part = jnp.dot(lhs, rhs, preferred_element_type=jnp.float32)
            total = part if total is None else total + part
        total = total + sb_ref[:, offs[b] : offs[b] + width]
        hidden = total / (1.0 + jnp.exp(-total))
        own[b][pl.ds(pl.multiple_of(i * ROWS, ROWS), ROWS), :] = hidden.astype(jnp.bfloat16)

    stage_start(0)

    zeros = jnp.zeros((breadth, 3 * chans), jnp.bfloat16)
    xcat[0:breadth, :] = zeros
    xcat[breadth + pixels :, :] = zeros
    vid_copy.wait()

    @pl.loop(0, height)
    def _(r):
        rows = pl.ds(pl.multiple_of((r + 1) * breadth, breadth), breadth)
        line = xcat[rows, chans : 2 * chans].astype(jnp.float32)
        at = lax.broadcasted_iota(jnp.int32, (breadth, chans), 0)
        left = jnp.where(at == 0, 0.0, pltpu.roll(line, 1, 0))
        right = jnp.where(at == breadth - 1, 0.0, pltpu.roll(line, breadth - 1, 0))
        xcat[rows, 0:chans] = left.astype(jnp.bfloat16)
        xcat[rows, 2 * chans : 3 * chans] = right.astype(jnp.bfloat16)

    stage_z(0)
    stage_y(0, 0)
    stage_y(0, 1)
    stage_start(1)
    stage_far(0)
    stage_done(0)

    for b in range(nb):
        more = b + 1 <= nb

        @pl.loop(0, chunks)
        def _(i, b=b):
            spatial(b, i)

            @pl.when(i > 0)
            def _():
                send_hidden(b, i - 1)

            if b > 0:
                @pl.when(i == 0)
                def _():
                    send_hidden(b - 1, chunks - 1)

            g = b + 1

            @pl.when(i == chunks // 4 - 1)
            def _():
                stage_z(g)

            @pl.when(i == chunks // 2 - 1)
            def _():
                stage_y(g, 0)

            @pl.when(i == chunks // 2)
            def _():
                stage_y(g, 1)

            if g < nb:
                @pl.when(i == chunks // 2 + 1)
                def _():
                    stage_start(g + 1)

            @pl.when(i == chunks - 2)
            def _():
                stage_far(g)

        stage_done(b + 1)

    def temporal_own(i):
        rows = pl.ds(pl.multiple_of(i * ROWS, ROWS), ROWS)
        total = tb_ref[...]
        for b in range(nb):
            total = total + jnp.dot(
                own[b][rows, :], wt[1, offs[b] : offs[b] + WIDTHS[b], :], preferred_element_type=jnp.float32
            )
        acc[rows, :] = total

    temporal_own(0)
    send_hidden(nb - 1, chunks - 1)

    @pl.loop(1, chunks)
    def _(i):
        temporal_own(i)

    for b in range(nb):
        @pl.loop(0, chunks)
        def _(i, b=b):
            rows = pl.ds(pl.multiple_of(i * ROWS, ROWS), ROWS)
            span = slice(offs[b], offs[b] + WIDTHS[b])

            @pl.when(has_before)
            def _():
                hcopy(b, i, 1).wait_recv()
                acc[rows, :] += jnp.dot(before[b][rows, :], wt[0, span, :], preferred_element_type=jnp.float32)

            @pl.when(has_after)
            def _():
                hcopy(b, i, 0).wait_recv()
                acc[rows, :] += jnp.dot(after[b][rows, :], wt[2, span, :], preferred_element_type=jnp.float32)

            if b == nb - 1:
                outv[rows, :] = acc[rows, :].astype(jnp.bfloat16)
                pltpu.make_async_copy(outv.at[rows], out_hbm.at[rows], osem.at[i]).start()

    for g in range(nb + 1):
        wait_sends(g)

    @pl.loop(0, chunks)
    def _(i):
        for b in range(nb):
            @pl.when(has_before)
            def _():
                hcopy(b, i, 0).wait_send()

            @pl.when(has_after)
            def _():
                hcopy(b, i, 1).wait_send()

        rows = pl.ds(pl.multiple_of(i * ROWS, ROWS), ROWS)
        pltpu.make_async_copy(outv.at[rows], out_hbm.at[rows], osem.at[i]).wait()


def per_device(videos, spatial_filter, temporal_filter, spatial_bias, temporal_bias):
    _, _, height, breadth, chans = videos.shape
    shard = spatial_filter.shape[1]
    pixels = height * breadth
    nb = len(WIDTHS)
    chunks = pixels // ROWS
    bf = jnp.bfloat16
    hid = [pltpu.VMEM((pixels, w), bf) for w in WIDTHS]
    anywhere = pl.BlockSpec(memory_space=pl.ANY)
    vmem = pl.BlockSpec(memory_space=pltpu.VMEM)
    out = pl.pallas_call(
        functools.partial(kernel, (height, breadth, chans, shard)),
        out_shape=jax.ShapeDtypeStruct((pixels, chans), bf),
        in_specs=[anywhere, anywhere, anywhere, vmem, vmem],
        out_specs=anywhere,
        scratch_shapes=[
            pltpu.VMEM((pixels + 2 * breadth, 3 * chans), bf),
            *[pltpu.VMEM((TAPS_S, chans, w), bf) for w in WIDTHS],
            pltpu.VMEM((TAPS_T, chans, chans), bf),
            *hid, *hid, *hid,
            pltpu.VMEM((pixels, chans), jnp.float32),
            pltpu.VMEM((pixels, chans), bf),
            pltpu.SemaphoreType.DMA((nb + 2,)),
            pltpu.SemaphoreType.DMA((nb + 1, 17)),
            pltpu.SemaphoreType.DMA((nb + 1, 17)),
            pltpu.SemaphoreType.DMA((2, nb * chunks)),
            pltpu.SemaphoreType.DMA((2, nb * chunks)),
            pltpu.SemaphoreType.DMA((chunks,)),
        ],
        compiler_params=pltpu.CompilerParams(
            collective_id=0, has_side_effects=True, vmem_limit_bytes=56 * 1024 * 1024
        ),
    )(
        videos.reshape(pixels, chans),
        spatial_filter,
        temporal_filter,
        spatial_bias.reshape(1, chans),
        temporal_bias.reshape(1, chans),
    )
    return out.reshape(videos.shape)


def solution(mesh):
    return jax.shard_map(
        per_device,
        mesh=mesh,
        in_specs=(
            P("dp", "tile", None, None, None),
            P(None, "dp", None),
            P(None, "dp", None),
            P(),
            P(),
        ),
        out_specs=P("dp", "tile", None, None, None),
        check_vma=False,
    )
```

```python
import functools

import jax
import jax.numpy as jnp
from jax import lax
from jax.experimental import pallas as pl
from jax.experimental.pallas import tpu as pltpu
from jax.sharding import PartitionSpec as P

BLOCK = 128
ROWS = 512
TAPS_S, TAPS_T = 9, 3
MESH = pl.DeviceIdType.MESH


def kernel(
    dims, vid_hbm, ws_hbm, wt_hbm, sb_ref, tb_ref, out_hbm,
    xcat, wb, wt, own, before, after, acc, outv,
    local_sem, wsend, wrecv, xsend, xrecv, psend, precv, hsend, hrecv, osem,
):
    height, breadth, chans, shard = dims
    pixels = height * breadth
    chunks = pixels // ROWS
    blocks = chans // BLOCK
    half = shard // 2

    dp, t = lax.axis_index("dp"), lax.axis_index("tile")
    tiles = lax.axis_size("tile")
    y, zh = dp // 2, dp % 2
    core, zl, x = t % 2, (t // 2) % 4, t // 8
    partner = t + 1 - 2 * core
    up, dn = ((y + 1) % 4) * 2 + zh, ((y + 3) % 4) * 2 + zh
    other = y * 2 + 1 - zh
    first, last = zl == 0, zl == 3
    edge = jnp.logical_or(first, last)
    base = t - zl * 2
    cross_tile = base + jnp.where(first, 6, 0)
    inward_tile = base + jnp.where(first, 2, 4)
    inward_back = base + jnp.where(zl == 1, 0, 6)
    x_next, x_prev = (t + 8) % tiles, (t + tiles - 8) % tiles
    has_before, has_after = t > 0, t < tiles - 1
    is_one = core == 1
    is_zero = core == 0

    block_a, block_b, block_c, block_d = x, (x + 2) % 4, (x + 1) % 4, (x + 3) % 4
    carried = jnp.where(is_zero, zh, 1 - zh)

    def shard_of(k, z_at):
        return ((y + k) % 4) * 2 + z_at

    def remote(src, dst, ssem, rsem, to_dp, to_tile):
        return pltpu.make_async_remote_copy(
            src_ref=src, dst_ref=dst, send_sem=ssem, recv_sem=rsem,
            device_id={"dp": to_dp, "tile": to_tile}, device_id_type=MESH,
        )

    mine = pl.ds(pl.multiple_of(dp * shard, shard), shard)

    def columns(j):
        return pl.ds(pl.multiple_of(j * BLOCK, BLOCK), BLOCK)

    def load_block(n, j):
        return pltpu.make_async_copy(ws_hbm.at[:, :, columns(j)], wb.at[j, :, mine, :], local_sem.at[n])

    vid_copy = pltpu.make_async_copy(
        vid_hbm, xcat.at[pl.ds(breadth, pixels), pl.ds(chans, chans)], local_sem.at[5]
    )
    loads = [load_block(n, j) for n, j in enumerate((block_a, block_b, block_c, block_d))]
    loads.append(pltpu.make_async_copy(wt_hbm, wt.at[:, mine, :], local_sem.at[4]))
    for n in (0, 1, 4):
        loads[n].start()
    vid_copy.start()
    for n in (2, 3):
        loads[n].start()

    barrier = pltpu.get_barrier_semaphore()

    def greet(to_dp, to_tile):
        pl.semaphore_signal(barrier, inc=1, device_id={"dp": to_dp, "tile": to_tile}, device_id_type=MESH)

    greet(dp, partner)
    greet(up, t)
    greet(dn, t)
    greet(dp, x_next)
    greet(dp, x_prev)

    @pl.when(edge)
    def _():
        greet(other, cross_tile)
        greet(dp, inward_tile)

    @pl.when(jnp.logical_not(edge))
    def _():
        greet(dp, inward_back)

    @pl.when(has_before)
    def _():
        greet(dp, t - 1)

    @pl.when(has_after)
    def _():
        greet(dp, t + 1)

    one = lambda flag: jnp.where(flag, 1, 0)
    pl.semaphore_wait(barrier, 6 + one(edge) + one(has_before) + one(has_after))

    bufs = [wb.at[block_a], wb.at[block_b], wt]

    def piece(g, shard_id, low=0, count=None):
        count = shard if count is None else count
        start = pl.multiple_of(shard_id * shard + low, half)
        return bufs[g].at[:, pl.ds(start, count), :]

    def ring(g, send, recv, shard_id, to_dp, to_tile, low=0, count=None):
        ref = piece(g, shard_id, low, count)
        return remote(ref, ref, wsend.at[g, send], wrecv.at[g, recv], to_dp, to_tile)

    def from_x(n, k, shard_id, to_tile):
        ref = wb.at[block_a, :, pl.ds(pl.multiple_of(shard_id * shard, shard), shard), :]
        return remote(ref, ref, xsend.at[n, k], xrecv.at[n, k], dp, to_tile)

    def spread(g, k):
        shard_id = shard_of(k, carried)
        ring(g, 6 + k, 5 + k, shard_id, dp, partner).start()
        if g == 0:
            from_x(0, k, shard_id, x_next).start()
            from_x(1, k, shard_id, x_prev).start()

    def start_z(g):
        @pl.when(jnp.logical_and(is_one, edge))
        def _():
            ring(g, 0, 0, dp, other, cross_tile).start()

    def start_y(g):
        shard_id = shard_of(0, carried)
        ring(g, 2, 1, shard_id, up, t).start()
        ring(g, 3, 2, shard_id, dn, t).start()

    def stage_z(g):
        @pl.when(is_one)
        def _():
            ring(g, 0, 0, other, dp, t).wait_recv()
            start_y(g)

            @pl.when(edge)
            def _():
                ring(g, 1, 0, other, dp, inward_tile).start()

            spread(g, 0)

    def stage_y(g):
        from_dn, from_up = shard_of(3, carried), shard_of(1, carried)
        ring(g, 2, 1, from_dn, up, t).wait_recv()
        ring(g, 4, 3, from_dn, up, t, 0, half).start()
        ring(g, 3, 2, from_up, dn, t).wait_recv()
        ring(g, 5, 4, from_up, dn, t, half, half).start()
        spread(g, 3)
        spread(g, 1)

    def stage_far(g):
        far = shard_of(2, carried)
        ring(g, 4, 3, far, up, t, 0, half).wait_recv()
        ring(g, 5, 4, far, dn, t, half, half).wait_recv()
        spread(g, 2)

    def stage_done(g):
        for k in range(4):
            wait = ring(g, 6 + k, 5 + k, shard_of(k, 1 - carried), dp, partner).wait_recv
            if k == 0:
                pl.when(is_zero)(wait)
            else:
                wait()

    def x_piece(n, k, shard_id):
        block = block_d if n == 0 else block_c
        ref = wb.at[block, :, pl.ds(pl.multiple_of(shard_id * shard, shard), shard), :]
        arrived = remote(ref, ref, xsend.at[n, k], xrecv.at[n, k], dp, x_next)
        onward = remote(ref, ref, psend.at[n, k], precv.at[n, k], dp, partner)
        return arrived, onward

    def stage_x(k):
        def run():
            for n in range(2):
                arrived, onward = x_piece(n, k, shard_of(k, carried))
                arrived.wait_recv()
                onward.start()

        if k == 0:
            pl.when(is_one)(run)
        else:
            run()

    def stage_x_done():
        for k in range(4):
            def run():
                for n in range(2):
                    x_piece(n, k, shard_of(k, 1 - carried))[1].wait_recv()

            if k == 0:
                pl.when(is_zero)(run)
            else:
                run()

    def wait_sends():
        for g in range(3):
            @pl.when(jnp.logical_and(is_one, edge))
            def _():
                ring(g, 0, 0, dp, other, cross_tile).wait_send()
                ring(g, 1, 0, dp, dp, inward_tile).wait_send()

            for slot in (2, 3):
                ring(g, slot, 0, dp, up, t).wait_send()
            for slot in (4, 5):
                ring(g, slot, 0, dp, up, t, 0, half).wait_send()
            for k in range(4):
                def run():
                    ring(g, 6 + k, 5 + k, dp, dp, partner).wait_send()
                    if g == 0:
                        for n in range(2):
                            from_x(n, k, dp, x_next).wait_send()
                            x_piece(n, k, dp)[1].wait_send()

                if k == 0:
                    pl.when(is_one)(run)
                else:
                    run()

    def rows_of(i):
        return pl.ds(pl.multiple_of(i * ROWS, ROWS), ROWS)

    def hcopy(j, i, side):
        slot = j * chunks + i
        src = own.at[j, rows_of(i), :]
        if side == 0:
            return remote(src, after.at[j, rows_of(i), :], hsend.at[0, slot], hrecv.at[0, slot], dp, t - 1)
        return remote(src, before.at[j, rows_of(i), :], hsend.at[1, slot], hrecv.at[1, slot], dp, t + 1)

    def send_hidden(pair, i):
        for j in pair:
            @pl.when(has_before)
            def _():
                hcopy(j, i, 0).start()

            @pl.when(has_after)
            def _():
                hcopy(j, i, 1).start()

    def spatial(pair, i):
        total = None
        for dy in range(3):
            start = pl.multiple_of(i * ROWS + dy * breadth, breadth)
            lhs = xcat[pl.ds(start, ROWS), :]
            rhs = jnp.concatenate(
                [wb[j, 3 * dy : 3 * dy + 3].reshape(3 * chans, BLOCK) for j in pair], axis=1
            )
            part = jnp.dot(lhs, rhs, preferred_element_type=jnp.float32)
            total = part if total is None else total + part
        total = total + jnp.concatenate([sb_ref[j] for j in pair], axis=1)
        hidden = (total / (1.0 + jnp.exp(-total))).astype(jnp.bfloat16)
        for n, j in enumerate(pair):
            own[j, rows_of(i), :] = hidden[:, n * BLOCK : (n + 1) * BLOCK]

    start_z_all = lambda: [start_z(g) for g in range(3)]
    loads[0].wait()
    start_z(0)
    pl.when(is_zero)(lambda: start_y(0))
    loads[1].wait()
    start_z(1)
    pl.when(is_zero)(lambda: start_y(1))
    loads[4].wait()
    start_z(2)

    zeros = jnp.zeros((breadth, 3 * chans), jnp.bfloat16)
    xcat[0:breadth, :] = zeros
    xcat[breadth + pixels :, :] = zeros
    vid_copy.wait()

    @pl.loop(0, height)
    def _(r):
        rows = pl.ds(pl.multiple_of((r + 1) * breadth, breadth), breadth)
        line = xcat[rows, chans : 2 * chans].astype(jnp.float32)
        at = lax.broadcasted_iota(jnp.int32, (breadth, chans), 0)
        left = jnp.where(at == 0, 0.0, pltpu.roll(line, 1, 0))
        right = jnp.where(at == breadth - 1, 0.0, pltpu.roll(line, breadth - 1, 0))
        xcat[rows, 0:chans] = left.astype(jnp.bfloat16)
        xcat[rows, 2 * chans : 3 * chans] = right.astype(jnp.bfloat16)

    stage_z(0)
    stage_y(0)
    stage_z(1)
    stage_far(0)
    stage_y(1)
    stage_far(1)
    pl.when(is_zero)(lambda: start_y(2))
    stage_done(0)
    stage_done(1)
    loads[2].wait()
    loads[3].wait()

    pair_0, pair_1 = (block_a, block_b), (block_c, block_d)

    @pl.loop(0, chunks)
    def _(i):
        spatial(pair_0, i)

        @pl.when(i > 0)
        def _():
            send_hidden(pair_0, i - 1)

        @pl.when(i == 0)
        def _():
            stage_x(0)
            stage_x(3)
            stage_x(1)

        @pl.when(i == 1)
        def _():
            stage_z(2)
            stage_x(2)

        @pl.when(i == 2)
        def _():
            stage_y(2)

    stage_x_done()

    @pl.loop(0, chunks)
    def _(i):
        spatial(pair_1, i)

        @pl.when(i == 0)
        def _():
            send_hidden(pair_0, chunks - 1)
            stage_far(2)

        @pl.when(i > 0)
        def _():
            send_hidden(pair_1, i - 1)

    stage_done(2)

    def taps(lag, j):
        return wt[lag, pl.ds(pl.multiple_of(j * BLOCK, BLOCK), BLOCK), :]

    def temporal(lag, src, pair, i):
        lhs = jnp.concatenate([src[j, rows_of(i), :] for j in pair], axis=1)
        rhs = jnp.concatenate([taps(lag, j) for j in pair], axis=0)
        return jnp.dot(lhs, rhs, preferred_element_type=jnp.float32)

    def temporal_own(i):
        acc[rows_of(i), :] = temporal(1, own, pair_0, i) + temporal(1, own, pair_1, i) + tb_ref[...]

    temporal_own(0)
    send_hidden(pair_1, chunks - 1)

    @pl.loop(1, chunks)
    def _(i):
        temporal_own(i)

    x_before, x_after = (t + tiles - 1) % tiles // 8, (t + 1) % tiles // 8
    for p in range(2):
        @pl.loop(0, chunks)
        def _(i, p=p):
            rows = rows_of(i)

            @pl.when(has_before)
            def _():
                pair = ((x_before + p) % 4, (x_before + p + 2) % 4)
                for j in pair:
                    hcopy(j, i, 1).wait_recv()
                acc[rows, :] += temporal(0, before, pair, i)

            @pl.when(has_after)
            def _():
                pair = ((x_after + p) % 4, (x_after + p + 2) % 4)
                for j in pair:
                    hcopy(j, i, 0).wait_recv()
                acc[rows, :] += temporal(2, after, pair, i)

            if p == 1:
                outv[rows, :] = acc[rows, :].astype(jnp.bfloat16)
                pltpu.make_async_copy(outv.at[rows], out_hbm.at[rows], osem.at[i]).start()

    wait_sends()

    @pl.loop(0, chunks)
    def _(i):
        for j in range(blocks):
            @pl.when(has_before)
            def _():
                hcopy(j, i, 0).wait_send()

            @pl.when(has_after)
            def _():
                hcopy(j, i, 1).wait_send()

        pltpu.make_async_copy(outv.at[rows_of(i)], out_hbm.at[rows_of(i)], osem.at[i]).wait()


def per_device(videos, spatial_filter, temporal_filter, spatial_bias, temporal_bias):
    _, _, height, breadth, chans = videos.shape
    shard = spatial_filter.shape[1]
    pixels = height * breadth
    blocks = chans // BLOCK
    chunks = pixels // ROWS
    bf = jnp.bfloat16
    anywhere = pl.BlockSpec(memory_space=pl.ANY)
    vmem = pl.BlockSpec(memory_space=pltpu.VMEM)
    dma = pltpu.SemaphoreType.DMA
    out = pl.pallas_call(
        functools.partial(kernel, (height, breadth, chans, shard)),
        out_shape=jax.ShapeDtypeStruct((pixels, chans), bf),
        in_specs=[anywhere, anywhere, anywhere, vmem, vmem],
        out_specs=anywhere,
        scratch_shapes=[
            pltpu.VMEM((pixels + 2 * breadth, 3 * chans), bf),
            pltpu.VMEM((blocks, TAPS_S, chans, BLOCK), bf),
            pltpu.VMEM((TAPS_T, chans, chans), bf),
            pltpu.VMEM((blocks, pixels, BLOCK), bf),
            pltpu.VMEM((blocks, pixels, BLOCK), bf),
            pltpu.VMEM((blocks, pixels, BLOCK), bf),
            pltpu.VMEM((pixels, chans), jnp.float32),
            pltpu.VMEM((pixels, chans), bf),
            dma((6,)),
            dma((3, 10)), dma((3, 9)),
            dma((2, 4)), dma((2, 4)),
            dma((2, 4)), dma((2, 4)),
            dma((2, blocks * chunks)), dma((2, blocks * chunks)),
            dma((chunks,)),
        ],
        compiler_params=pltpu.CompilerParams(
            collective_id=0, has_side_effects=True, vmem_limit_bytes=56 * 1024 * 1024
        ),
    )(
        videos.reshape(pixels, chans),
        spatial_filter,
        temporal_filter,
        spatial_bias.reshape(blocks, 1, BLOCK),
        temporal_bias.reshape(1, chans),
    )
    return out.reshape(videos.shape)


def solution(mesh):
    return jax.shard_map(
        per_device,
        mesh=mesh,
        in_specs=(
            P("dp", "tile", None, None, None),
            P(None, "dp", None),
            P(None, "dp", None),
            P(),
            P(),
        ),
        out_specs=P("dp", "tile", None, None, None),
        check_vma=False,
    )
```

```python
import functools

import jax
import jax.numpy as jnp
from jax import lax
from jax.experimental import pallas as pl
from jax.experimental.pallas import tpu as pltpu
from jax.sharding import PartitionSpec as P

BLOCK = 128
ROWS = 512
FAR_CHUNKS = 3
TAPS_S, TAPS_T = 9, 3
MESH = pl.DeviceIdType.MESH


def kernel(
    dims, vid_hbm, ws_hbm, wt_hbm, sb_ref, tb_ref, out_hbm,
    xcat, xcat_far, vid_far, wb, wt, own, near, acc, outv,
    local_sem, wsend, wrecv, xsend, xrecv, psend, precv, hsend, hrecv, vsem, osem,
):
    height, breadth, chans, shard = dims
    pixels = height * breadth
    chunks = pixels // ROWS
    blocks = chans // BLOCK
    group = chans // 2
    half = shard // 2

    dp, t = lax.axis_index("dp"), lax.axis_index("tile")
    tiles = lax.axis_size("tile")
    y, zh = dp // 2, dp % 2
    core, zl, x = t % 2, (t // 2) % 4, t // 8
    partner = t + 1 - 2 * core
    up, dn = ((y + 1) % 4) * 2 + zh, ((y + 3) % 4) * 2 + zh
    other = y * 2 + 1 - zh
    first, last = zl == 0, zl == 3
    edge = jnp.logical_or(first, last)
    base = t - zl * 2
    cross_edge = base + jnp.where(first, 6, 0)
    cross_inner = base + jnp.where(first, 4, 2)
    inner_source = base + jnp.where(zl == 1, 6, 0)
    x_next, x_prev = (t + 8) % tiles, (t + tiles - 8) % tiles
    has_before, has_after = t > 0, t < tiles - 1
    far_before = jnp.logical_and(t % 8 == 0, has_before)
    far_after = jnp.logical_and(t % 8 == 7, has_after)
    far_any = jnp.logical_or(far_before, far_after)
    far_side = jnp.where(far_after, 1, 0)
    far_tile = jnp.where(far_after, t + 1, t - 1)
    is_one = core == 1
    is_zero = core == 0

    block_a, block_b, block_c, block_d = x, (x + 2) % 4, (x + 1) % 4, (x + 3) % 4
    carried = jnp.where(is_zero, zh, 1 - zh)

    def remote(src, dst, ssem, rsem, to_dp, to_tile):
        return pltpu.make_async_remote_copy(
            src_ref=src, dst_ref=dst, send_sem=ssem, recv_sem=rsem,
            device_id={"dp": to_dp, "tile": to_tile}, device_id_type=MESH,
        )

    def columns(j):
        return pl.ds(pl.multiple_of(j * BLOCK, BLOCK), BLOCK)

    def block_piece(j, y_at, z_at, low=0, count=None):
        count = shard if count is None else count
        return wb.at[j, z_at, :, pl.ds(pl.multiple_of(y_at * shard + low, half), count), :]

    def piece(g, y_at, z_at, low=0, count=None):
        if g < 2:
            return block_piece((block_a, block_b)[g], y_at, z_at, low, count)
        count = shard if count is None else count
        return wt.at[:, pl.ds(pl.multiple_of((y_at * 2 + z_at) * shard + low, half), count), :]

    def source(g):
        return wt_hbm if g == 2 else ws_hbm.at[:, :, columns((block_a, block_b)[g])]

    vid_copy = pltpu.make_async_copy(vid_hbm, outv, local_sem.at[5])
    loads = [
        pltpu.make_async_copy(ws_hbm.at[:, :, columns(j)], block_piece(j, y, zh), local_sem.at[n])
        for n, j in enumerate((block_a, block_b, block_c, block_d))
    ]
    loads.append(pltpu.make_async_copy(wt_hbm, piece(2, y, zh), local_sem.at[4]))
    vid_copy.start()
    for load in loads:
        load.start()

    barrier = pltpu.get_barrier_semaphore()

    def greet(to_dp, to_tile):
        pl.semaphore_signal(barrier, inc=1, device_id={"dp": to_dp, "tile": to_tile}, device_id_type=MESH)

    greet(dp, partner)
    greet(up, t)
    greet(dn, t)
    greet(dp, x_next)
    greet(dp, x_prev)

    @pl.when(edge)
    def _():
        greet(other, cross_edge)
        greet(other, cross_inner)

    @pl.when(jnp.logical_not(edge))
    def _():
        greet(other, inner_source)

    @pl.when(has_before)
    def _():
        greet(dp, t - 1)

    @pl.when(has_after)
    def _():
        greet(dp, t + 1)

    one = lambda flag: jnp.where(flag, 1, 0)
    pl.semaphore_wait(barrier, 6 + one(edge) + one(has_before) + one(has_after))

    def ring(g, send, recv, y_at, z_at, to_dp, to_tile, low=0, count=None, src=None):
        ref = piece(g, y_at, z_at, low, count)
        return remote(ref if src is None else src, ref, wsend.at[g, send], wrecv.at[g, recv], to_dp, to_tile)

    def from_x(n, k, y_at, to_tile):
        ref = block_piece(block_a, y_at, carried)
        return remote(ref, ref, xsend.at[n, k], xrecv.at[n, k], dp, to_tile)

    def y_of(k):
        return (y + k) % 4

    def spread(g, k):
        ring(g, 6 + k, 5 + k, y_of(k), carried, dp, partner).start()
        if g == 0:
            from_x(0, k, y_of(k), x_next).start()
            from_x(1, k, y_of(k), x_prev).start()

    def start_z(g):
        ring(g, 1, 0, y, zh, other, cross_inner, src=source(g)).start()
        ring(g, 0, 0, y, zh, other, cross_edge, src=source(g)).start()

    def start_y(g, src=None):
        ring(g, 2, 1, y, carried, up, t, src=src).start()
        ring(g, 3, 2, y, carried, dn, t, src=src).start()

    def stage_z(g):
        ring(g, 0, 0, y, 1 - zh, dp, partner).wait_recv()
        start_y(g)
        spread(g, 0)

    def stage_y(g):
        ring(g, 2, 1, y_of(3), carried, up, t).wait_recv()
        ring(g, 4, 3, y_of(3), carried, up, t, 0, half).start()
        ring(g, 3, 2, y_of(1), carried, dn, t).wait_recv()
        ring(g, 5, 4, y_of(1), carried, dn, t, half, half).start()
        spread(g, 3)
        spread(g, 1)

    def stage_far(g):
        ring(g, 4, 3, y_of(2), carried, up, t, 0, half).wait_recv()
        ring(g, 5, 4, y_of(2), carried, dn, t, half, half).wait_recv()
        spread(g, 2)

    def stage_done(g, ks):
        for k in ks:
            ring(g, 6 + k, 5 + k, y_of(k), 1 - carried, dp, partner).wait_recv()

    def onward(n, k, z_at):
        ref = block_piece((block_d, block_c)[n], y_of(k), z_at)
        return remote(ref, ref, psend.at[n, k], precv.at[n, k], dp, partner)

    def stage_x(k):
        for n in range(2):
            ref = block_piece((block_d, block_c)[n], y_of(k), carried)
            remote(ref, ref, xsend.at[n, k], xrecv.at[n, k], dp, x_next).wait_recv()
            onward(n, k, carried).start()

    def stage_x_done(ks):
        for k in ks:
            for n in range(2):
                onward(n, k, 1 - carried).wait_recv()

    def wait_sends():
        for g in range(3):
            @pl.when(jnp.logical_and(is_one, edge))
            def _():
                ring(g, 0, 0, y, zh, other, cross_edge).wait_send()
                ring(g, 1, 0, y, zh, other, cross_inner).wait_send()

            for slot in (2, 3):
                ring(g, slot, 0, y, carried, up, t).wait_send()
            for slot in (4, 5):
                ring(g, slot, 0, y, carried, up, t, 0, half).wait_send()
            for k in range(4):
                def run():
                    ring(g, 6 + k, 5 + k, y, carried, dp, partner).wait_send()
                    if g == 0:
                        for n in range(2):
                            from_x(n, k, y, x_next).wait_send()
                            onward(n, k, carried).wait_send()

                if k == 0:
                    pl.when(is_one)(run)
                else:
                    run()

    def rows_of(i):
        return pl.ds(pl.multiple_of(i * ROWS, ROWS), ROWS)

    def hcopy(j, i, side):
        slot = j * chunks + i
        return remote(
            own.at[j, rows_of(i), :], near.at[1 - side, j, rows_of(i), :],
            hsend.at[side, slot], hrecv.at[side, slot], dp, t - 1 if side == 0 else t + 1,
        )

    def exchanged(side, i):
        there, far = ((has_before, far_before), (has_after, far_after))[side]
        return jnp.logical_and(there, jnp.logical_not(jnp.logical_and(far, i < FAR_CHUNKS)))

    def send_hidden(pair, i):
        for side in range(2):
            @pl.when(exchanged(side, i))
            def _():
                for j in pair:
                    hcopy(j, i, side).start()

    far_rows = (FAR_CHUNKS * ROWS // breadth + 1) * breadth
    far_copy = remote(vid_hbm.at[pl.ds(0, far_rows)], vid_far, vsem.at[0], vsem.at[1], dp, far_tile)

    def prepare(src, dst, lines):
        lanes = lax.broadcasted_iota(jnp.int32, (breadth, BLOCK), 1)
        at = lax.broadcasted_iota(jnp.int32, (breadth, group), 0)

        @pl.loop(0, lines)
        def _(r):
            line = src[pl.ds(pl.multiple_of(r * breadth, breadth), breadth), :].astype(jnp.float32)
            rows = pl.ds(pl.multiple_of((r + 1) * breadth, breadth), breadth)
            parts = [line[:, n * BLOCK : (n + 1) * BLOCK] for n in range(blocks)]
            turned = [pltpu.roll(part, shard, 1) for part in parts]
            low = lanes < shard
            for z_at in range(2):
                left_of, right_of = (parts, turned) if z_at == 0 else (turned, parts)
                mid = jnp.concatenate(
                    [jnp.where(low, left_of[n], right_of[n + 1]) for n in range(0, blocks, 2)], axis=1
                )
                left = jnp.where(at == 0, 0.0, pltpu.roll(mid, 1, 0))
                right = jnp.where(at == breadth - 1, 0.0, pltpu.roll(mid, breadth - 1, 0))
                for dx, value in enumerate((left, mid, right)):
                    start = (3 * z_at + dx) * group
                    dst[rows, start : start + group] = value.astype(jnp.bfloat16)

    def half_dot(xs, z_at, pair, i):
        total = None
        for dy in range(3):
            start = pl.multiple_of(i * ROWS + dy * breadth, breadth)
            lhs = xs[pl.ds(start, ROWS), pl.ds(pl.multiple_of(z_at * (3 * group), 3 * group), 3 * group)]
            rhs = jnp.concatenate(
                [wb[j, z_at, 3 * dy : 3 * dy + 3].reshape(3 * group, BLOCK) for j in pair], axis=1
            )
            part = jnp.dot(lhs, rhs, preferred_element_type=jnp.float32)
            total = part if total is None else total + part
        return total

    def activate(total, pair):
        total = total + jnp.concatenate([sb_ref[j] for j in pair], axis=1)
        return (total / (1.0 + jnp.exp(-total))).astype(jnp.bfloat16)

    pairs = (block_a, block_b), (block_c, block_d)

    def spatial_first(p, i):
        acc[rows_of(i), 2 * BLOCK * p : 2 * BLOCK * (p + 1)] = half_dot(xcat, zh, pairs[p], i)

    def spatial_rest(p, i):
        total = acc[rows_of(i), 2 * BLOCK * p : 2 * BLOCK * (p + 1)] + half_dot(xcat, 1 - zh, pairs[p], i)
        hidden = activate(total, pairs[p])
        for n, j in enumerate(pairs[p]):
            own[j, rows_of(i), :] = hidden[:, n * BLOCK : (n + 1) * BLOCK]

    @pl.when(jnp.logical_and(is_one, edge))
    def _():
        for g in range(3):
            start_z(g)

    @pl.when(is_zero)
    def _():
        start_y(0, source(0))
        start_y(1, source(1))

    @pl.when(far_any)
    def _():
        far_copy.start()

    zeros = jnp.zeros((breadth, 6 * group), jnp.bfloat16)
    xcat[0:breadth, :] = zeros
    xcat[breadth + pixels :, :] = zeros
    vid_copy.wait()
    prepare(outv, xcat, height)
    for load in loads:
        load.wait()

    @pl.when(is_zero)
    def _():
        stage_y(0)
        stage_y(1)
        stage_far(0)
        stage_far(1)
        start_y(2, source(2))

    @pl.when(is_one)
    def _():
        stage_z(0)
        stage_z(1)
        stage_done(0, (1, 2, 3))
        stage_done(1, (1, 2, 3))

    def on(flag, n, at, *stages):
        @pl.when(jnp.logical_and(flag, n == at))
        def _():
            for stage in stages:
                stage()

    @pl.loop(0, chunks)
    def _(n):
        spatial_first(0, chunks - 1 - n)
        on(is_zero, n, 0, lambda: stage_x(3), lambda: stage_x(1))
        on(is_zero, n, 1, lambda: stage_x(2))
        on(is_one, n, 0, lambda: stage_y(0))
        on(is_one, n, 1, lambda: stage_y(1))
        on(is_one, n, 2, lambda: stage_far(0))
        on(is_one, n, 3, lambda: stage_far(1))

    @pl.when(is_one)
    def _():
        stage_x_done((1, 2, 3))

    @pl.loop(0, chunks)
    def _(n):
        spatial_first(1, chunks - 1 - n)
        on(is_zero, n, 1, lambda: stage_y(2))
        on(is_zero, n, 3, lambda: stage_far(2))
        on(is_one, n, 0, lambda: stage_x(0), lambda: stage_x(3))
        on(is_one, n, 1, lambda: stage_x(1))
        on(is_one, n, 2, lambda: stage_x(2))
        on(is_one, n, 3, lambda: stage_z(2))

    @pl.when(is_zero)
    def _():
        stage_done(0, range(4))
        stage_done(1, range(4))

    @pl.loop(0, chunks)
    def _(n):
        spatial_rest(0, chunks - 1 - n)

        @pl.when(n > 0)
        def _():
            send_hidden(pairs[0], chunks - n)

        on(is_one, n, 1, lambda: stage_y(2))
        on(is_one, n, 3, lambda: stage_far(2))

    @pl.when(is_zero)
    def _():
        stage_x_done(range(4))

    @pl.loop(0, chunks)
    def _(n):
        spatial_rest(1, chunks - 1 - n)

        @pl.when(n == 0)
        def _():
            send_hidden(pairs[0], 0)

        @pl.when(n > 0)
        def _():
            send_hidden(pairs[1], chunks - n)

    pl.when(is_zero)(lambda: stage_done(2, range(4)))
    pl.when(is_one)(lambda: stage_done(2, (1, 2, 3)))

    def taps(lag, j):
        return wt[lag, columns(j), :]

    def temporal(lag, ref, pair, i):
        lhs = jnp.concatenate([ref[j, rows_of(i), :] for j in pair], axis=1)
        rhs = jnp.concatenate([taps(lag, j) for j in pair], axis=0)
        return jnp.dot(lhs, rhs, preferred_element_type=jnp.float32)

    @pl.loop(0, chunks)
    def _(n):
        acc[rows_of(n), :] = temporal(1, own, pairs[0], n) + temporal(1, own, pairs[1], n) + tb_ref[...]

        @pl.when(n == 0)
        def _():
            send_hidden(pairs[1], 0)

    @pl.when(far_any)
    def _():
        far_copy.wait()
        xcat_far[0:breadth, :] = zeros
        prepare(vid_far, xcat_far, far_rows // breadth)

        @pl.loop(0, 2 * FAR_CHUNKS)
        def _(n):
            p, i = n // FAR_CHUNKS, n % FAR_CHUNKS
            pair = ((x + p) % 4, (x + p + 2) % 4)
            hidden = activate(half_dot(xcat_far, 0, pair, i) + half_dot(xcat_far, 1, pair, i), pair)
            for m, j in enumerate(pair):
                near[far_side, j, rows_of(i), :] = hidden[:, m * BLOCK : (m + 1) * BLOCK]

    x_before, x_after = (t + tiles - 1) % tiles // 8, (t + 1) % tiles // 8
    for p in range(2):
        @pl.loop(0, chunks)
        def _(n, p=p):
            i = chunks - 1 - n
            rows = rows_of(i)
            for side, there, x_there in ((0, has_before, x_before), (1, has_after, x_after)):
                pair = ((x_there + p) % 4, (x_there + p + 2) % 4)

                @pl.when(exchanged(side, i))
                def _():
                    for j in pair:
                        hcopy(j, i, 1 - side).wait_recv()

                @pl.when(there)
                def _():
                    acc[rows, :] += temporal(2 * side, near.at[side], pair, i)

            if p == 1:
                outv[rows, :] = acc[rows, :].astype(jnp.bfloat16)
                pltpu.make_async_copy(outv.at[rows], out_hbm.at[rows], osem.at[i]).start()

    wait_sends()

    @pl.loop(0, chunks)
    def _(i):
        for side in range(2):
            @pl.when(exchanged(side, i))
            def _():
                for j in range(blocks):
                    hcopy(j, i, side).wait_send()

        pltpu.make_async_copy(outv.at[rows_of(i)], out_hbm.at[rows_of(i)], osem.at[i]).wait()


def per_device(videos, spatial_filter, temporal_filter, spatial_bias, temporal_bias):
    _, _, height, breadth, chans = videos.shape
    shard = spatial_filter.shape[1]
    pixels = height * breadth
    blocks = chans // BLOCK
    chunks = pixels // ROWS
    far_pixels = FAR_CHUNKS * ROWS + breadth
    bf = jnp.bfloat16
    anywhere = pl.BlockSpec(memory_space=pl.ANY)
    vmem = pl.BlockSpec(memory_space=pltpu.VMEM)
    dma = pltpu.SemaphoreType.DMA
    out = pl.pallas_call(
        functools.partial(kernel, (height, breadth, chans, shard)),
        out_shape=jax.ShapeDtypeStruct((pixels, chans), bf),
        in_specs=[anywhere, anywhere, anywhere, vmem, vmem],
        out_specs=anywhere,
        scratch_shapes=[
            pltpu.VMEM((pixels + 2 * breadth, 3 * chans), bf),
            pltpu.VMEM((far_pixels + breadth, 3 * chans), bf),
            pltpu.VMEM((far_pixels, chans), bf),
            pltpu.VMEM((blocks, 2, TAPS_S, chans // 2, BLOCK), bf),
            pltpu.VMEM((TAPS_T, chans, chans), bf),
            pltpu.VMEM((blocks, pixels, BLOCK), bf),
            pltpu.VMEM((2, blocks, pixels, BLOCK), bf),
            pltpu.VMEM((pixels, chans), jnp.float32),
            pltpu.VMEM((pixels, chans), bf),
            dma((6,)),
            dma((3, 10)), dma((3, 9)),
            dma((2, 4)), dma((2, 4)),
            dma((2, 4)), dma((2, 4)),
            dma((2, blocks * chunks)), dma((2, blocks * chunks)),
            dma((2,)),
            dma((chunks,)),
        ],
        compiler_params=pltpu.CompilerParams(
            collective_id=0, has_side_effects=True, vmem_limit_bytes=56 * 1024 * 1024
        ),
    )(
        videos.reshape(pixels, chans),
        spatial_filter,
        temporal_filter,
        spatial_bias.reshape(blocks, 1, BLOCK),
        temporal_bias.reshape(1, chans),
    )
    return out.reshape(videos.shape)


def solution(mesh):
    return jax.shard_map(
        per_device,
        mesh=mesh,
        in_specs=(
            P("dp", "tile", None, None, None),
            P(None, "dp", None),
            P(None, "dp", None),
            P(),
            P(),
        ),
        out_specs=P("dp", "tile", None, None, None),
        check_vma=False,
    )
```

```python
import functools

import jax
import jax.numpy as jnp
from jax import lax
from jax.experimental import pallas as pl
from jax.experimental.pallas import tpu as pltpu
from jax.sharding import PartitionSpec as P

BLOCK = 128
ROWS = 512
FAR_CHUNKS = 3
FAR_PARTS = 1
TAPS_S, TAPS_T = 9, 3
MESH = pl.DeviceIdType.MESH


def kernel(
    dims, vid_hbm, ws_hbm, wt_hbm, sb_ref, tb_ref, out_hbm,
    xcat, xcat_far, vid_far, wb, wt, own, near, acc, outv,
    local_sem, wsend, wrecv, xsend, xrecv, psend, precv, hsend, hrecv, vsem, osem,
):
    height, breadth, chans, shard = dims
    pixels = height * breadth
    chunks = pixels // ROWS
    blocks = chans // BLOCK
    group = chans // 2
    half = shard // 2

    dp, t = lax.axis_index("dp"), lax.axis_index("tile")
    tiles = lax.axis_size("tile")
    y, zh = dp // 2, dp % 2
    core, zl, x = t % 2, (t // 2) % 4, t // 8
    partner = t + 1 - 2 * core
    up, dn = ((y + 1) % 4) * 2 + zh, ((y + 3) % 4) * 2 + zh
    other = y * 2 + 1 - zh
    first, last = zl == 0, zl == 3
    edge = jnp.logical_or(first, last)
    base = t - zl * 2
    cross_edge = base + jnp.where(first, 6, 0)
    cross_inner = base + jnp.where(first, 4, 2)
    inner_source = base + jnp.where(zl == 1, 6, 0)
    x_next, x_prev = (t + 8) % tiles, (t + tiles - 8) % tiles
    has_before, has_after = t > 0, t < tiles - 1
    far_before = jnp.logical_and(t % 8 == 0, has_before)
    far_after = jnp.logical_and(t % 8 == 7, has_after)
    far_any = jnp.logical_or(far_before, far_after)
    far_side = jnp.where(far_after, 1, 0)
    far_tile = jnp.where(far_after, t + 1, t - 1)
    is_one = core == 1
    is_zero = core == 0

    block_a, block_b, block_c, block_d = x, (x + 2) % 4, (x + 1) % 4, (x + 3) % 4
    block_e, cross_e = jnp.where(first, block_d, block_c), jnp.where(first, block_c, block_d)
    ring_blocks = {0: block_a, 1: block_b, 3: block_e}
    carried = jnp.where(is_zero, zh, 1 - zh)

    def remote(src, dst, ssem, rsem, to_dp, to_tile):
        return pltpu.make_async_remote_copy(
            src_ref=src, dst_ref=dst, send_sem=ssem, recv_sem=rsem,
            device_id={"dp": to_dp, "tile": to_tile}, device_id_type=MESH,
        )

    def columns(j):
        return pl.ds(pl.multiple_of(j * BLOCK, BLOCK), BLOCK)

    def block_piece(j, y_at, z_at, low=0, count=None):
        count = shard if count is None else count
        return wb.at[j, z_at, :, pl.ds(pl.multiple_of(y_at * shard + low, half), count), :]

    def piece(g, y_at, z_at, low=0, count=None):
        if g != 2:
            return block_piece(ring_blocks[g], y_at, z_at, low, count)
        count = shard if count is None else count
        return wt.at[:, pl.ds(pl.multiple_of((y_at * 2 + z_at) * shard + low, half), count), :]

    def source(g):
        return wt_hbm if g == 2 else ws_hbm.at[:, :, columns(ring_blocks[g])]

    vid_copy = pltpu.make_async_copy(vid_hbm, outv, local_sem.at[5])
    loads = [
        pltpu.make_async_copy(ws_hbm.at[:, :, columns(j)], block_piece(j, y, zh), local_sem.at[n])
        for n, j in enumerate((block_a, block_b, block_c, block_d))
    ]
    loads.append(pltpu.make_async_copy(wt_hbm, piece(2, y, zh), local_sem.at[4]))
    vid_copy.start()
    for load in loads:
        load.start()

    barrier = pltpu.get_barrier_semaphore()

    def greet(to_dp, to_tile):
        pl.semaphore_signal(barrier, inc=1, device_id={"dp": to_dp, "tile": to_tile}, device_id_type=MESH)

    greet(dp, partner)
    greet(up, t)
    greet(dn, t)
    greet(dp, x_next)
    greet(dp, x_prev)

    @pl.when(edge)
    def _():
        greet(other, cross_edge)
        greet(other, cross_inner)

    @pl.when(jnp.logical_not(edge))
    def _():
        greet(other, inner_source)

    @pl.when(has_before)
    def _():
        greet(dp, t - 1)

    @pl.when(has_after)
    def _():
        greet(dp, t + 1)

    one = lambda flag: jnp.where(flag, 1, 0)
    pl.semaphore_wait(barrier, 6 + one(edge) + one(has_before) + one(has_after))

    def ring(g, send, recv, y_at, z_at, to_dp, to_tile, low=0, count=None, src=None):
        ref = piece(g, y_at, z_at, low, count)
        return remote(ref if src is None else src, ref, wsend.at[g, send], wrecv.at[g, recv], to_dp, to_tile)

    def from_x(n, k, y_at, to_tile):
        ref = block_piece(block_a, y_at, carried)
        return remote(ref, ref, xsend.at[n, k], xrecv.at[n, k], dp, to_tile)

    by_x = jnp.logical_not(first), jnp.logical_not(last)

    def y_of(k):
        return (y + k) % 4

    def spread(g, k):
        ring(g, 6 + k, 5 + k, y_of(k), carried, dp, partner).start()
        if g == 0:
            pl.when(by_x[0])(lambda: from_x(0, k, y_of(k), x_next).start())
            pl.when(by_x[1])(lambda: from_x(1, k, y_of(k), x_prev).start())

    def cross_copy():
        return remote(
            ws_hbm.at[:, :, columns(cross_e)], block_piece(cross_e, y, zh), wsend.at[3, 0], wrecv.at[3, 0],
            other, cross_edge,
        )

    def start_z(g):
        if g == 3:
            cross_copy().start()
            return
        ring(g, 1, 0, y, zh, other, cross_inner, src=source(g)).start()
        ring(g, 0, 0, y, zh, other, cross_edge, src=source(g)).start()

    def start_y(g, src=None):
        ring(g, 2, 1, y, carried, up, t, src=src).start()
        ring(g, 3, 2, y, carried, dn, t, src=src).start()

    def stage_z(g):
        ring(g, 0, 0, y, 1 - zh, dp, partner).wait_recv()
        start_y(g)
        spread(g, 0)

    def stage_y(g):
        ring(g, 2, 1, y_of(3), carried, up, t).wait_recv()
        ring(g, 4, 3, y_of(3), carried, up, t, 0, half).start()
        ring(g, 3, 2, y_of(1), carried, dn, t).wait_recv()
        ring(g, 5, 4, y_of(1), carried, dn, t, half, half).start()
        spread(g, 3)
        spread(g, 1)

    def stage_far(g):
        ring(g, 4, 3, y_of(2), carried, up, t, 0, half).wait_recv()
        ring(g, 5, 4, y_of(2), carried, dn, t, half, half).wait_recv()
        spread(g, 2)

    def stage_done(g, ks):
        for k in ks:
            ring(g, 6 + k, 5 + k, y_of(k), 1 - carried, dp, partner).wait_recv()

    def onward(n, k, z_at):
        ref = block_piece((block_d, block_c)[n], y_of(k), z_at)
        return remote(ref, ref, psend.at[n, k], precv.at[n, k], dp, partner)

    def stage_x(k):
        for n in range(2):
            @pl.when(by_x[n])
            def _():
                ref = block_piece((block_d, block_c)[n], y_of(k), carried)
                remote(ref, ref, xsend.at[n, k], xrecv.at[n, k], dp, x_next).wait_recv()
                onward(n, k, carried).start()

    def stage_x_done(ks):
        for n in range(2):
            @pl.when(by_x[n])
            def _():
                for k in ks:
                    onward(n, k, 1 - carried).wait_recv()

        pl.when(edge)(lambda: stage_done(3, ks))

    def wait_ring(g):
        for slot in (2, 3):
            ring(g, slot, 0, y, carried, up, t).wait_send()
        for slot in (4, 5):
            ring(g, slot, 0, y, carried, up, t, 0, half).wait_send()
        for k in range(1, 4):
            ring(g, 6 + k, 5 + k, y, carried, dp, partner).wait_send()

        @pl.when(is_one)
        def _():
            ring(g, 6, 5, y, carried, dp, partner).wait_send()

    def wait_sends():
        for g in range(3):
            wait_ring(g)
        pl.when(edge)(lambda: wait_ring(3))

        @pl.when(jnp.logical_and(is_one, edge))
        def _():
            for g in range(3):
                ring(g, 0, 0, y, zh, other, cross_edge).wait_send()
                ring(g, 1, 0, y, zh, other, cross_inner).wait_send()
            cross_copy().wait_send()

        def wait_x(n, k):
            from_x(n, k, y, x_next).wait_send()
            onward(n, k, carried).wait_send()

        for n in range(2):
            @pl.when(by_x[n])
            def _():
                for k in range(1, 4):
                    wait_x(n, k)

            pl.when(jnp.logical_and(by_x[n], is_one))(lambda: wait_x(n, 0))

    def rows_of(i):
        return pl.ds(pl.multiple_of(i * ROWS, ROWS), ROWS)

    def hcopy(j, i, side):
        slot = j * chunks + i
        return remote(
            own.at[j, rows_of(i), :], near.at[1 - side, j, rows_of(i), :],
            hsend.at[side, slot], hrecv.at[side, slot], dp, t - 1 if side == 0 else t + 1,
        )

    def exchanged(side, i):
        there, far = ((has_before, far_before), (has_after, far_after))[side]
        return jnp.logical_and(there, jnp.logical_not(jnp.logical_and(far, i < FAR_CHUNKS)))

    def send_hidden(pair, i):
        for side in range(2):
            @pl.when(exchanged(side, i))
            def _():
                for j in pair:
                    hcopy(j, i, side).start()

    far_rows = (FAR_CHUNKS * ROWS // breadth + 1) * breadth
    far_cuts = [far_rows * n // (FAR_PARTS * breadth) * breadth for n in range(FAR_PARTS + 1)]

    def far_copy(n):
        rows = pl.ds(far_cuts[n], far_cuts[n + 1] - far_cuts[n])
        return remote(vid_hbm.at[rows], vid_far.at[rows], vsem.at[0, n], vsem.at[1, n], dp, far_tile)

    def far_start(n):
        pl.when(far_any)(lambda: far_copy(n).start())

    def prepare(src, dst, lines):
        lanes = lax.broadcasted_iota(jnp.int32, (breadth, BLOCK), 1)
        at = lax.broadcasted_iota(jnp.int32, (breadth, group), 0)

        @pl.loop(0, lines)
        def _(r):
            line = src[pl.ds(pl.multiple_of(r * breadth, breadth), breadth), :].astype(jnp.float32)
            rows = pl.ds(pl.multiple_of((r + 1) * breadth, breadth), breadth)
            parts = [line[:, n * BLOCK : (n + 1) * BLOCK] for n in range(blocks)]
            turned = [pltpu.roll(part, shard, 1) for part in parts]
            low = lanes < shard
            for z_at in range(2):
                left_of, right_of = (parts, turned) if z_at == 0 else (turned, parts)
                mid = jnp.concatenate(
                    [jnp.where(low, left_of[n], right_of[n + 1]) for n in range(0, blocks, 2)], axis=1
                )
                left = jnp.where(at == 0, 0.0, pltpu.roll(mid, 1, 0))
                right = jnp.where(at == breadth - 1, 0.0, pltpu.roll(mid, breadth - 1, 0))
                for dx, value in enumerate((left, mid, right)):
                    start = (3 * z_at + dx) * group
                    dst[rows, start : start + group] = value.astype(jnp.bfloat16)

    def half_dot(xs, z_at, pair, i):
        total = None
        for dy in range(3):
            start = pl.multiple_of(i * ROWS + dy * breadth, breadth)
            lhs = xs[pl.ds(start, ROWS), pl.ds(pl.multiple_of(z_at * (3 * group), 3 * group), 3 * group)]
            rhs = jnp.concatenate(
                [wb[j, z_at, 3 * dy : 3 * dy + 3].reshape(3 * group, BLOCK) for j in pair], axis=1
            )
            part = jnp.dot(lhs, rhs, preferred_element_type=jnp.float32)
            total = part if total is None else total + part
        return total

    def activate(total, pair):
        total = total + jnp.concatenate([sb_ref[j] for j in pair], axis=1)
        return (total / (1.0 + jnp.exp(-total))).astype(jnp.bfloat16)

    pairs = (block_a, block_b), (block_c, block_d)

    def spatial_first(p, i):
        acc[rows_of(i), 2 * BLOCK * p : 2 * BLOCK * (p + 1)] = half_dot(xcat, zh, pairs[p], i)

    def spatial_rest(p, i):
        total = acc[rows_of(i), 2 * BLOCK * p : 2 * BLOCK * (p + 1)] + half_dot(xcat, 1 - zh, pairs[p], i)
        hidden = activate(total, pairs[p])
        for n, j in enumerate(pairs[p]):
            own[j, rows_of(i), :] = hidden[:, n * BLOCK : (n + 1) * BLOCK]

    @pl.when(jnp.logical_and(is_one, edge))
    def _():
        for g in (0, 1, 3, 2):
            start_z(g)

    @pl.when(is_zero)
    def _():
        start_y(0, source(0))
        start_y(1, source(1))

    far_start(0)

    zeros = jnp.zeros((breadth, 6 * group), jnp.bfloat16)
    xcat[0:breadth, :] = zeros
    xcat[breadth + pixels :, :] = zeros
    vid_copy.wait()
    prepare(outv, xcat, height)
    for load in loads:
        load.wait()

    @pl.when(is_zero)
    def _():
        stage_y(0)
        stage_y(1)
        stage_far(0)
        stage_far(1)
        pl.when(edge)(lambda: start_y(3, source(3)))

    @pl.when(is_one)
    def _():
        stage_z(0)
        stage_z(1)
        stage_y(0)
        stage_y(1)
        stage_done(0, (1, 2, 3))
        stage_done(1, (1, 2, 3))

    edge_zero, edge_one = jnp.logical_and(edge, is_zero), jnp.logical_and(edge, is_one)

    def on(flag, n, at, *stages):
        @pl.when(jnp.logical_and(flag, n == at))
        def _():
            for stage in stages:
                stage()

    @pl.loop(0, chunks)
    def _(n):
        spatial_first(0, chunks - 1 - n)
        on(is_zero, n, 1, lambda: stage_x(3))
        on(is_zero, n, 2, lambda: stage_x(1))
        on(is_zero, n, 3, lambda: stage_x(2))
        on(is_one, n, 0, lambda: stage_far(0))
        on(is_one, n, 1, lambda: stage_far(1))
        on(edge_one, n, 2, lambda: stage_z(3))

    @pl.when(is_zero)
    def _():
        stage_done(0, range(4))
        stage_done(1, range(4))

    @pl.loop(0, chunks)
    def _(n):
        spatial_rest(0, chunks - 1 - n)

        @pl.when(n > 0)
        def _():
            send_hidden(pairs[0], chunks - n)

        on(is_zero, n, 0, lambda: start_y(2, source(2)))
        on(edge_zero, n, 0, lambda: stage_y(3))
        on(is_one, n, 0, lambda: stage_x(0))
        on(is_one, n, 1, lambda: stage_x(3))
        on(edge_one, n, 1, lambda: stage_y(3))
        on(is_one, n, 2, lambda: stage_x(1))
        on(edge_zero, n, 3, lambda: stage_far(3))

    pl.when(is_one)(lambda: stage_x_done((1, 2, 3)))

    @pl.loop(0, chunks)
    def _(n):
        spatial_first(1, chunks - 1 - n)

        @pl.when(n == 0)
        def _():
            send_hidden(pairs[0], 0)

        on(is_one, n, 0, lambda: stage_x(2))
        on(edge_one, n, 1, lambda: stage_far(3))
        on(is_one, n, 2, lambda: stage_z(2))

    pl.when(is_zero)(lambda: stage_x_done(range(4)))

    @pl.loop(0, chunks)
    def _(n):
        spatial_rest(1, chunks - 1 - n)

        @pl.when(n > 0)
        def _():
            send_hidden(pairs[1], chunks - n)

        on(is_zero, n, 1, lambda: stage_y(2))
        on(is_one, n, 2, lambda: stage_y(2))

    stage_far(2)
    send_hidden(pairs[1], 0)

    @pl.when(far_any)
    def _():
        for n in range(FAR_PARTS):
            far_copy(n).wait()
        xcat_far[0:breadth, :] = zeros
        prepare(vid_far, xcat_far, far_rows // breadth)

        @pl.loop(0, 2 * FAR_CHUNKS)
        def _(n):
            p, i = n // FAR_CHUNKS, n % FAR_CHUNKS
            pair = ((x + p) % 4, (x + p + 2) % 4)
            hidden = activate(half_dot(xcat_far, 0, pair, i) + half_dot(xcat_far, 1, pair, i), pair)
            for m, j in enumerate(pair):
                near[far_side, j, rows_of(i), :] = hidden[:, m * BLOCK : (m + 1) * BLOCK]

    pl.when(is_zero)(lambda: stage_done(2, range(4)))
    pl.when(is_one)(lambda: stage_done(2, (1, 2, 3)))

    def taps(lag, j):
        return wt[lag, columns(j), :]

    def temporal(lag, ref, pair, i):
        lhs = jnp.concatenate([ref[j, rows_of(i), :] for j in pair], axis=1)
        rhs = jnp.concatenate([taps(lag, j) for j in pair], axis=0)
        return jnp.dot(lhs, rhs, preferred_element_type=jnp.float32)

    @pl.loop(0, chunks)
    def _(n):
        acc[rows_of(n), :] = temporal(1, own, pairs[0], n) + temporal(1, own, pairs[1], n) + tb_ref[...]

    x_before, x_after = (t + tiles - 1) % tiles // 8, (t + 1) % tiles // 8
    for p in range(2):
        @pl.loop(0, chunks)
        def _(n, p=p):
            i = chunks - 1 - n
            rows = rows_of(i)
            for side, there, x_there in ((0, has_before, x_before), (1, has_after, x_after)):
                pair = ((x_there + p) % 4, (x_there + p + 2) % 4)

                @pl.when(exchanged(side, i))
                def _():
                    for j in pair:
                        hcopy(j, i, 1 - side).wait_recv()

                @pl.when(there)
                def _():
                    acc[rows, :] += temporal(2 * side, near.at[side], pair, i)

            if p == 1:
                outv[rows, :] = acc[rows, :].astype(jnp.bfloat16)
                pltpu.make_async_copy(outv.at[rows], out_hbm.at[rows], osem.at[i]).start()

    wait_sends()

    @pl.loop(0, chunks)
    def _(i):
        for side in range(2):
            @pl.when(exchanged(side, i))
            def _():
                for j in range(blocks):
                    hcopy(j, i, side).wait_send()

        pltpu.make_async_copy(outv.at[rows_of(i)], out_hbm.at[rows_of(i)], osem.at[i]).wait()


def per_device(videos, spatial_filter, temporal_filter, spatial_bias, temporal_bias):
    _, _, height, breadth, chans = videos.shape
    shard = spatial_filter.shape[1]
    pixels = height * breadth
    blocks = chans // BLOCK
    chunks = pixels // ROWS
    far_pixels = FAR_CHUNKS * ROWS + breadth
    bf = jnp.bfloat16
    anywhere = pl.BlockSpec(memory_space=pl.ANY)
    vmem = pl.BlockSpec(memory_space=pltpu.VMEM)
    dma = pltpu.SemaphoreType.DMA
    out = pl.pallas_call(
        functools.partial(kernel, (height, breadth, chans, shard)),
        out_shape=jax.ShapeDtypeStruct((pixels, chans), bf),
        in_specs=[anywhere, anywhere, anywhere, vmem, vmem],
        out_specs=anywhere,
        scratch_shapes=[
            pltpu.VMEM((pixels + 2 * breadth, 3 * chans), bf),
            pltpu.VMEM((far_pixels + breadth, 3 * chans), bf),
            pltpu.VMEM((far_pixels, chans), bf),
            pltpu.VMEM((blocks, 2, TAPS_S, chans // 2, BLOCK), bf),
            pltpu.VMEM((TAPS_T, chans, chans), bf),
            pltpu.VMEM((blocks, pixels, BLOCK), bf),
            pltpu.VMEM((2, blocks, pixels, BLOCK), bf),
            pltpu.VMEM((pixels, chans), jnp.float32),
            pltpu.VMEM((pixels, chans), bf),
            dma((6,)),
            dma((4, 10)), dma((4, 9)),
            dma((2, 4)), dma((2, 4)),
            dma((2, 4)), dma((2, 4)),
            dma((2, blocks * chunks)), dma((2, blocks * chunks)),
            dma((2, FAR_PARTS)),
            dma((chunks,)),
        ],
        compiler_params=pltpu.CompilerParams(
            collective_id=0, has_side_effects=True, vmem_limit_bytes=56 * 1024 * 1024
        ),
    )(
        videos.reshape(pixels, chans),
        spatial_filter,
        temporal_filter,
        spatial_bias.reshape(blocks, 1, BLOCK),
        temporal_bias.reshape(1, chans),
    )
    return out.reshape(videos.shape)


def solution(mesh):
    return jax.shard_map(
        per_device,
        mesh=mesh,
        in_specs=(
            P("dp", "tile", None, None, None),
            P(None, "dp", None),
            P(None, "dp", None),
            P(),
            P(),
        ),
        out_specs=P("dp", "tile", None, None, None),
        check_vma=False,
    )
```

```python
import functools

import jax
import jax.numpy as jnp
from jax import lax
from jax.experimental import pallas as pl
from jax.experimental.pallas import tpu as pltpu
from jax.sharding import PartitionSpec as P

BLOCK = 128
ROWS = 512
FAR_CHUNKS = 2
FAR_PARTS = 1
TAPS_S, TAPS_T = 9, 3
MESH = pl.DeviceIdType.MESH


def kernel(
    dims, vid_hbm, ws_hbm, wt_hbm, sb_hbm, tb_hbm, outv,
    xcat, xcat_far, vid_far, wb, wt, own, near, acc, sb_ref, tb_ref,
    local_sem, wsend, wrecv, xsend, xrecv, psend, precv, hsend, hrecv, vsem,
):
    height, breadth, chans, shard = dims
    pixels = height * breadth
    chunks = pixels // ROWS
    blocks = chans // BLOCK
    group = chans // 2
    half = shard // 2

    dp, t = lax.axis_index("dp"), lax.axis_index("tile")
    tiles = lax.axis_size("tile")
    y, zh = dp // 2, dp % 2
    core, zl, x = t % 2, (t // 2) % 4, t // 8
    partner = t + 1 - 2 * core
    up, dn = ((y + 1) % 4) * 2 + zh, ((y + 3) % 4) * 2 + zh
    other = y * 2 + 1 - zh
    first, last = zl == 0, zl == 3
    edge = jnp.logical_or(first, last)
    base = t - zl * 2
    cross_edge = base + jnp.where(first, 6, 0)
    cross_inner = base + jnp.where(first, 4, 2)
    inner_source = base + jnp.where(zl == 1, 6, 0)
    x_next, x_prev = (t + 8) % tiles, (t + tiles - 8) % tiles
    has_before, has_after = t > 0, t < tiles - 1
    far_before = jnp.logical_and(t % 8 == 0, has_before)
    far_after = jnp.logical_and(t % 8 == 7, has_after)
    far_any = jnp.logical_or(far_before, far_after)
    far_side = jnp.where(far_after, 1, 0)
    far_tile = jnp.where(far_after, t + 1, t - 1)
    is_one = core == 1
    is_zero = core == 0

    block_a, block_b, block_c, block_d = x, (x + 2) % 4, (x + 1) % 4, (x + 3) % 4
    block_e, cross_e = jnp.where(first, block_d, block_c), jnp.where(first, block_c, block_d)
    ring_blocks = {0: block_a, 1: block_b, 3: block_e}
    carried = jnp.where(is_zero, zh, 1 - zh)

    def remote(src, dst, ssem, rsem, to_dp, to_tile):
        return pltpu.make_async_remote_copy(
            src_ref=src, dst_ref=dst, send_sem=ssem, recv_sem=rsem,
            device_id={"dp": to_dp, "tile": to_tile}, device_id_type=MESH,
        )

    def columns(j):
        return pl.ds(pl.multiple_of(j * BLOCK, BLOCK), BLOCK)

    def block_piece(j, y_at, z_at, low=0, count=None):
        count = shard if count is None else count
        return wb.at[j, z_at, :, pl.ds(pl.multiple_of(y_at * shard + low, half), count), :]

    def piece(g, y_at, z_at, low=0, count=None):
        if g != 2:
            return block_piece(ring_blocks[g], y_at, z_at, low, count)
        count = shard if count is None else count
        return wt.at[:, pl.ds(pl.multiple_of((y_at * 2 + z_at) * shard + low, half), count), :]

    def source(g):
        return wt_hbm if g == 2 else ws_hbm.at[:, :, columns(ring_blocks[g])]

    vid_copy = pltpu.make_async_copy(vid_hbm, outv, local_sem.at[5])
    loads = [
        pltpu.make_async_copy(ws_hbm.at[:, :, columns(j)], block_piece(j, y, zh), local_sem.at[n])
        for n, j in enumerate((block_a, block_b, block_c, block_d))
    ]
    loads.append(pltpu.make_async_copy(wt_hbm, piece(2, y, zh), local_sem.at[4]))
    loads.append(pltpu.make_async_copy(sb_hbm, sb_ref, local_sem.at[6]))
    loads.append(pltpu.make_async_copy(tb_hbm, tb_ref, local_sem.at[7]))
    vid_copy.start()
    for load in loads:
        load.start()

    barrier = pltpu.get_barrier_semaphore()

    def greet(to_dp, to_tile):
        pl.semaphore_signal(barrier, inc=1, device_id={"dp": to_dp, "tile": to_tile}, device_id_type=MESH)

    greet(dp, partner)
    greet(up, t)
    greet(dn, t)
    greet(dp, x_next)
    greet(dp, x_prev)

    @pl.when(edge)
    def _():
        greet(other, cross_edge)
        greet(other, cross_inner)

    @pl.when(jnp.logical_not(edge))
    def _():
        greet(other, inner_source)

    @pl.when(has_before)
    def _():
        greet(dp, t - 1)

    @pl.when(has_after)
    def _():
        greet(dp, t + 1)

    one = lambda flag: jnp.where(flag, 1, 0)
    pl.semaphore_wait(barrier, 6 + one(edge) + one(has_before) + one(has_after))

    def ring(g, send, recv, y_at, z_at, to_dp, to_tile, low=0, count=None, src=None):
        ref = piece(g, y_at, z_at, low, count)
        return remote(ref if src is None else src, ref, wsend.at[g, send], wrecv.at[g, recv], to_dp, to_tile)

    def from_x(n, k, y_at, to_tile):
        ref = block_piece(block_a, y_at, carried)
        return remote(ref, ref, xsend.at[n, k], xrecv.at[n, k], dp, to_tile)

    by_x = jnp.logical_not(first), jnp.logical_not(last)

    def y_of(k):
        return (y + k) % 4

    def spread(g, k):
        ring(g, 6 + k, 5 + k, y_of(k), carried, dp, partner).start()
        if g == 0:
            pl.when(by_x[0])(lambda: from_x(0, k, y_of(k), x_next).start())
            pl.when(by_x[1])(lambda: from_x(1, k, y_of(k), x_prev).start())

    def cross_copy():
        return remote(
            ws_hbm.at[:, :, columns(cross_e)], block_piece(cross_e, y, zh), wsend.at[3, 0], wrecv.at[3, 0],
            other, cross_edge,
        )

    def start_z(g):
        if g == 3:
            cross_copy().start()
            return
        ring(g, 1, 0, y, zh, other, cross_inner, src=source(g)).start()
        ring(g, 0, 0, y, zh, other, cross_edge, src=source(g)).start()

    def start_y(g, src=None):
        ring(g, 2, 1, y, carried, up, t, src=src).start()
        ring(g, 3, 2, y, carried, dn, t, src=src).start()

    def stage_z(g):
        ring(g, 0, 0, y, 1 - zh, dp, partner).wait_recv()
        start_y(g)
        spread(g, 0)

    def stage_y(g):
        ring(g, 2, 1, y_of(3), carried, up, t).wait_recv()
        ring(g, 4, 3, y_of(3), carried, up, t, 0, half).start()
        ring(g, 3, 2, y_of(1), carried, dn, t).wait_recv()
        ring(g, 5, 4, y_of(1), carried, dn, t, half, half).start()
        spread(g, 3)
        spread(g, 1)

    def stage_far(g):
        ring(g, 4, 3, y_of(2), carried, up, t, 0, half).wait_recv()
        ring(g, 5, 4, y_of(2), carried, dn, t, half, half).wait_recv()
        spread(g, 2)

    def stage_done(g, ks):
        for k in ks:
            ring(g, 6 + k, 5 + k, y_of(k), 1 - carried, dp, partner).wait_recv()

    def onward(n, k, z_at):
        ref = block_piece((block_d, block_c)[n], y_of(k), z_at)
        return remote(ref, ref, psend.at[n, k], precv.at[n, k], dp, partner)

    def stage_x(k):
        for n in range(2):
            @pl.when(by_x[n])
            def _():
                ref = block_piece((block_d, block_c)[n], y_of(k), carried)
                remote(ref, ref, xsend.at[n, k], xrecv.at[n, k], dp, x_next).wait_recv()
                onward(n, k, carried).start()

    def stage_x_done(ks):
        for n in range(2):
            @pl.when(by_x[n])
            def _():
                for k in ks:
                    onward(n, k, 1 - carried).wait_recv()

        pl.when(edge)(lambda: stage_done(3, ks))

    def wait_ring(g):
        for slot in (2, 3):
            ring(g, slot, 0, y, carried, up, t).wait_send()
        for slot in (4, 5):
            ring(g, slot, 0, y, carried, up, t, 0, half).wait_send()
        for k in range(1, 4):
            ring(g, 6 + k, 5 + k, y, carried, dp, partner).wait_send()

        @pl.when(is_one)
        def _():
            ring(g, 6, 5, y, carried, dp, partner).wait_send()

    def wait_sends():
        for g in range(3):
            wait_ring(g)
        pl.when(edge)(lambda: wait_ring(3))

        @pl.when(jnp.logical_and(is_one, edge))
        def _():
            for g in range(3):
                ring(g, 0, 0, y, zh, other, cross_edge).wait_send()
                ring(g, 1, 0, y, zh, other, cross_inner).wait_send()
            cross_copy().wait_send()

        def wait_x(n, k):
            from_x(n, k, y, x_next).wait_send()
            onward(n, k, carried).wait_send()

        for n in range(2):
            @pl.when(by_x[n])
            def _():
                for k in range(1, 4):
                    wait_x(n, k)

            pl.when(jnp.logical_and(by_x[n], is_one))(lambda: wait_x(n, 0))

    def rows_of(i):
        return pl.ds(pl.multiple_of(i * ROWS, ROWS), ROWS)

    def hcopy(q, i, side):
        slot = q * chunks + i
        return remote(
            own.at[q, :, rows_of(i), :], near.at[1 - side, q, :, rows_of(i), :],
            hsend.at[side, slot], hrecv.at[side, slot], dp, t - 1 if side == 0 else t + 1,
        )

    def exchanged(side, i):
        there, far = ((has_before, far_before), (has_after, far_after))[side]
        return jnp.logical_and(there, jnp.logical_not(jnp.logical_and(far, i < FAR_CHUNKS)))

    def send_hidden(p, i):
        for side in range(2):
            pl.when(exchanged(side, i))(lambda: hcopy((x + p) % 2, i, side).start())

    far_rows = (FAR_CHUNKS * ROWS // breadth + 1) * breadth
    far_cuts = [far_rows * n // (FAR_PARTS * breadth) * breadth for n in range(FAR_PARTS + 1)]

    def far_copy(n):
        rows = pl.ds(far_cuts[n], far_cuts[n + 1] - far_cuts[n])
        return remote(vid_hbm.at[rows], vid_far.at[rows], vsem.at[0, n], vsem.at[1, n], dp, far_tile)

    def far_start(n):
        pl.when(far_any)(lambda: far_copy(n).start())

    def prepare(src, dst, lines):
        lanes = lax.broadcasted_iota(jnp.int32, (breadth, BLOCK), 1)
        at = lax.broadcasted_iota(jnp.int32, (breadth, group), 0)

        @pl.loop(0, lines)
        def _(r):
            line = src[pl.ds(pl.multiple_of(r * breadth, breadth), breadth), :].astype(jnp.float32)
            rows = pl.ds(pl.multiple_of((r + 1) * breadth, breadth), breadth)
            parts = [line[:, n * BLOCK : (n + 1) * BLOCK] for n in range(blocks)]
            turned = [pltpu.roll(part, shard, 1) for part in parts]
            low = lanes < shard
            for z_at in range(2):
                left_of, right_of = (parts, turned) if z_at == 0 else (turned, parts)
                mid = jnp.concatenate(
                    [jnp.where(low, left_of[n], right_of[n + 1]) for n in range(0, blocks, 2)], axis=1
                )
                left = jnp.where(at == 0, 0.0, pltpu.roll(mid, 1, 0))
                right = jnp.where(at == breadth - 1, 0.0, pltpu.roll(mid, breadth - 1, 0))
                for dx, value in enumerate((left, mid, right)):
                    start = (3 * z_at + dx) * group
                    dst[rows, start : start + group] = value.astype(jnp.bfloat16)

    def half_dot(xs, z_at, pair, i):
        total = None
        for dy in range(3):
            start = pl.multiple_of(i * ROWS + dy * breadth, breadth)
            lhs = xs[pl.ds(start, ROWS), pl.ds(pl.multiple_of(z_at * (3 * group), 3 * group), 3 * group)]
            rhs = jnp.concatenate(
                [wb[j, z_at, 3 * dy : 3 * dy + 3].reshape(3 * group, BLOCK) for j in pair], axis=1
            )
            part = jnp.dot(lhs, rhs, preferred_element_type=jnp.float32)
            total = part if total is None else total + part
        return total

    def activate(total, pair):
        total = total + jnp.concatenate([sb_ref[j] for j in pair], axis=1)
        return (total / (1.0 + jnp.exp(-total))).astype(jnp.bfloat16)

    pairs = (block_a, block_b), (block_c, block_d)

    def spatial_first(p, i):
        acc[rows_of(i), 2 * BLOCK * p : 2 * BLOCK * (p + 1)] = half_dot(xcat, zh, pairs[p], i)

    def spatial_rest(p, i):
        total = acc[rows_of(i), 2 * BLOCK * p : 2 * BLOCK * (p + 1)] + half_dot(xcat, 1 - zh, pairs[p], i)
        hidden = activate(total, pairs[p])
        for n, j in enumerate(pairs[p]):
            own[j % 2, j // 2, rows_of(i), :] = hidden[:, n * BLOCK : (n + 1) * BLOCK]

    @pl.when(jnp.logical_and(is_one, edge))
    def _():
        for g in (0, 1, 3, 2):
            start_z(g)

    @pl.when(is_zero)
    def _():
        start_y(0, source(0))
        start_y(1, source(1))

    far_start(0)

    zeros = jnp.zeros((breadth, 6 * group), jnp.bfloat16)
    xcat[0:breadth, :] = zeros
    xcat[breadth + pixels :, :] = zeros
    vid_copy.wait()
    prepare(outv, xcat, height)
    for load in loads:
        load.wait()

    @pl.when(is_zero)
    def _():
        stage_y(0)
        stage_y(1)
        stage_far(0)
        stage_far(1)
        pl.when(edge)(lambda: start_y(3, source(3)))

    @pl.when(is_one)
    def _():
        stage_z(0)
        stage_z(1)
        stage_y(0)
        stage_y(1)
        stage_done(0, (1, 2, 3))
        stage_done(1, (1, 2, 3))

    edge_zero, edge_one = jnp.logical_and(edge, is_zero), jnp.logical_and(edge, is_one)

    def on(flag, n, at, *stages):
        @pl.when(jnp.logical_and(flag, n == at))
        def _():
            for stage in stages:
                stage()

    @pl.loop(0, chunks)
    def _(n):
        spatial_first(0, chunks - 1 - n)
        on(is_zero, n, 1, lambda: stage_x(3))
        on(is_zero, n, 2, lambda: stage_x(1))
        on(is_zero, n, 3, lambda: stage_x(2))
        on(is_one, n, 0, lambda: stage_far(0))
        on(is_one, n, 1, lambda: stage_far(1))
        on(edge_one, n, 2, lambda: stage_z(3))

    @pl.when(is_zero)
    def _():
        stage_done(0, range(4))
        stage_done(1, range(4))

    @pl.loop(0, chunks)
    def _(n):
        spatial_rest(0, chunks - 1 - n)

        @pl.when(n > 0)
        def _():
            send_hidden(0, chunks - n)

        on(is_zero, n, 0, lambda: start_y(2, source(2)))
        on(edge_zero, n, 0, lambda: stage_y(3))
        on(is_one, n, 0, lambda: stage_x(0))
        on(is_one, n, 1, lambda: stage_x(3))
        on(edge_one, n, 1, lambda: stage_y(3))
        on(is_one, n, 2, lambda: stage_x(1))
        on(edge_zero, n, 3, lambda: stage_far(3))

    pl.when(is_one)(lambda: stage_x_done((1, 2, 3)))

    @pl.loop(0, chunks)
    def _(n):
        spatial_first(1, chunks - 1 - n)

        @pl.when(n == 0)
        def _():
            send_hidden(0, 0)

        on(is_one, n, 0, lambda: stage_x(2))
        on(edge_one, n, 1, lambda: stage_far(3))
        on(is_one, n, 2, lambda: stage_z(2))

    pl.when(is_zero)(lambda: stage_x_done(range(4)))

    @pl.loop(0, chunks)
    def _(n):
        spatial_rest(1, chunks - 1 - n)

        @pl.when(n > 0)
        def _():
            send_hidden(1, chunks - n)

        on(is_zero, n, 1, lambda: stage_y(2))
        on(is_one, n, 2, lambda: stage_y(2))

    stage_far(2)
    send_hidden(1, 0)

    @pl.when(far_any)
    def _():
        for n in range(FAR_PARTS):
            far_copy(n).wait()
        xcat_far[0:breadth, :] = zeros
        prepare(vid_far, xcat_far, far_rows // breadth)

        @pl.loop(0, 2 * FAR_CHUNKS)
        def _(n):
            p, i = n // FAR_CHUNKS, n % FAR_CHUNKS
            pair = ((x + p) % 4, (x + p + 2) % 4)
            hidden = activate(half_dot(xcat_far, 0, pair, i) + half_dot(xcat_far, 1, pair, i), pair)
            for m, j in enumerate(pair):
                near[far_side, j % 2, j // 2, rows_of(i), :] = hidden[:, m * BLOCK : (m + 1) * BLOCK]

    pl.when(is_zero)(lambda: stage_done(2, range(4)))
    pl.when(is_one)(lambda: stage_done(2, (1, 2, 3)))

    def taps(lag, j):
        return wt[lag, columns(j), :]

    def temporal(lag, ref, q, i):
        lhs = jnp.concatenate([ref[q, m, rows_of(i), :] for m in range(2)], axis=1)
        rhs = jnp.concatenate([taps(lag, q), taps(lag, q + 2)], axis=0)
        return jnp.dot(lhs, rhs, preferred_element_type=jnp.float32)

    @pl.loop(0, chunks)
    def _(n):
        acc[rows_of(n), :] = temporal(1, own, 0, n) + temporal(1, own, 1, n) + tb_ref[...]

    wait_sends()

    x_before, x_after = (t + tiles - 1) % tiles // 8, (t + 1) % tiles // 8
    for p in range(2):
        @pl.loop(0, chunks)
        def _(n, p=p):
            i = chunks - 1 - n
            rows = rows_of(i)
            for side, there, x_there in ((0, has_before, x_before), (1, has_after, x_after)):
                q = (x_there + p) % 2
                pl.when(exchanged(side, i))(lambda: hcopy(q, i, 1 - side).wait_recv())

                @pl.when(there)
                def _():
                    acc[rows, :] += temporal(2 * side, near.at[side], q, i)

            if p == 1:
                outv[rows, :] = acc[rows, :].astype(jnp.bfloat16)

    @pl.loop(0, chunks)
    def _(i):
        for side in range(2):
            @pl.when(exchanged(side, i))
            def _():
                for q in range(2):
                    hcopy(q, i, side).wait_send()


def per_device(videos, spatial_filter, temporal_filter, spatial_bias, temporal_bias):
    _, _, height, breadth, chans = videos.shape
    shard = spatial_filter.shape[1]
    pixels = height * breadth
    blocks = chans // BLOCK
    chunks = pixels // ROWS
    far_pixels = FAR_CHUNKS * ROWS + breadth
    bf = jnp.bfloat16
    anywhere = pl.BlockSpec(memory_space=pl.ANY)
    vmem = pl.BlockSpec(memory_space=pltpu.VMEM)
    dma = pltpu.SemaphoreType.DMA
    out = pl.pallas_call(
        functools.partial(kernel, (height, breadth, chans, shard)),
        out_shape=pltpu.VMEM((pixels, chans), bf),
        in_specs=[anywhere] * 5,
        out_specs=vmem,
        scratch_shapes=[
            pltpu.VMEM((pixels + 2 * breadth, 3 * chans), bf),
            pltpu.VMEM((far_pixels + breadth, 3 * chans), bf),
            pltpu.VMEM((far_pixels, chans), bf),
            pltpu.VMEM((blocks, 2, TAPS_S, chans // 2, BLOCK), bf),
            pltpu.VMEM((TAPS_T, chans, chans), bf),
            pltpu.VMEM((2, blocks // 2, pixels, BLOCK), bf),
            pltpu.VMEM((2, 2, blocks // 2, pixels, BLOCK), bf),
            pltpu.VMEM((pixels, chans), jnp.float32),
            pltpu.VMEM((blocks, 1, BLOCK), jnp.float32),
            pltpu.VMEM((1, chans), jnp.float32),
            dma((8,)),
            dma((4, 10)), dma((4, 9)),
            dma((2, 4)), dma((2, 4)),
            dma((2, 4)), dma((2, 4)),
            dma((2, 2 * chunks)), dma((2, 2 * chunks)),
            dma((2, FAR_PARTS)),
        ],
        compiler_params=pltpu.CompilerParams(
            collective_id=0, has_side_effects=True, vmem_limit_bytes=56 * 1024 * 1024
        ),
    )(
        videos.reshape(pixels, chans),
        spatial_filter,
        temporal_filter,
        spatial_bias.reshape(blocks, 1, BLOCK),
        temporal_bias.reshape(1, chans),
    )
    return out.reshape(videos.shape)


def solution(mesh):
    return jax.shard_map(
        per_device,
        mesh=mesh,
        in_specs=(
            P("dp", "tile", None, None, None),
            P(None, "dp", None),
            P(None, "dp", None),
            P(),
            P(),
        ),
        out_specs=P("dp", "tile", None, None, None),
        check_vma=False,
    )
```

```python
import functools

import jax
import jax.numpy as jnp
from jax import lax
from jax.experimental import pallas as pl
from jax.experimental.pallas import tpu as pltpu
from jax.sharding import PartitionSpec as P

BLOCK = 128
ROWS = 512
FAR_CHUNKS = 2
RELAYED = 3
FLOWS = 3
TAPS_S, TAPS_T = 9, 3
MESH = pl.DeviceIdType.MESH


def kernel(
    dims, vid_hbm, ws_hbm, wt_hbm, sb_hbm, tb_hbm, outv,
    xcat, xcat_far, vid_far, relayed, made, wb, wt, own, near, acc, sb_ref, tb_ref,
    local_sem, wsend, wrecv, xsend, xrecv, psend, precv, hsend, hrecv, vsem, rsem, csend, crecv,
):
    height, breadth, chans, shard = dims
    pixels = height * breadth
    chunks = pixels // ROWS
    blocks = chans // BLOCK
    group = chans // 2
    half = shard // 2

    dp, t = lax.axis_index("dp"), lax.axis_index("tile")
    tiles = lax.axis_size("tile")
    y, zh = dp // 2, dp % 2
    core, zl, x = t % 2, (t // 2) % 4, t // 8
    partner = t + 1 - 2 * core
    up, dn = ((y + 1) % 4) * 2 + zh, ((y + 3) % 4) * 2 + zh
    other = y * 2 + 1 - zh
    first, last = zl == 0, zl == 3
    edge = jnp.logical_or(first, last)
    base = t - zl * 2
    cross_edge = base + jnp.where(first, 6, 0)
    cross_inner = base + jnp.where(first, 4, 2)
    inner_source = base + jnp.where(zl == 1, 6, 0)
    x_next, x_prev = (t + 8) % tiles, (t + tiles - 8) % tiles
    has_before, has_after = t > 0, t < tiles - 1
    far_before = jnp.logical_and(t % 8 == 0, has_before)
    far_after = jnp.logical_and(t % 8 == 7, has_after)
    far_any = jnp.logical_or(far_before, far_after)
    aid_before = jnp.logical_and(t % 8 == 1, t > 1)
    aid_after = jnp.logical_and(t % 8 == 6, t < tiles - 2)
    aid_any = jnp.logical_or(aid_before, aid_after)
    team = jnp.logical_or(far_any, aid_any)
    far_side = jnp.where(jnp.logical_or(far_after, aid_after), 1, 0)
    two_off = jnp.where(far_side == 1, t + 2, t - 2)
    feeding_relay = jnp.where(aid_after, 0, tiles - 1)
    far_tile = jnp.where(far_after, t + 1, t - 1)
    is_relay = jnp.logical_or(t == 0, t == tiles - 1)
    my_relay = jnp.where(far_after, tiles - 1, 0)
    flow = jnp.where(far_after, x, x - 1)
    x_free = jnp.where(jnp.logical_or(first, zl == 2), FLOWS, 0)
    in_free = x == x_free
    x_across = (t + 16) % tiles
    is_one = core == 1
    is_zero = core == 0

    block_a, block_b, block_c, block_d = x, (x + 2) % 4, (x + 1) % 4, (x + 3) % 4
    block_e, cross_e = jnp.where(first, block_d, block_c), jnp.where(first, block_c, block_d)
    ring_blocks = {0: block_a, 1: block_b, 3: block_e}
    carried = jnp.where(is_zero, zh, 1 - zh)

    def remote(src, dst, ssem, rsem, to_dp, to_tile):
        return pltpu.make_async_remote_copy(
            src_ref=src, dst_ref=dst, send_sem=ssem, recv_sem=rsem,
            device_id={"dp": to_dp, "tile": to_tile}, device_id_type=MESH,
        )

    def columns(j):
        return pl.ds(pl.multiple_of(j * BLOCK, BLOCK), BLOCK)

    def block_piece(j, y_at, z_at, low=0, count=None):
        count = shard if count is None else count
        return wb.at[j, z_at, :, pl.ds(pl.multiple_of(y_at * shard + low, half), count), :]

    def piece(g, y_at, z_at, low=0, count=None):
        if g != 2:
            return block_piece(ring_blocks[g], y_at, z_at, low, count)
        count = shard if count is None else count
        return wt.at[:, pl.ds(pl.multiple_of((y_at * 2 + z_at) * shard + low, half), count), :]

    def source(g):
        return wt_hbm if g == 2 else ws_hbm.at[:, :, columns(ring_blocks[g])]

    vid_copy = pltpu.make_async_copy(vid_hbm, outv, local_sem.at[5])
    loads = [
        pltpu.make_async_copy(ws_hbm.at[:, :, columns(j)], block_piece(j, y, zh), local_sem.at[n])
        for n, j in enumerate((block_a, block_b, block_c, block_d))
    ]
    loads.append(pltpu.make_async_copy(wt_hbm, piece(2, y, zh), local_sem.at[4]))
    loads.append(pltpu.make_async_copy(sb_hbm, sb_ref, local_sem.at[6]))
    loads.append(pltpu.make_async_copy(tb_hbm, tb_ref, local_sem.at[7]))
    vid_copy.start()
    for load in loads:
        load.start()

    barrier = pltpu.get_barrier_semaphore()

    def greet(to_dp, to_tile):
        pl.semaphore_signal(barrier, inc=1, device_id={"dp": to_dp, "tile": to_tile}, device_id_type=MESH)

    greet(dp, partner)
    greet(up, t)
    greet(dn, t)
    greet(dp, x_next)
    greet(dp, x_prev)
    greet(dp, x_across)

    @pl.when(far_any)
    def _():
        greet(dp, my_relay)

    @pl.when(aid_any)
    def _():
        greet(dp, feeding_relay)

    @pl.when(team)
    def _():
        greet(dp, two_off)

    @pl.when(is_relay)
    def _():
        for n in range(FLOWS):
            greet(dp, jnp.where(t == 0, 8 * n + 8, 8 * n + 7))
            greet(dp, jnp.where(t == 0, 8 * n + 6, 8 * n + 9))

    @pl.when(edge)
    def _():
        greet(other, cross_edge)
        greet(other, cross_inner)

    @pl.when(jnp.logical_not(edge))
    def _():
        greet(other, inner_source)

    @pl.when(has_before)
    def _():
        greet(dp, t - 1)

    @pl.when(has_after)
    def _():
        greet(dp, t + 1)

    one = lambda flag: jnp.where(flag, 1, 0)
    pl.semaphore_wait(barrier, 7 + one(edge) + one(has_before) + one(has_after) + 2 * one(team) + 2 * FLOWS * one(is_relay))

    def ring(g, send, recv, y_at, z_at, to_dp, to_tile, low=0, count=None, src=None):
        ref = piece(g, y_at, z_at, low, count)
        return remote(ref if src is None else src, ref, wsend.at[g, send], wrecv.at[g, recv], to_dp, to_tile)

    def from_x(n, k, y_at, to_tile):
        ref = block_piece(block_a, y_at, carried)
        return remote(ref, ref, xsend.at[n, k], xrecv.at[n, k], dp, to_tile)

    by_x = jnp.logical_not(first), jnp.logical_not(last)

    def y_of(k):
        return (y + k) % 4

    def spread(g, k):
        ring(g, 6 + k, 5 + k, y_of(k), carried, dp, partner).start()
        if g == 0:
            pl.when(by_x[0])(lambda: from_x(0, k, y_of(k), x_next).start())
            pl.when(by_x[1])(lambda: from_x(1, k, y_of(k), x_prev).start())

    def cross_copy():
        return remote(
            ws_hbm.at[:, :, columns(cross_e)], block_piece(cross_e, y, zh), wsend.at[3, 0], wrecv.at[3, 0],
            other, cross_edge,
        )

    def start_z(g):
        if g == 3:
            cross_copy().start()
            return
        inner = lambda: ring(g, 1, 0, y, zh, other, cross_inner, src=source(g)).start()
        if g == 2:
            pl.when(in_free)(inner)
        else:
            inner()
        ring(g, 0, 0, y, zh, other, cross_edge, src=source(g)).start()

    def start_y(g, src=None):
        ring(g, 2, 1, y, carried, up, t, src=src).start()
        ring(g, 3, 2, y, carried, dn, t, src=src).start()

    inner_source_of_two = jnp.logical_and(jnp.logical_not(edge), in_free)

    def share(slot, to_tile):
        return ring(2, slot, 0, y, 1 - zh, dp, to_tile)

    def stage_share():
        ring(2, 0, 0, y, 1 - zh, dp, partner).wait_recv()
        for slot, to_tile in ((0, x_next), (1, x_prev), (10, x_across)):
            share(slot, to_tile).start()

    def stage_z(g):
        arrived = lambda: ring(g, 0, 0, y, 1 - zh, dp, partner).wait_recv()
        if g == 2:
            pl.when(jnp.logical_not(inner_source_of_two))(arrived)
        else:
            arrived()
        start_y(g)
        spread(g, 0)

    def stage_y(g):
        ring(g, 2, 1, y_of(3), carried, up, t).wait_recv()
        ring(g, 4, 3, y_of(3), carried, up, t, 0, half).start()
        ring(g, 3, 2, y_of(1), carried, dn, t).wait_recv()
        ring(g, 5, 4, y_of(1), carried, dn, t, half, half).start()
        spread(g, 3)
        spread(g, 1)

    def stage_far(g):
        ring(g, 4, 3, y_of(2), carried, up, t, 0, half).wait_recv()
        ring(g, 5, 4, y_of(2), carried, dn, t, half, half).wait_recv()
        spread(g, 2)

    def stage_done(g, ks):
        for k in ks:
            ring(g, 6 + k, 5 + k, y_of(k), 1 - carried, dp, partner).wait_recv()

    def onward(n, k, z_at):
        ref = block_piece((block_d, block_c)[n], y_of(k), z_at)
        return remote(ref, ref, psend.at[n, k], precv.at[n, k], dp, partner)

    def stage_x(k):
        for n in range(2):
            @pl.when(by_x[n])
            def _():
                ref = block_piece((block_d, block_c)[n], y_of(k), carried)
                remote(ref, ref, xsend.at[n, k], xrecv.at[n, k], dp, x_next).wait_recv()
                onward(n, k, carried).start()

    def stage_x_done(ks):
        for n in range(2):
            @pl.when(by_x[n])
            def _():
                for k in ks:
                    onward(n, k, 1 - carried).wait_recv()

        pl.when(edge)(lambda: stage_done(3, ks))

    def wait_ring(g):
        for slot in (2, 3):
            ring(g, slot, 0, y, carried, up, t).wait_send()
        for slot in (4, 5):
            ring(g, slot, 0, y, carried, up, t, 0, half).wait_send()
        for k in range(1, 4):
            ring(g, 6 + k, 5 + k, y, carried, dp, partner).wait_send()

        @pl.when(is_one)
        def _():
            ring(g, 6, 5, y, carried, dp, partner).wait_send()

    def wait_sends():
        for g in range(3):
            wait_ring(g)
        pl.when(edge)(lambda: wait_ring(3))

        @pl.when(jnp.logical_and(is_one, edge))
        def _():
            for g in range(3):
                ring(g, 0, 0, y, zh, other, cross_edge).wait_send()
            for g in range(2):
                ring(g, 1, 0, y, zh, other, cross_inner).wait_send()
            pl.when(in_free)(lambda: ring(2, 1, 0, y, zh, other, cross_inner).wait_send())
            cross_copy().wait_send()

        @pl.when(jnp.logical_and(is_one, inner_source_of_two))
        def _():
            for slot in (0, 1, 10):
                share(slot, x_next).wait_send()

        def wait_x(n, k):
            from_x(n, k, y, x_next).wait_send()
            onward(n, k, carried).wait_send()

        for n in range(2):
            @pl.when(by_x[n])
            def _():
                for k in range(1, 4):
                    wait_x(n, k)

            pl.when(jnp.logical_and(by_x[n], is_one))(lambda: wait_x(n, 0))

    def rows_of(i):
        return pl.ds(pl.multiple_of(i * ROWS, ROWS), ROWS)

    def hcopy(q, i, side):
        slot = q * chunks + i
        return remote(
            own.at[q, :, rows_of(i), :], near.at[1 - side, q, :, rows_of(i), :],
            hsend.at[side, slot], hrecv.at[side, slot], dp, t - 1 if side == 0 else t + 1,
        )

    def exchanged(side):
        there, far = ((has_before, far_before), (has_after, far_after))[side]
        return jnp.logical_and(there, jnp.logical_not(far))

    def send_hidden(p, i):
        for side in range(2):
            pl.when(exchanged(side))(lambda: hcopy((x + p) % 2, i, side).start())

    far_rows = (FAR_CHUNKS * ROWS // breadth + 1) * breadth
    low_from = pixels - far_rows
    kept = far_rows - RELAYED * breadth
    passed = pl.ds(low_from + kept, RELAYED * breadth)

    def far_upper():
        rows = pl.ds(0, far_rows)
        return remote(vid_hbm.at[rows], vid_far.at[rows], vsem.at[0, 0], vsem.at[1, 0], dp, far_tile)

    def far_lower():
        return remote(
            vid_hbm.at[pl.ds(low_from, kept)], vid_far.at[pl.ds(0, kept)], vsem.at[0, 1], vsem.at[1, 1], dp, two_off
        )

    def to_relay():
        return remote(vid_hbm.at[passed], relayed.at[flow], vsem.at[0, 2], rsem.at[0, flow], dp, my_relay)

    def from_relay(n, to_tile):
        return remote(
            relayed.at[n], vid_far.at[pl.ds(kept, RELAYED * breadth)], rsem.at[1, n], vsem.at[1, 2], dp, to_tile
        )

    def relay_pass(distance):
        n = jnp.where(t == 0, distance - 1, FLOWS - distance)

        @pl.when(is_relay)
        def _():
            remote(vid_hbm.at[passed], relayed.at[n], vsem.at[0, 2], rsem.at[0, n], dp, partner).wait_recv()
            from_relay(n, jnp.where(t == 0, 8 * n + 6, 8 * n + 9)).start()

    def prepare(src, dst, lines, above=1):
        lanes = lax.broadcasted_iota(jnp.int32, (breadth, BLOCK), 1)
        at = lax.broadcasted_iota(jnp.int32, (breadth, group), 0)

        @pl.loop(0, lines)
        def _(r):
            line = src[pl.ds(pl.multiple_of(r * breadth, breadth), breadth), :].astype(jnp.float32)
            rows = pl.ds(pl.multiple_of((r + above) * breadth, breadth), breadth)
            parts = [line[:, n * BLOCK : (n + 1) * BLOCK] for n in range(blocks)]
            turned = [pltpu.roll(part, shard, 1) for part in parts]
            low = lanes < shard
            for z_at in range(2):
                left_of, right_of = (parts, turned) if z_at == 0 else (turned, parts)
                mid = jnp.concatenate(
                    [jnp.where(low, left_of[n], right_of[n + 1]) for n in range(0, blocks, 2)], axis=1
                )
                left = jnp.where(at == 0, 0.0, pltpu.roll(mid, 1, 0))
                right = jnp.where(at == breadth - 1, 0.0, pltpu.roll(mid, breadth - 1, 0))
                for dx, value in enumerate((left, mid, right)):
                    start = (3 * z_at + dx) * group
                    dst[rows, start : start + group] = value.astype(jnp.bfloat16)

    def half_dot(xs, z_at, pair, i):
        total = None
        for dy in range(3):
            start = pl.multiple_of(i * ROWS + dy * breadth, breadth)
            lhs = xs[pl.ds(start, ROWS), pl.ds(pl.multiple_of(z_at * (3 * group), 3 * group), 3 * group)]
            rhs = jnp.concatenate(
                [wb[j, z_at, 3 * dy : 3 * dy + 3].reshape(3 * group, BLOCK) for j in pair], axis=1
            )
            part = jnp.dot(lhs, rhs, preferred_element_type=jnp.float32)
            total = part if total is None else total + part
        return total

    def activate(total, pair):
        total = total + jnp.concatenate([sb_ref[j] for j in pair], axis=1)
        return (total / (1.0 + jnp.exp(-total))).astype(jnp.bfloat16)

    pairs = (block_a, block_b), (block_c, block_d)

    def spatial_first(p, i):
        acc[rows_of(i), 2 * BLOCK * p : 2 * BLOCK * (p + 1)] = half_dot(xcat, zh, pairs[p], i)

    def spatial_rest(p, i):
        total = acc[rows_of(i), 2 * BLOCK * p : 2 * BLOCK * (p + 1)] + half_dot(xcat, 1 - zh, pairs[p], i)
        hidden = activate(total, pairs[p])
        for n, j in enumerate(pairs[p]):
            own[j % 2, j // 2, rows_of(i), :] = hidden[:, n * BLOCK : (n + 1) * BLOCK]

    @pl.when(jnp.logical_and(is_one, edge))
    def _():
        for g in (0, 1, 3, 2):
            start_z(g)

    @pl.when(is_zero)
    def _():
        start_y(0, source(0))
        start_y(1, source(1))
        pl.when(edge)(lambda: start_y(3, source(3)))

    @pl.when(far_any)
    def _():
        to_relay().start()
        far_upper().start()
        far_lower().start()


    zeros = jnp.zeros((breadth, 6 * group), jnp.bfloat16)
    xcat[0:breadth, :] = zeros
    xcat[breadth + pixels :, :] = zeros
    vid_copy.wait()
    prepare(outv, xcat, height)
    for load in loads:
        load.wait()

    @pl.when(is_zero)
    def _():
        stage_y(0)
        stage_y(1)
        relay_pass(1)
        stage_far(0)
        stage_far(1)

    @pl.when(is_one)
    def _():
        stage_z(0)
        stage_z(1)
        relay_pass(1)
        stage_y(0)
        stage_y(1)
        pl.when(edge)(lambda: stage_z(3))
        stage_done(0, (1, 2, 3))
        stage_done(1, (1, 2, 3))

    relay_pass(2)
    relay_pass(3)
    edge_zero, edge_one = jnp.logical_and(edge, is_zero), jnp.logical_and(edge, is_one)
    sharing = jnp.logical_and(is_one, inner_source_of_two)

    def on(flag, n, at, *stages):
        @pl.when(jnp.logical_and(flag, n == at))
        def _():
            for stage in stages:
                stage()

    @pl.loop(0, chunks)
    def _(n):
        spatial_first(0, chunks - 1 - n)
        on(is_zero, n, 1, lambda: stage_x(3))
        on(is_zero, n, 2, lambda: stage_x(1))
        on(is_zero, n, 3, lambda: stage_x(2))
        on(is_one, n, 0, lambda: stage_far(0))
        on(is_one, n, 1, lambda: stage_far(1))
        on(edge_zero, n, 0, lambda: stage_y(3))
        on(edge_one, n, 2, lambda: stage_y(3))
        on(is_zero, n, 2, lambda: start_y(2, source(2)))
        on(edge_zero, n, 3, lambda: stage_far(3))
        on(sharing, n, 3, stage_share)

    @pl.when(is_zero)
    def _():
        stage_done(0, range(4))
        stage_done(1, range(4))

    @pl.loop(0, chunks)
    def _(n):
        spatial_rest(0, chunks - 1 - n)

        @pl.when(n > 0)
        def _():
            send_hidden(0, chunks - n)

        on(is_one, n, 0, lambda: stage_x(0))
        on(is_one, n, 1, lambda: stage_x(3))
        on(edge_one, n, 0, lambda: stage_far(3))
        on(is_one, n, 2, lambda: stage_x(1))
        on(is_one, n, 3, lambda: stage_z(2))

    pl.when(is_one)(lambda: stage_x_done((1, 2, 3)))

    @pl.loop(0, chunks)
    def _(n):
        spatial_first(1, chunks - 1 - n)

        @pl.when(n == 0)
        def _():
            send_hidden(0, 0)

        on(is_one, n, 0, lambda: stage_x(2))
        on(is_zero, n, 2, lambda: stage_y(2))

    pl.when(is_zero)(lambda: stage_x_done(range(4)))

    @pl.loop(0, chunks)
    def _(n):
        spatial_rest(1, chunks - 1 - n)

        @pl.when(n > 0)
        def _():
            send_hidden(1, chunks - n)

        on(is_one, n, 0, lambda: stage_y(2))

    stage_far(2)
    send_hidden(1, 0)

    def made_copy(q, i):
        rows = rows_of(i + FAR_CHUNKS)
        return remote(
            made.at[q, :, rows_of(i), :], near.at[far_side, q, :, rows, :], csend.at[q, i], crecv.at[q, i], dp, partner
        )

    def far_step(n):
        p, i = n // FAR_CHUNKS, n % FAR_CHUNKS
        return (x + p) % 2, i

    @pl.when(far_any)
    def _():
        far_upper().wait()
        far_lower().wait_send()
        to_relay().wait_send()

    @pl.when(aid_any)
    def _():
        far_lower().wait_recv()
        from_relay(0, partner).wait_recv()

    @pl.when(team)
    def _():
        blank = jnp.where(far_any, 0, far_rows)
        xcat_far[pl.ds(pl.multiple_of(blank, breadth), breadth), :] = zeros
        prepare(vid_far, xcat_far, far_rows // breadth, one(far_any))

        @pl.loop(0, 2 * FAR_CHUNKS)
        def _(n):
            p, i = n // FAR_CHUNKS, n % FAR_CHUNKS
            pair = ((x + p) % 4, (x + p + 2) % 4)
            hidden = activate(half_dot(xcat_far, 0, pair, i) + half_dot(xcat_far, 1, pair, i), pair)

            @pl.when(far_any)
            def _():
                for m, j in enumerate(pair):
                    near[far_side, j % 2, j // 2, rows_of(i), :] = hidden[:, m * BLOCK : (m + 1) * BLOCK]

            @pl.when(aid_any)
            def _():
                for m, j in enumerate(pair):
                    made[j % 2, j // 2, rows_of(i), :] = hidden[:, m * BLOCK : (m + 1) * BLOCK]

            pl.when(jnp.logical_and(aid_any, n > 0))(lambda: made_copy(*far_step(n - 1)).start())

    pl.when(is_zero)(lambda: stage_done(2, range(4)))
    pl.when(is_one)(lambda: stage_done(2, (1, 2, 3)))

    def taps(lag, j):
        return wt[lag, columns(j), :]

    def temporal(lag, ref, q, i):
        lhs = jnp.concatenate([ref[q, m, rows_of(i), :] for m in range(2)], axis=1)
        rhs = jnp.concatenate([taps(lag, q), taps(lag, q + 2)], axis=0)
        return jnp.dot(lhs, rhs, preferred_element_type=jnp.float32)

    @pl.loop(0, chunks)
    def _(n):
        acc[rows_of(n), :] = temporal(1, own, 0, n) + temporal(1, own, 1, n) + tb_ref[...]

    pl.when(aid_any)(lambda: made_copy(*far_step(2 * FAR_CHUNKS - 1)).start())
    wait_sends()

    @pl.when(is_relay)
    def _():
        for n in range(FLOWS):
            from_relay(n, partner).wait_send()

    x_before = jnp.where(far_before, x, (t + tiles - 1) % tiles // 8)
    x_after = jnp.where(far_after, x, (t + 1) % tiles // 8)
    for p in range(2):
        @pl.loop(0, chunks)
        def _(n, p=p):
            i = chunks - 1 - n
            rows = rows_of(i)
            for side, there, x_there in ((0, has_before, x_before), (1, has_after, x_after)):
                q = (x_there + p) % 2
                pl.when(exchanged(side))(lambda: hcopy(q, i, 1 - side).wait_recv())
                from_aid = jnp.logical_and((far_before, far_after)[side], i >= FAR_CHUNKS)
                pl.when(from_aid)(lambda: made_copy(q, i - FAR_CHUNKS).wait_recv())

                @pl.when(there)
                def _():
                    acc[rows, :] += temporal(2 * side, near.at[side], q, i)

            if p == 1:
                outv[rows, :] = acc[rows, :].astype(jnp.bfloat16)

    @pl.loop(0, chunks)
    def _(i):
        for side in range(2):
            @pl.when(exchanged(side))
            def _():
                for q in range(2):
                    hcopy(q, i, side).wait_send()

    @pl.when(aid_any)
    def _():
        for q in range(2):
            for i in range(FAR_CHUNKS):
                made_copy(q, i).wait_send()


def per_device(videos, spatial_filter, temporal_filter, spatial_bias, temporal_bias):
    _, _, height, breadth, chans = videos.shape
    shard = spatial_filter.shape[1]
    pixels = height * breadth
    blocks = chans // BLOCK
    chunks = pixels // ROWS
    far_pixels = FAR_CHUNKS * ROWS + breadth
    bf = jnp.bfloat16
    anywhere = pl.BlockSpec(memory_space=pl.ANY)
    vmem = pl.BlockSpec(memory_space=pltpu.VMEM)
    dma = pltpu.SemaphoreType.DMA
    out = pl.pallas_call(
        functools.partial(kernel, (height, breadth, chans, shard)),
        out_shape=pltpu.VMEM((pixels, chans), bf),
        in_specs=[anywhere] * 5,
        out_specs=vmem,
        scratch_shapes=[
            pltpu.VMEM((pixels + 2 * breadth, 3 * chans), bf),
            pltpu.VMEM((far_pixels + breadth, 3 * chans), bf),
            pltpu.VMEM((far_pixels, chans), bf),
            pltpu.VMEM((FLOWS, RELAYED * breadth, chans), bf),
            pltpu.VMEM((2, blocks // 2, FAR_CHUNKS * ROWS, BLOCK), bf),
            pltpu.VMEM((blocks, 2, TAPS_S, chans // 2, BLOCK), bf),
            pltpu.VMEM((TAPS_T, chans, chans), bf),
            pltpu.VMEM((2, blocks // 2, pixels, BLOCK), bf),
            pltpu.VMEM((2, 2, blocks // 2, pixels, BLOCK), bf),
            pltpu.VMEM((pixels, chans), jnp.float32),
            pltpu.VMEM((blocks, 1, BLOCK), jnp.float32),
            pltpu.VMEM((1, chans), jnp.float32),
            dma((8,)),
            dma((4, 11)), dma((4, 9)),
            dma((2, 4)), dma((2, 4)),
            dma((2, 4)), dma((2, 4)),
            dma((2, 2 * chunks)), dma((2, 2 * chunks)),
            dma((2, 3)),
            dma((2, FLOWS)),
            dma((2, FAR_CHUNKS)), dma((2, FAR_CHUNKS)),
        ],
        compiler_params=pltpu.CompilerParams(
            collective_id=0, has_side_effects=True, vmem_limit_bytes=56 * 1024 * 1024
        ),
    )(
        videos.reshape(pixels, chans),
        spatial_filter,
        temporal_filter,
        spatial_bias.reshape(blocks, 1, BLOCK),
        temporal_bias.reshape(1, chans),
    )
    return out.reshape(videos.shape)


def solution(mesh):
    return jax.shard_map(
        per_device,
        mesh=mesh,
        in_specs=(
            P("dp", "tile", None, None, None),
            P(None, "dp", None),
            P(None, "dp", None),
            P(),
            P(),
        ),
        out_specs=P("dp", "tile", None, None, None),
        check_vma=False,
    )
```

```python
import functools

import jax
import jax.numpy as jnp
from jax import lax
from jax.experimental import pallas as pl
from jax.experimental.pallas import tpu as pltpu
from jax.sharding import PartitionSpec as P

BLOCK = 128
ROWS = 512
FAR_CHUNKS = 2
RELAYED = 4
FLOWS = 3
TAPS_S, TAPS_T = 9, 3
MESH = pl.DeviceIdType.MESH


def kernel(
    dims, vid_hbm, ws_hbm, wt_hbm, sb_hbm, tb_hbm, outv,
    xcat, xcat_far, vid_far, relayed, made, wb, wt, own, near, acc, sb_ref, tb_ref,
    local_sem, wsend, wrecv, xsend, xrecv, psend, precv, hsend, hrecv, vsem, rsem, csend, crecv,
):
    height, breadth, chans, shard = dims
    pixels = height * breadth
    chunks = pixels // ROWS
    blocks = chans // BLOCK
    group = chans // 2
    half = shard // 2

    dp, t = lax.axis_index("dp"), lax.axis_index("tile")
    tiles = lax.axis_size("tile")
    y, zh = dp // 2, dp % 2
    core, zl, x = t % 2, (t // 2) % 4, t // 8
    partner = t + 1 - 2 * core
    up, dn = ((y + 1) % 4) * 2 + zh, ((y + 3) % 4) * 2 + zh
    other = y * 2 + 1 - zh
    first, last = zl == 0, zl == 3
    edge = jnp.logical_or(first, last)
    base = t - zl * 2
    cross_edge = base + jnp.where(first, 6, 0)
    cross_inner = base + jnp.where(first, 4, 2)
    inner_source = base + jnp.where(zl == 1, 6, 0)
    x_next, x_prev = (t + 8) % tiles, (t + tiles - 8) % tiles
    has_before, has_after = t > 0, t < tiles - 1
    far_before = jnp.logical_and(t % 8 == 0, has_before)
    far_after = jnp.logical_and(t % 8 == 7, has_after)
    far_any = jnp.logical_or(far_before, far_after)
    aid_before = jnp.logical_and(t % 8 == 1, t > 1)
    aid_after = jnp.logical_and(t % 8 == 6, t < tiles - 2)
    aid_any = jnp.logical_or(aid_before, aid_after)
    team = jnp.logical_or(far_any, aid_any)
    far_side = jnp.where(jnp.logical_or(far_after, aid_after), 1, 0)
    two_off = jnp.where(far_side == 1, t + 2, t - 2)
    feeding_relay = jnp.where(aid_after, 0, tiles - 1)
    far_tile = jnp.where(far_after, t + 1, t - 1)
    is_relay = jnp.logical_or(t == 0, t == tiles - 1)
    my_relay = jnp.where(far_after, tiles - 1, 0)
    flow = jnp.where(far_after, x, x - 1)
    x_free = jnp.where(jnp.logical_or(first, zl == 2), FLOWS, 0)
    in_free = x == x_free
    x_across = (t + 16) % tiles
    is_one = core == 1
    is_zero = core == 0

    block_a, block_b, block_c, block_d = x, (x + 2) % 4, (x + 1) % 4, (x + 3) % 4
    block_e, cross_e = jnp.where(first, block_d, block_c), jnp.where(first, block_c, block_d)
    ring_blocks = {0: block_a, 1: block_b, 3: block_e}
    carried = jnp.where(is_zero, zh, 1 - zh)

    def remote(src, dst, ssem, rsem, to_dp, to_tile):
        return pltpu.make_async_remote_copy(
            src_ref=src, dst_ref=dst, send_sem=ssem, recv_sem=rsem,
            device_id={"dp": to_dp, "tile": to_tile}, device_id_type=MESH,
        )

    def columns(j):
        return pl.ds(pl.multiple_of(j * BLOCK, BLOCK), BLOCK)

    def block_piece(j, y_at, z_at, low=0, count=None):
        count = shard if count is None else count
        return wb.at[j, z_at, :, pl.ds(pl.multiple_of(y_at * shard + low, half), count), :]

    def piece(g, y_at, z_at, low=0, count=None):
        if g != 2:
            return block_piece(ring_blocks[g], y_at, z_at, low, count)
        count = shard if count is None else count
        return wt.at[:, pl.ds(pl.multiple_of((y_at * 2 + z_at) * shard + low, half), count), :]

    def source(g):
        return wt_hbm if g == 2 else ws_hbm.at[:, :, columns(ring_blocks[g])]

    vid_copy = pltpu.make_async_copy(vid_hbm, outv, local_sem.at[5])
    loads = [
        pltpu.make_async_copy(ws_hbm.at[:, :, columns(j)], block_piece(j, y, zh), local_sem.at[n])
        for n, j in enumerate((block_a, block_b, block_c, block_d))
    ]
    loads.append(pltpu.make_async_copy(wt_hbm, piece(2, y, zh), local_sem.at[4]))
    loads.append(pltpu.make_async_copy(sb_hbm, sb_ref, local_sem.at[6]))
    loads.append(pltpu.make_async_copy(tb_hbm, tb_ref, local_sem.at[7]))
    vid_copy.start()
    for load in loads:
        load.start()

    barrier = pltpu.get_barrier_semaphore()

    def greet(to_dp, to_tile):
        pl.semaphore_signal(barrier, inc=1, device_id={"dp": to_dp, "tile": to_tile}, device_id_type=MESH)

    greet(dp, partner)
    greet(up, t)
    greet(dn, t)
    greet(dp, x_next)
    greet(dp, x_prev)
    greet(dp, x_across)

    @pl.when(far_any)
    def _():
        greet(dp, my_relay)

    @pl.when(aid_any)
    def _():
        greet(dp, feeding_relay)

    @pl.when(team)
    def _():
        greet(dp, two_off)

    @pl.when(is_relay)
    def _():
        for n in range(FLOWS):
            greet(dp, jnp.where(t == 0, 8 * n + 8, 8 * n + 7))
            greet(dp, jnp.where(t == 0, 8 * n + 6, 8 * n + 9))

    @pl.when(edge)
    def _():
        greet(other, cross_edge)
        greet(other, cross_inner)

    @pl.when(jnp.logical_not(edge))
    def _():
        greet(other, inner_source)

    @pl.when(has_before)
    def _():
        greet(dp, t - 1)

    @pl.when(has_after)
    def _():
        greet(dp, t + 1)

    one = lambda flag: jnp.where(flag, 1, 0)
    pl.semaphore_wait(barrier, 7 + one(edge) + one(has_before) + one(has_after) + 2 * one(team) + 2 * FLOWS * one(is_relay))

    def ring(g, send, recv, y_at, z_at, to_dp, to_tile, low=0, count=None, src=None):
        ref = piece(g, y_at, z_at, low, count)
        return remote(ref if src is None else src, ref, wsend.at[g, send], wrecv.at[g, recv], to_dp, to_tile)

    def from_x(n, k, y_at, to_tile):
        ref = block_piece(block_a, y_at, carried)
        return remote(ref, ref, xsend.at[n, k], xrecv.at[n, k], dp, to_tile)

    by_x = jnp.logical_not(first), jnp.logical_not(last)

    def y_of(k):
        return (y + k) % 4

    def spread(g, k):
        ring(g, 6 + k, 5 + k, y_of(k), carried, dp, partner).start()
        if g == 0:
            pl.when(by_x[0])(lambda: from_x(0, k, y_of(k), x_next).start())
            pl.when(by_x[1])(lambda: from_x(1, k, y_of(k), x_prev).start())

    def cross_copy():
        return remote(
            ws_hbm.at[:, :, columns(cross_e)], block_piece(cross_e, y, zh), wsend.at[3, 0], wrecv.at[3, 0],
            other, cross_edge,
        )

    def start_z(g):
        if g == 3:
            cross_copy().start()
            return
        inner = lambda: ring(g, 1, 0, y, zh, other, cross_inner, src=source(g)).start()
        if g == 2:
            pl.when(in_free)(inner)
        else:
            inner()
        ring(g, 0, 0, y, zh, other, cross_edge, src=source(g)).start()

    def start_y(g, src=None):
        ring(g, 2, 1, y, carried, up, t, src=src).start()
        ring(g, 3, 2, y, carried, dn, t, src=src).start()

    inner_source_of_two = jnp.logical_and(jnp.logical_not(edge), in_free)

    def share(slot, to_tile):
        return ring(2, slot, 0, y, 1 - zh, dp, to_tile)

    def stage_share():
        ring(2, 0, 0, y, 1 - zh, dp, partner).wait_recv()
        for slot, to_tile in ((0, x_next), (1, x_prev), (10, x_across)):
            share(slot, to_tile).start()

    def stage_z(g):
        arrived = lambda: ring(g, 0, 0, y, 1 - zh, dp, partner).wait_recv()
        if g == 2:
            pl.when(jnp.logical_not(inner_source_of_two))(arrived)
        else:
            arrived()
        start_y(g)
        spread(g, 0)

    def stage_y(g):
        ring(g, 2, 1, y_of(3), carried, up, t).wait_recv()
        ring(g, 4, 3, y_of(3), carried, up, t, 0, half).start()
        ring(g, 3, 2, y_of(1), carried, dn, t).wait_recv()
        ring(g, 5, 4, y_of(1), carried, dn, t, half, half).start()
        spread(g, 3)
        spread(g, 1)

    def stage_far(g):
        ring(g, 4, 3, y_of(2), carried, up, t, 0, half).wait_recv()
        ring(g, 5, 4, y_of(2), carried, dn, t, half, half).wait_recv()
        spread(g, 2)

    def stage_done(g, ks):
        for k in ks:
            ring(g, 6 + k, 5 + k, y_of(k), 1 - carried, dp, partner).wait_recv()

    def onward(n, k, z_at):
        ref = block_piece((block_d, block_c)[n], y_of(k), z_at)
        return remote(ref, ref, psend.at[n, k], precv.at[n, k], dp, partner)

    def stage_x(k):
        for n in range(2):
            @pl.when(by_x[n])
            def _():
                ref = block_piece((block_d, block_c)[n], y_of(k), carried)
                remote(ref, ref, xsend.at[n, k], xrecv.at[n, k], dp, x_next).wait_recv()
                onward(n, k, carried).start()

    def stage_x_done(ks):
        for n in range(2):
            @pl.when(by_x[n])
            def _():
                for k in ks:
                    onward(n, k, 1 - carried).wait_recv()

        pl.when(edge)(lambda: stage_done(3, ks))

    def wait_ring(g):
        for slot in (2, 3):
            ring(g, slot, 0, y, carried, up, t).wait_send()
        for slot in (4, 5):
            ring(g, slot, 0, y, carried, up, t, 0, half).wait_send()
        for k in range(1, 4):
            ring(g, 6 + k, 5 + k, y, carried, dp, partner).wait_send()

        @pl.when(is_one)
        def _():
            ring(g, 6, 5, y, carried, dp, partner).wait_send()

    def wait_sends():
        for g in range(3):
            wait_ring(g)
        pl.when(edge)(lambda: wait_ring(3))

        @pl.when(jnp.logical_and(is_one, edge))
        def _():
            for g in range(3):
                ring(g, 0, 0, y, zh, other, cross_edge).wait_send()
            for g in range(2):
                ring(g, 1, 0, y, zh, other, cross_inner).wait_send()
            pl.when(in_free)(lambda: ring(2, 1, 0, y, zh, other, cross_inner).wait_send())
            cross_copy().wait_send()

        @pl.when(jnp.logical_and(is_one, inner_source_of_two))
        def _():
            for slot in (0, 1, 10):
                share(slot, x_next).wait_send()

        def wait_x(n, k):
            from_x(n, k, y, x_next).wait_send()
            onward(n, k, carried).wait_send()

        for n in range(2):
            @pl.when(by_x[n])
            def _():
                for k in range(1, 4):
                    wait_x(n, k)

            pl.when(jnp.logical_and(by_x[n], is_one))(lambda: wait_x(n, 0))

    def rows_of(i):
        return pl.ds(pl.multiple_of(i * ROWS, ROWS), ROWS)

    def hcopy(q, i, side):
        slot = q * chunks + i
        return remote(
            own.at[q, :, rows_of(i), :], near.at[1 - side, q, :, rows_of(i), :],
            hsend.at[side], hrecv.at[side, slot], dp, t - 1 if side == 0 else t + 1,
        )

    def exchanged(side):
        there, far = ((has_before, far_before), (has_after, far_after))[side]
        return jnp.logical_and(there, jnp.logical_not(far))

    def send_hidden(p, i):
        for side in range(2):
            pl.when(exchanged(side))(lambda: hcopy((x + p) % 2, i, side).start())

    far_rows = (FAR_CHUNKS * ROWS // breadth + 1) * breadth
    half_rows = far_rows - breadth
    kept = half_rows - RELAYED * breadth
    passed = pl.ds(half_rows + kept, RELAYED * breadth)

    def far_upper():
        rows = pl.ds(0, half_rows)
        return remote(vid_hbm.at[rows], vid_far.at[rows], vsem.at[0, 0], vsem.at[1, 0], dp, far_tile)

    def far_lower():
        return remote(
            vid_hbm.at[pl.ds(half_rows, kept)], vid_far.at[pl.ds(breadth, kept)],
            vsem.at[0, 1], vsem.at[1, 1], dp, two_off,
        )

    def hand_row():
        src = pl.multiple_of(jnp.where(far_any, half_rows - breadth, breadth), breadth)
        dst = pl.multiple_of(jnp.where(far_any, 0, half_rows), breadth)
        return remote(
            vid_far.at[pl.ds(src, breadth)], vid_far.at[pl.ds(dst, breadth)], vsem.at[0, 3], vsem.at[1, 3], dp, partner
        )

    def to_relay():
        return remote(vid_hbm.at[passed], relayed.at[flow], vsem.at[0, 2], rsem.at[0, flow], dp, my_relay)

    def from_relay(n, to_tile):
        return remote(
            relayed.at[n], vid_far.at[pl.ds(breadth + kept, RELAYED * breadth)], rsem.at[1, n], vsem.at[1, 2], dp, to_tile
        )

    def relay_pass(distance):
        n = jnp.where(t == 0, distance - 1, FLOWS - distance)

        @pl.when(is_relay)
        def _():
            remote(vid_hbm.at[passed], relayed.at[n], vsem.at[0, 2], rsem.at[0, n], dp, partner).wait_recv()
            from_relay(n, jnp.where(t == 0, 8 * n + 6, 8 * n + 9)).start()

    def prepare(src, dst, lines, above=1):
        lanes = lax.broadcasted_iota(jnp.int32, (breadth, BLOCK), 1)
        at = lax.broadcasted_iota(jnp.int32, (breadth, group), 0)

        @pl.loop(0, lines)
        def _(r):
            line = src[pl.ds(pl.multiple_of(r * breadth, breadth), breadth), :].astype(jnp.float32)
            rows = pl.ds(pl.multiple_of((r + above) * breadth, breadth), breadth)
            parts = [line[:, n * BLOCK : (n + 1) * BLOCK] for n in range(blocks)]
            turned = [pltpu.roll(part, shard, 1) for part in parts]
            low = lanes < shard
            for z_at in range(2):
                left_of, right_of = (parts, turned) if z_at == 0 else (turned, parts)
                mid = jnp.concatenate(
                    [jnp.where(low, left_of[n], right_of[n + 1]) for n in range(0, blocks, 2)], axis=1
                )
                left = jnp.where(at == 0, 0.0, pltpu.roll(mid, 1, 0))
                right = jnp.where(at == breadth - 1, 0.0, pltpu.roll(mid, breadth - 1, 0))
                for dx, value in enumerate((left, mid, right)):
                    start = (3 * z_at + dx) * group
                    dst[rows, start : start + group] = value.astype(jnp.bfloat16)

    def half_dot(xs, z_at, pair, i):
        total = None
        for dy in range(3):
            start = pl.multiple_of(i * ROWS + dy * breadth, breadth)
            lhs = xs[pl.ds(start, ROWS), pl.ds(pl.multiple_of(z_at * (3 * group), 3 * group), 3 * group)]
            rhs = jnp.concatenate(
                [wb[j, z_at, 3 * dy : 3 * dy + 3].reshape(3 * group, BLOCK) for j in pair], axis=1
            )
            part = jnp.dot(lhs, rhs, preferred_element_type=jnp.float32)
            total = part if total is None else total + part
        return total

    def activate(total, pair):
        total = total + jnp.concatenate([sb_ref[j] for j in pair], axis=1)
        return (total / (1.0 + jnp.exp(-total))).astype(jnp.bfloat16)

    pairs = (block_a, block_b), (block_c, block_d)

    def spatial_first(p, i):
        acc[rows_of(i), 2 * BLOCK * p : 2 * BLOCK * (p + 1)] = half_dot(xcat, zh, pairs[p], i)

    def spatial_rest(p, i):
        total = acc[rows_of(i), 2 * BLOCK * p : 2 * BLOCK * (p + 1)] + half_dot(xcat, 1 - zh, pairs[p], i)
        hidden = activate(total, pairs[p])
        for n, j in enumerate(pairs[p]):
            own[j % 2, j // 2, rows_of(i), :] = hidden[:, n * BLOCK : (n + 1) * BLOCK]

    @pl.when(jnp.logical_and(is_one, edge))
    def _():
        for g in (0, 1, 3, 2):
            start_z(g)

    @pl.when(is_zero)
    def _():
        start_y(0, source(0))
        start_y(1, source(1))
        pl.when(edge)(lambda: start_y(3, source(3)))

    @pl.when(far_any)
    def _():
        to_relay().start()
        far_upper().start()
        far_lower().start()


    zeros = jnp.zeros((breadth, 6 * group), jnp.bfloat16)
    xcat[0:breadth, :] = zeros
    xcat[breadth + pixels :, :] = zeros
    vid_copy.wait()
    prepare(outv, xcat, height)
    for load in loads:
        load.wait()

    @pl.when(is_zero)
    def _():
        stage_y(0)
        stage_y(1)
        relay_pass(1)
        stage_far(0)
        stage_far(1)

    @pl.when(is_one)
    def _():
        stage_z(0)
        stage_z(1)
        relay_pass(1)
        stage_y(0)
        stage_y(1)
        pl.when(edge)(lambda: stage_z(3))
        stage_done(0, (1, 2, 3))
        stage_done(1, (1, 2, 3))

    relay_pass(2)
    relay_pass(3)
    edge_zero, edge_one = jnp.logical_and(edge, is_zero), jnp.logical_and(edge, is_one)
    sharing = jnp.logical_and(is_one, inner_source_of_two)

    def on(flag, n, at, *stages):
        @pl.when(jnp.logical_and(flag, n == at))
        def _():
            for stage in stages:
                stage()

    @pl.loop(0, chunks)
    def _(n):
        spatial_first(0, chunks - 1 - n)
        on(is_zero, n, 1, lambda: stage_x(3))
        on(is_zero, n, 2, lambda: stage_x(1))
        on(is_zero, n, 3, lambda: stage_x(2))
        on(is_one, n, 0, lambda: stage_far(0))
        on(is_one, n, 1, lambda: stage_far(1))
        on(edge_zero, n, 0, lambda: stage_y(3))
        on(edge_one, n, 2, lambda: stage_y(3))
        on(is_zero, n, 2, lambda: start_y(2, source(2)))
        on(edge_zero, n, 3, lambda: stage_far(3))
        on(sharing, n, 3, stage_share)

    @pl.when(is_zero)
    def _():
        stage_done(0, range(4))
        stage_done(1, range(4))

    @pl.loop(0, chunks)
    def _(n):
        spatial_rest(0, chunks - 1 - n)

        @pl.when(n > 0)
        def _():
            send_hidden(0, chunks - n)

        on(is_one, n, 0, lambda: stage_x(0))
        on(is_one, n, 1, lambda: stage_x(3))
        on(edge_one, n, 0, lambda: stage_far(3))
        on(is_one, n, 2, lambda: stage_x(1))
        on(is_one, n, 3, lambda: stage_z(2))

    pl.when(is_one)(lambda: stage_x_done((1, 2, 3)))

    @pl.loop(0, chunks)
    def _(n):
        spatial_first(1, chunks - 1 - n)

        @pl.when(n == 0)
        def _():
            send_hidden(0, 0)

        on(is_one, n, 0, lambda: stage_x(2))
        on(is_zero, n, 2, lambda: stage_y(2))

    pl.when(is_zero)(lambda: stage_x_done(range(4)))

    @pl.loop(0, chunks)
    def _(n):
        spatial_rest(1, chunks - 1 - n)

        @pl.when(n > 0)
        def _():
            send_hidden(1, chunks - n)

        on(far_any, n, 1, lambda: far_upper().wait_recv(), lambda: hand_row().start())
        on(aid_any, n, 0, lambda: far_lower().wait_recv(), lambda: hand_row().start())
        on(is_one, n, 0, lambda: stage_y(2))

    stage_far(2)
    send_hidden(1, 0)

    def made_copy(q, i):
        rows = rows_of(i + FAR_CHUNKS)
        return remote(
            made.at[q, :, rows_of(i), :], near.at[far_side, q, :, rows, :], csend.at[q, i], crecv.at[q, i], dp, partner
        )

    def far_step(n):
        p, i = n // FAR_CHUNKS, n % FAR_CHUNKS
        return (x + p) % 2, i

    @pl.when(far_any)
    def _():
        far_upper().wait_send()
        far_lower().wait_send()
        to_relay().wait_send()

    @pl.when(aid_any)
    def _():
        from_relay(0, partner).wait_recv()

    @pl.when(team)
    def _():
        hand_row().wait()
        blank = jnp.where(far_any, 0, far_rows)
        xcat_far[pl.ds(pl.multiple_of(blank, breadth), breadth), :] = zeros
        prepare(vid_far, xcat_far, far_rows // breadth, one(far_any))

        @pl.loop(0, 2 * FAR_CHUNKS)
        def _(n):
            p, i = n // FAR_CHUNKS, n % FAR_CHUNKS
            pair = ((x + p) % 4, (x + p + 2) % 4)
            hidden = activate(half_dot(xcat_far, 0, pair, i) + half_dot(xcat_far, 1, pair, i), pair)

            @pl.when(far_any)
            def _():
                for m, j in enumerate(pair):
                    near[far_side, j % 2, j // 2, rows_of(i), :] = hidden[:, m * BLOCK : (m + 1) * BLOCK]

            @pl.when(aid_any)
            def _():
                for m, j in enumerate(pair):
                    made[j % 2, j // 2, rows_of(i), :] = hidden[:, m * BLOCK : (m + 1) * BLOCK]

            pl.when(jnp.logical_and(aid_any, n > 0))(lambda: made_copy(*far_step(n - 1)).start())

    pl.when(is_zero)(lambda: stage_done(2, range(4)))
    pl.when(is_one)(lambda: stage_done(2, (1, 2, 3)))

    def taps(lag, j):
        return wt[lag, columns(j), :]

    def temporal(lag, ref, q, i):
        lhs = jnp.concatenate([ref[q, m, rows_of(i), :] for m in range(2)], axis=1)
        rhs = jnp.concatenate([taps(lag, q), taps(lag, q + 2)], axis=0)
        return jnp.dot(lhs, rhs, preferred_element_type=jnp.float32)

    @pl.when(jnp.logical_not(team))
    def _():
        @pl.loop(0, chunks)
        def _(n):
            acc[rows_of(n), :] = temporal(1, own, 0, n) + temporal(1, own, 1, n) + tb_ref[...]

    pl.when(aid_any)(lambda: made_copy(*far_step(2 * FAR_CHUNKS - 1)).start())
    wait_sends()

    @pl.when(is_relay)
    def _():
        for n in range(FLOWS):
            from_relay(n, partner).wait_send()

    there, x_there = (has_before, has_after), ((t + tiles - 1) % tiles // 8, (t + 1) % tiles // 8)

    @pl.when(jnp.logical_not(team))
    def _():
        for p in range(2):
            @pl.loop(0, chunks)
            def _(n, p=p):
                i = chunks - 1 - n
                rows = rows_of(i)
                for side in range(2):
                    @pl.when(there[side])
                    def _():
                        q = (x_there[side] + p) % 2
                        hcopy(q, i, 1 - side).wait_recv()
                        acc[rows, :] += temporal(2 * side, near.at[side], q, i)

                if p == 1:
                    outv[rows, :] = acc[rows, :].astype(jnp.bfloat16)

    @pl.when(aid_any)
    def _():
        z_side = jnp.where(aid_before, 1, 0)
        q_first = jnp.where(aid_before, x_there[1], x_there[0]) % 2

        @pl.loop(0, chunks)
        def _(n):
            i = chunks - 1 - n

            @pl.when(aid_before)
            def _():
                hcopy(q_first, i, 0).wait_recv()
                for q in range(2):
                    hcopy(q, i, 1).wait_recv()

            @pl.when(aid_after)
            def _():
                hcopy(q_first, i, 1).wait_recv()
                for q in range(2):
                    hcopy(q, i, 0).wait_recv()

            total = tb_ref[...] + temporal(2 * z_side, near.at[z_side], q_first, i)
            for q in range(2):
                total = total + temporal(1, own, q, i) + temporal(2 - 2 * z_side, near.at[1 - z_side], q, i)
            acc[rows_of(i), :] = total

        @pl.loop(0, chunks)
        def _(n):
            i = chunks - 1 - n
            pl.when(aid_before)(lambda: hcopy(1 - q_first, i, 0).wait_recv())
            pl.when(aid_after)(lambda: hcopy(1 - q_first, i, 1).wait_recv())
            rest = temporal(2 * z_side, near.at[z_side], 1 - q_first, i)
            outv[rows_of(i), :] = (acc[rows_of(i), :] + rest).astype(jnp.bfloat16)

    @pl.when(far_any)
    def _():
        @pl.loop(0, chunks)
        def _(i):
            pl.when(far_before)(lambda: [hcopy(q, i, 0).wait_recv() for q in range(2)] and None)
            pl.when(far_after)(lambda: [hcopy(q, i, 1).wait_recv() for q in range(2)] and None)

            @pl.when(i >= FAR_CHUNKS)
            def _():
                for q in range(2):
                    made_copy(q, i - FAR_CHUNKS).wait_recv()

            total = tb_ref[...]
            for q in range(2):
                total = total + temporal(1, own, q, i)
                for side in range(2):
                    total = total + temporal(2 * side, near.at[side], q, i)
            outv[rows_of(i), :] = total.astype(jnp.bfloat16)

    for side in range(2):
        @pl.when(exchanged(side))
        def _():
            remote(own, near.at[1 - side], hsend.at[side], hrecv.at[side, 0], dp, partner).wait_send()

    @pl.when(aid_any)
    def _():
        for q in range(2):
            for i in range(FAR_CHUNKS):
                made_copy(q, i).wait_send()


def per_device(videos, spatial_filter, temporal_filter, spatial_bias, temporal_bias):
    _, _, height, breadth, chans = videos.shape
    shard = spatial_filter.shape[1]
    pixels = height * breadth
    blocks = chans // BLOCK
    chunks = pixels // ROWS
    far_pixels = FAR_CHUNKS * ROWS + breadth
    bf = jnp.bfloat16
    anywhere = pl.BlockSpec(memory_space=pl.ANY)
    vmem = pl.BlockSpec(memory_space=pltpu.VMEM)
    dma = pltpu.SemaphoreType.DMA
    out = pl.pallas_call(
        functools.partial(kernel, (height, breadth, chans, shard)),
        out_shape=pltpu.VMEM((pixels, chans), bf),
        in_specs=[anywhere] * 5,
        out_specs=vmem,
        scratch_shapes=[
            pltpu.VMEM((pixels + 2 * breadth, 3 * chans), bf),
            pltpu.VMEM((far_pixels + breadth, 3 * chans), bf),
            pltpu.VMEM((far_pixels, chans), bf),
            pltpu.VMEM((FLOWS, RELAYED * breadth, chans), bf),
            pltpu.VMEM((2, blocks // 2, FAR_CHUNKS * ROWS, BLOCK), bf),
            pltpu.VMEM((blocks, 2, TAPS_S, chans // 2, BLOCK), bf),
            pltpu.VMEM((TAPS_T, chans, chans), bf),
            pltpu.VMEM((2, blocks // 2, pixels, BLOCK), bf),
            pltpu.VMEM((2, 2, blocks // 2, pixels, BLOCK), bf),
            pltpu.VMEM((pixels, chans), jnp.float32),
            pltpu.VMEM((blocks, 1, BLOCK), jnp.float32),
            pltpu.VMEM((1, chans), jnp.float32),
            dma((8,)),
            dma((4, 11)), dma((4, 9)),
            dma((2, 4)), dma((2, 4)),
            dma((2, 4)), dma((2, 4)),
            dma((2,)), dma((2, 2 * chunks)),
            dma((2, 4)),
            dma((2, FLOWS)),
            dma((2, FAR_CHUNKS)), dma((2, FAR_CHUNKS)),
        ],
        compiler_params=pltpu.CompilerParams(
            collective_id=0, has_side_effects=True, vmem_limit_bytes=56 * 1024 * 1024
        ),
    )(
        videos.reshape(pixels, chans),
        spatial_filter,
        temporal_filter,
        spatial_bias.reshape(blocks, 1, BLOCK),
        temporal_bias.reshape(1, chans),
    )
    return out.reshape(videos.shape)


def solution(mesh):
    return jax.shard_map(
        per_device,
        mesh=mesh,
        in_specs=(
            P("dp", "tile", None, None, None),
            P(None, "dp", None),
            P(None, "dp", None),
            P(),
            P(),
        ),
        out_specs=P("dp", "tile", None, None, None),
        check_vma=False,
    )
```

```python
import functools

import jax
import jax.numpy as jnp
from jax import lax
from jax.experimental import pallas as pl
from jax.experimental.pallas import tpu as pltpu
from jax.sharding import PartitionSpec as P

BLOCK = 128
ROWS = 512
FAR_CHUNKS = 2
RELAYED = 4
FLOWS = 3
TAPS_S, TAPS_T = 9, 3
MESH = pl.DeviceIdType.MESH


def kernel(
    dims, vid_hbm, ws_hbm, wt_hbm, sb_hbm, tb_hbm, outv,
    xcat, xcat_far, vid_far, relayed, made, wb, wt, own, near, acc, sb_ref, tb_ref,
    local_sem, wsend, wrecv, xsend, xrecv, psend, precv, hsend, hrecv, vsem, rsem, csend, crecv,
):
    height, breadth, chans, shard = dims
    pixels = height * breadth
    chunks = pixels // ROWS
    blocks = chans // BLOCK
    group = chans // 2
    half = shard // 2

    dp, t = lax.axis_index("dp"), lax.axis_index("tile")
    tiles = lax.axis_size("tile")
    y, zh = dp // 2, dp % 2
    core, zl, x = t % 2, (t // 2) % 4, t // 8
    partner = t + 1 - 2 * core
    up, dn = ((y + 1) % 4) * 2 + zh, ((y + 3) % 4) * 2 + zh
    other = y * 2 + 1 - zh
    first, last = zl == 0, zl == 3
    edge = jnp.logical_or(first, last)
    base = t - zl * 2
    cross_edge = base + jnp.where(first, 6, 0)
    cross_inner = base + jnp.where(first, 4, 2)
    inner_source = base + jnp.where(zl == 1, 6, 0)
    x_next, x_prev = (t + 8) % tiles, (t + tiles - 8) % tiles
    has_before, has_after = t > 0, t < tiles - 1
    far_before = jnp.logical_and(t % 8 == 0, has_before)
    far_after = jnp.logical_and(t % 8 == 7, has_after)
    far_any = jnp.logical_or(far_before, far_after)
    aid_before = jnp.logical_and(t % 8 == 1, t > 1)
    aid_after = jnp.logical_and(t % 8 == 6, t < tiles - 2)
    aid_any = jnp.logical_or(aid_before, aid_after)
    team = jnp.logical_or(far_any, aid_any)
    far_side = jnp.where(jnp.logical_or(far_after, aid_after), 1, 0)
    two_off = jnp.where(far_side == 1, t + 2, t - 2)
    feeding_relay = jnp.where(aid_after, 0, tiles - 1)
    far_tile = jnp.where(far_after, t + 1, t - 1)
    is_relay = jnp.logical_or(t == 0, t == tiles - 1)
    my_relay = jnp.where(far_after, tiles - 1, 0)
    flow = jnp.where(far_after, x, x - 1)
    x_free = jnp.where(jnp.logical_or(first, zl == 2), FLOWS, 0)
    in_free = x == x_free
    x_across = (t + 16) % tiles
    is_one = core == 1
    is_zero = core == 0

    block_a, block_b, block_c, block_d = x, (x + 2) % 4, (x + 1) % 4, (x + 3) % 4
    block_e, cross_e = jnp.where(first, block_d, block_c), jnp.where(first, block_c, block_d)
    ring_blocks = {0: block_a, 1: block_b, 3: block_e}
    carried = jnp.where(is_zero, zh, 1 - zh)

    def remote(src, dst, ssem, rsem, to_dp, to_tile):
        return pltpu.make_async_remote_copy(
            src_ref=src, dst_ref=dst, send_sem=ssem, recv_sem=rsem,
            device_id={"dp": to_dp, "tile": to_tile}, device_id_type=MESH,
        )

    def columns(j):
        return pl.ds(pl.multiple_of(j * BLOCK, BLOCK), BLOCK)

    def block_piece(j, y_at, z_at, low=0, count=None):
        count = shard if count is None else count
        return wb.at[j, z_at, :, pl.ds(pl.multiple_of(y_at * shard + low, half), count), :]

    def piece(g, y_at, z_at, low=0, count=None):
        if g != 2:
            return block_piece(ring_blocks[g], y_at, z_at, low, count)
        count = shard if count is None else count
        return wt.at[:, pl.ds(pl.multiple_of((y_at * 2 + z_at) * shard + low, half), count), :]

    def source(g):
        return wt_hbm if g == 2 else ws_hbm.at[:, :, columns(ring_blocks[g])]

    vid_copy = pltpu.make_async_copy(vid_hbm, outv, local_sem.at[5])
    loads = [
        pltpu.make_async_copy(ws_hbm.at[:, :, columns(j)], block_piece(j, y, zh), local_sem.at[n])
        for n, j in enumerate((block_a, block_b, block_c, block_d))
    ]
    loads.append(pltpu.make_async_copy(wt_hbm, piece(2, y, zh), local_sem.at[4]))
    loads.append(pltpu.make_async_copy(sb_hbm, sb_ref, local_sem.at[6]))
    loads.append(pltpu.make_async_copy(tb_hbm, tb_ref, local_sem.at[7]))
    vid_copy.start()
    for load in loads:
        load.start()

    barrier = pltpu.get_barrier_semaphore()

    def greet(to_dp, to_tile):
        pl.semaphore_signal(barrier, inc=1, device_id={"dp": to_dp, "tile": to_tile}, device_id_type=MESH)

    greet(dp, partner)
    greet(up, t)
    greet(dn, t)
    greet(dp, x_next)
    greet(dp, x_prev)
    greet(dp, x_across)

    @pl.when(far_any)
    def _():
        greet(dp, my_relay)

    @pl.when(aid_any)
    def _():
        greet(dp, feeding_relay)

    @pl.when(team)
    def _():
        greet(dp, two_off)

    @pl.when(is_relay)
    def _():
        for n in range(FLOWS):
            greet(dp, jnp.where(t == 0, 8 * n + 8, 8 * n + 7))
            greet(dp, jnp.where(t == 0, 8 * n + 6, 8 * n + 9))

    @pl.when(edge)
    def _():
        greet(other, cross_edge)
        greet(other, cross_inner)

    @pl.when(jnp.logical_not(edge))
    def _():
        greet(other, inner_source)

    @pl.when(has_before)
    def _():
        greet(dp, t - 1)

    @pl.when(has_after)
    def _():
        greet(dp, t + 1)

    one = lambda flag: jnp.where(flag, 1, 0)
    pl.semaphore_wait(barrier, 7 + one(edge) + one(has_before) + one(has_after) + 2 * one(team) + 2 * FLOWS * one(is_relay))

    def ring(g, send, recv, y_at, z_at, to_dp, to_tile, low=0, count=None, src=None):
        ref = piece(g, y_at, z_at, low, count)
        return remote(ref if src is None else src, ref, wsend.at[g, send], wrecv.at[g, recv], to_dp, to_tile)

    def ring_many(g, send, recv, count):
        return ring(g, send, recv, 0, 0, dp, partner, 0, count * shard)

    def from_x(n, k, y_at, to_tile):
        ref = block_piece(block_a, y_at, carried)
        return remote(ref, ref, xsend.at[n], xrecv.at[n, k], dp, to_tile)

    by_x = jnp.logical_not(first), jnp.logical_not(last)

    def y_of(k):
        return (y + k) % 4

    def spread(g, k):
        ring(g, 3, 4, y_of(k), carried, dp, partner).start()
        if g == 0:
            pl.when(by_x[0])(lambda: from_x(0, k, y_of(k), x_next).start())
            pl.when(by_x[1])(lambda: from_x(1, k, y_of(k), x_prev).start())

    def cross_copy():
        return remote(
            ws_hbm.at[:, :, columns(cross_e)], block_piece(cross_e, y, zh), wsend.at[3, 0], wrecv.at[3, 0],
            other, cross_edge,
        )

    def start_z(g):
        if g == 3:
            cross_copy().start()
            return
        inner = lambda: ring(g, 1, 0, y, zh, other, cross_inner, src=source(g)).start()
        if g == 2:
            pl.when(in_free)(inner)
        else:
            inner()
        ring(g, 0, 0, y, zh, other, cross_edge, src=source(g)).start()

    def start_y(g, src=None):
        ring(g, 2, 1, y, carried, up, t, src=src).start()
        ring(g, 2, 2, y, carried, dn, t, src=src).start()

    inner_source_of_two = jnp.logical_and(jnp.logical_not(edge), in_free)

    def share(slot, to_tile):
        return ring(2, slot, 0, y, 1 - zh, dp, to_tile)

    def stage_share():
        ring(2, 0, 0, y, 1 - zh, dp, partner).wait_recv()
        for slot, to_tile in ((0, x_next), (0, x_prev), (0, x_across)):
            share(slot, to_tile).start()

    def stage_z(g):
        arrived = lambda: ring(g, 0, 0, y, 1 - zh, dp, partner).wait_recv()
        if g == 2:
            pl.when(jnp.logical_not(inner_source_of_two))(arrived)
        else:
            arrived()
        start_y(g)
        spread(g, 0)

    def stage_y(g):
        ring(g, 2, 1, y_of(3), carried, up, t).wait_recv()
        ring(g, 2, 3, y_of(3), carried, up, t, 0, half).start()
        ring(g, 2, 2, y_of(1), carried, dn, t).wait_recv()
        ring(g, 2, 3, y_of(1), carried, dn, t, half, half).start()
        spread(g, 3)
        spread(g, 1)

    def stage_far(g):
        ring(g, 2, 3, y_of(2), carried, up, t).wait_recv()
        spread(g, 2)

    def stage_done(g, ks):
        ring_many(g, 3, 4, len(ks)).wait_recv()

    def onward(n, k, z_at):
        ref = block_piece((block_d, block_c)[n], y_of(k), z_at)
        return remote(ref, ref, psend.at[n], precv.at[n], dp, partner)

    def many(n, count, send, recv):
        ref = block_piece(0, 0, 0, 0, count * shard)
        return remote(ref, ref, send.at[n], recv, dp, partner)

    def stage_x(k):
        for n in range(2):
            @pl.when(by_x[n])
            def _():
                ref = block_piece((block_d, block_c)[n], y_of(k), carried)
                remote(ref, ref, xsend.at[n], xrecv.at[n, k], dp, x_next).wait_recv()
                onward(n, k, carried).start()

    def stage_x_done(ks):
        for n in range(2):
            @pl.when(by_x[n])
            def _():
                many(n, len(ks), psend, precv.at[n]).wait_recv()

        pl.when(edge)(lambda: stage_done(3, ks))

    def by_core(wait):
        pl.when(is_zero)(lambda: wait(3))
        pl.when(is_one)(lambda: wait(4))

    def wait_ring(g):
        ring_many(g, 2, 0, 3).wait_send()
        by_core(lambda count: ring_many(g, 3, 0, count).wait_send())

    def wait_sends():
        for g in range(3):
            wait_ring(g)
        pl.when(edge)(lambda: wait_ring(3))

        @pl.when(jnp.logical_and(is_one, edge))
        def _():
            for g in range(3):
                ring(g, 0, 0, y, zh, other, cross_edge).wait_send()
            for g in range(2):
                ring(g, 1, 0, y, zh, other, cross_inner).wait_send()
            pl.when(in_free)(lambda: ring(2, 1, 0, y, zh, other, cross_inner).wait_send())
            cross_copy().wait_send()

        @pl.when(jnp.logical_and(is_one, inner_source_of_two))
        def _():
            ring_many(2, 0, 0, 3).wait_send()

        for n in range(2):
            @pl.when(by_x[n])
            def _():
                by_core(lambda count: many(n, count, xsend, xrecv.at[n, 0]).wait_send())
                by_core(lambda count: many(n, count, psend, precv.at[n]).wait_send())

    def rows_of(i):
        return pl.ds(pl.multiple_of(i * ROWS, ROWS), ROWS)

    def hcopy(q, i, side):
        slot = q * chunks + i
        return remote(
            own.at[q, :, rows_of(i), :], near.at[1 - side, q, :, rows_of(i), :],
            hsend.at[side], hrecv.at[side, slot], dp, t - 1 if side == 0 else t + 1,
        )

    def exchanged(side):
        there, far = ((has_before, far_before), (has_after, far_after))[side]
        return jnp.logical_and(there, jnp.logical_not(far))

    def send_hidden(p, i):
        for side in range(2):
            pl.when(exchanged(side))(lambda: hcopy((x + p) % 2, i, side).start())

    far_rows = (FAR_CHUNKS * ROWS // breadth + 1) * breadth
    half_rows = far_rows - breadth
    kept = half_rows - RELAYED * breadth
    passed = pl.ds(half_rows + kept, RELAYED * breadth)

    def far_upper():
        rows = pl.ds(0, half_rows)
        return remote(vid_hbm.at[rows], vid_far.at[rows], vsem.at[0, 0], vsem.at[1, 0], dp, far_tile)

    def far_lower():
        return remote(
            vid_hbm.at[pl.ds(half_rows, kept)], vid_far.at[pl.ds(breadth, kept)],
            vsem.at[0, 1], vsem.at[1, 1], dp, two_off,
        )

    def hand_row():
        src = pl.multiple_of(jnp.where(far_any, half_rows - breadth, breadth), breadth)
        dst = pl.multiple_of(jnp.where(far_any, 0, half_rows), breadth)
        return remote(
            vid_far.at[pl.ds(src, breadth)], vid_far.at[pl.ds(dst, breadth)], vsem.at[0, 3], vsem.at[1, 3], dp, partner
        )

    def to_relay():
        return remote(vid_hbm.at[passed], relayed.at[flow], vsem.at[0, 2], rsem.at[0, flow], dp, my_relay)

    def from_relay(n, to_tile):
        return remote(
            relayed.at[n], vid_far.at[pl.ds(breadth + kept, RELAYED * breadth)], rsem.at[1, n], vsem.at[1, 2], dp, to_tile
        )

    def relay_pass(distance):
        n = jnp.where(t == 0, distance - 1, FLOWS - distance)

        @pl.when(is_relay)
        def _():
            remote(vid_hbm.at[passed], relayed.at[n], vsem.at[0, 2], rsem.at[0, n], dp, partner).wait_recv()
            from_relay(n, jnp.where(t == 0, 8 * n + 6, 8 * n + 9)).start()

    def prepare(src, dst, lines, above=1):
        lanes = lax.broadcasted_iota(jnp.int32, (breadth, BLOCK), 1)
        at = lax.broadcasted_iota(jnp.int32, (breadth, group), 0)

        @pl.loop(0, lines)
        def _(r):
            line = src[pl.ds(pl.multiple_of(r * breadth, breadth), breadth), :].astype(jnp.float32)
            rows = pl.ds(pl.multiple_of((r + above) * breadth, breadth), breadth)
            parts = [line[:, n * BLOCK : (n + 1) * BLOCK] for n in range(blocks)]
            turned = [pltpu.roll(part, shard, 1) for part in parts]
            low = lanes < shard
            for z_at in range(2):
                left_of, right_of = (parts, turned) if z_at == 0 else (turned, parts)
                mid = jnp.concatenate(
                    [jnp.where(low, left_of[n], right_of[n + 1]) for n in range(0, blocks, 2)], axis=1
                )
                left = jnp.where(at == 0, 0.0, pltpu.roll(mid, 1, 0))
                right = jnp.where(at == breadth - 1, 0.0, pltpu.roll(mid, breadth - 1, 0))
                for dx, value in enumerate((left, mid, right)):
                    start = (3 * z_at + dx) * group
                    dst[rows, start : start + group] = value.astype(jnp.bfloat16)

    def half_dot(xs, z_at, pair, i):
        total = None
        for dy in range(3):
            start = pl.multiple_of(i * ROWS + dy * breadth, breadth)
            lhs = xs[pl.ds(start, ROWS), pl.ds(pl.multiple_of(z_at * (3 * group), 3 * group), 3 * group)]
            rhs = jnp.concatenate(
                [wb[j, z_at, 3 * dy : 3 * dy + 3].reshape(3 * group, BLOCK) for j in pair], axis=1
            )
            part = jnp.dot(lhs, rhs, preferred_element_type=jnp.float32)
            total = part if total is None else total + part
        return total

    def activate(total, pair):
        total = total + jnp.concatenate([sb_ref[j] for j in pair], axis=1)
        return (total / (1.0 + jnp.exp(-total))).astype(jnp.bfloat16)

    pairs = (block_a, block_b), (block_c, block_d)

    def spatial_first(p, i):
        acc[rows_of(i), 2 * BLOCK * p : 2 * BLOCK * (p + 1)] = half_dot(xcat, zh, pairs[p], i)

    def spatial_rest(p, i):
        total = acc[rows_of(i), 2 * BLOCK * p : 2 * BLOCK * (p + 1)] + half_dot(xcat, 1 - zh, pairs[p], i)
        hidden = activate(total, pairs[p])
        for n, j in enumerate(pairs[p]):
            own[j % 2, j // 2, rows_of(i), :] = hidden[:, n * BLOCK : (n + 1) * BLOCK]

    @pl.when(jnp.logical_and(is_one, edge))
    def _():
        for g in (0, 1, 3, 2):
            start_z(g)

    @pl.when(is_zero)
    def _():
        start_y(0, source(0))
        start_y(1, source(1))
        pl.when(edge)(lambda: start_y(3, source(3)))

    @pl.when(far_any)
    def _():
        to_relay().start()
        far_upper().start()
        far_lower().start()


    zeros = jnp.zeros((breadth, 6 * group), jnp.bfloat16)
    xcat[0:breadth, :] = zeros
    xcat[breadth + pixels :, :] = zeros
    vid_copy.wait()
    prepare(outv, xcat, height)
    for load in loads:
        load.wait()

    @pl.when(is_zero)
    def _():
        stage_y(0)
        stage_y(1)
        relay_pass(1)
        stage_far(0)
        stage_far(1)

    @pl.when(is_one)
    def _():
        stage_z(0)
        stage_z(1)
        relay_pass(1)
        stage_y(0)
        stage_y(1)
        pl.when(edge)(lambda: stage_z(3))
        stage_done(0, (1, 2, 3))
        stage_done(1, (1, 2, 3))

    relay_pass(2)
    relay_pass(3)
    edge_zero, edge_one = jnp.logical_and(edge, is_zero), jnp.logical_and(edge, is_one)
    sharing = jnp.logical_and(is_one, inner_source_of_two)

    def on(flag, n, at, *stages):
        @pl.when(jnp.logical_and(flag, n == at))
        def _():
            for stage in stages:
                stage()

    @pl.loop(0, chunks)
    def _(n):
        spatial_first(0, chunks - 1 - n)
        on(is_zero, n, 1, lambda: stage_x(3))
        on(is_zero, n, 2, lambda: stage_x(1))
        on(is_zero, n, 3, lambda: stage_x(2))
        on(is_one, n, 0, lambda: stage_far(0))
        on(is_one, n, 1, lambda: stage_far(1))
        on(edge_zero, n, 0, lambda: stage_y(3))
        on(edge_one, n, 2, lambda: stage_y(3))
        on(is_zero, n, 2, lambda: start_y(2, source(2)))
        on(edge_zero, n, 3, lambda: stage_far(3))
        on(sharing, n, 3, stage_share)

    @pl.when(is_zero)
    def _():
        stage_done(0, range(4))
        stage_done(1, range(4))

    @pl.loop(0, chunks)
    def _(n):
        spatial_rest(0, chunks - 1 - n)

        @pl.when(n > 0)
        def _():
            send_hidden(0, chunks - n)

        on(is_one, n, 0, lambda: stage_x(0))
        on(is_one, n, 1, lambda: stage_x(3))
        on(edge_one, n, 0, lambda: stage_far(3))
        on(is_one, n, 2, lambda: stage_x(1))
        on(is_one, n, 3, lambda: stage_z(2))

    pl.when(is_one)(lambda: stage_x_done((1, 2, 3)))

    @pl.loop(0, chunks)
    def _(n):
        spatial_first(1, chunks - 1 - n)

        @pl.when(n == 0)
        def _():
            send_hidden(0, 0)

        on(is_one, n, 0, lambda: stage_x(2))
        on(is_zero, n, 2, lambda: stage_y(2))

    pl.when(is_zero)(lambda: stage_x_done(range(4)))

    @pl.loop(0, chunks)
    def _(n):
        spatial_rest(1, chunks - 1 - n)

        @pl.when(n > 0)
        def _():
            send_hidden(1, chunks - n)

        on(far_any, n, 1, lambda: far_upper().wait_recv(), lambda: hand_row().start())
        on(aid_any, n, 0, lambda: far_lower().wait_recv(), lambda: hand_row().start())
        on(is_one, n, 0, lambda: stage_y(2))

    stage_far(2)
    send_hidden(1, 0)

    def made_copy(q, i):
        rows = rows_of(i + FAR_CHUNKS)
        return remote(
            made.at[q, :, rows_of(i), :], near.at[far_side, q, :, rows, :], csend.at[0], crecv.at[i], dp, partner
        )

    def far_step(n):
        p, i = n // FAR_CHUNKS, n % FAR_CHUNKS
        return (x + p) % 2, i

    @pl.when(far_any)
    def _():
        far_upper().wait_send()
        far_lower().wait_send()
        to_relay().wait_send()

    @pl.when(aid_any)
    def _():
        from_relay(0, partner).wait_recv()

    @pl.when(team)
    def _():
        hand_row().wait()
        blank = jnp.where(far_any, 0, far_rows)
        xcat_far[pl.ds(pl.multiple_of(blank, breadth), breadth), :] = zeros
        prepare(vid_far, xcat_far, far_rows // breadth, one(far_any))

        @pl.loop(0, 2 * FAR_CHUNKS)
        def _(n):
            p, i = n // FAR_CHUNKS, n % FAR_CHUNKS
            pair = ((x + p) % 4, (x + p + 2) % 4)
            hidden = activate(half_dot(xcat_far, 0, pair, i) + half_dot(xcat_far, 1, pair, i), pair)

            @pl.when(far_any)
            def _():
                for m, j in enumerate(pair):
                    near[far_side, j % 2, j // 2, rows_of(i), :] = hidden[:, m * BLOCK : (m + 1) * BLOCK]

            @pl.when(aid_any)
            def _():
                for m, j in enumerate(pair):
                    made[j % 2, j // 2, rows_of(i), :] = hidden[:, m * BLOCK : (m + 1) * BLOCK]

            pl.when(jnp.logical_and(aid_any, n > 0))(lambda: made_copy(*far_step(n - 1)).start())

    pl.when(is_zero)(lambda: stage_done(2, range(4)))
    pl.when(is_one)(lambda: stage_done(2, (1, 2, 3)))

    def taps(lag, j):
        return wt[lag, columns(j), :]

    def temporal(lag, ref, q, i):
        lhs = jnp.concatenate([ref[q, m, rows_of(i), :] for m in range(2)], axis=1)
        rhs = jnp.concatenate([taps(lag, q), taps(lag, q + 2)], axis=0)
        return jnp.dot(lhs, rhs, preferred_element_type=jnp.float32)

    @pl.when(jnp.logical_not(team))
    def _():
        @pl.loop(0, chunks)
        def _(n):
            acc[rows_of(n), :] = temporal(1, own, 0, n) + temporal(1, own, 1, n) + tb_ref[...]

    pl.when(aid_any)(lambda: made_copy(*far_step(2 * FAR_CHUNKS - 1)).start())
    wait_sends()

    @pl.when(is_relay)
    def _():
        for n in range(FLOWS):
            from_relay(n, partner).wait_send()

    there, x_there = (has_before, has_after), ((t + tiles - 1) % tiles // 8, (t + 1) % tiles // 8)

    def exchange_rest(chip, z):
        for p in range(2):
            @pl.loop(0, chunks)
            def _(n, p=p):
                i = chunks - 1 - n
                rows = rows_of(i)
                q = (x_there[chip] + p) % 2
                hcopy(q, i, 1 - chip).wait_recv()
                acc[rows, :] += temporal(2 * chip, near.at[chip], q, i)

                @pl.when(there[z])
                def _():
                    q = (x_there[z] + p) % 2
                    hcopy(q, i, 1 - z).wait_recv()
                    total = acc[rows, :] + temporal(2 * z, near.at[z], q, i)
                    if p == 0:
                        acc[rows, :] = total
                    else:
                        outv[rows, :] = total.astype(jnp.bfloat16)

                if p == 1:
                    @pl.when(jnp.logical_not(there[z]))
                    def _():
                        outv[rows, :] = acc[rows, :].astype(jnp.bfloat16)

    pl.when(jnp.logical_and(jnp.logical_not(team), is_zero))(lambda: exchange_rest(1, 0))
    pl.when(jnp.logical_and(jnp.logical_not(team), is_one))(lambda: exchange_rest(0, 1))

    @pl.when(aid_any)
    def _():
        z_side = jnp.where(aid_before, 1, 0)
        q_first = jnp.where(aid_before, x_there[1], x_there[0]) % 2

        @pl.loop(0, chunks)
        def _(n):
            i = chunks - 1 - n

            @pl.when(aid_before)
            def _():
                hcopy(q_first, i, 0).wait_recv()
                for q in range(2):
                    hcopy(q, i, 1).wait_recv()

            @pl.when(aid_after)
            def _():
                hcopy(q_first, i, 1).wait_recv()
                for q in range(2):
                    hcopy(q, i, 0).wait_recv()

            total = tb_ref[...] + temporal(2 * z_side, near.at[z_side], q_first, i)
            for q in range(2):
                total = total + temporal(1, own, q, i) + temporal(2 - 2 * z_side, near.at[1 - z_side], q, i)
            acc[rows_of(i), :] = total

        @pl.loop(0, chunks)
        def _(n):
            i = chunks - 1 - n
            pl.when(aid_before)(lambda: hcopy(1 - q_first, i, 0).wait_recv())
            pl.when(aid_after)(lambda: hcopy(1 - q_first, i, 1).wait_recv())
            rest = temporal(2 * z_side, near.at[z_side], 1 - q_first, i)
            outv[rows_of(i), :] = (acc[rows_of(i), :] + rest).astype(jnp.bfloat16)

    @pl.when(far_any)
    def _():
        @pl.loop(0, chunks)
        def _(i):
            pl.when(far_before)(lambda: [hcopy(q, i, 0).wait_recv() for q in range(2)] and None)
            pl.when(far_after)(lambda: [hcopy(q, i, 1).wait_recv() for q in range(2)] and None)

            @pl.when(i >= FAR_CHUNKS)
            def _():
                both = made.at[:, :, rows_of(i - FAR_CHUNKS), :]
                remote(both, both, csend.at[0], crecv.at[i - FAR_CHUNKS], dp, partner).wait_recv()

            total = tb_ref[...]
            for q in range(2):
                total = total + temporal(1, own, q, i)
                for side in range(2):
                    total = total + temporal(2 * side, near.at[side], q, i)
            outv[rows_of(i), :] = total.astype(jnp.bfloat16)

    for side in range(2):
        @pl.when(exchanged(side))
        def _():
            remote(own, near.at[1 - side], hsend.at[side], hrecv.at[side, 0], dp, partner).wait_send()

    @pl.when(aid_any)
    def _():
        remote(made, made, csend.at[0], crecv.at[0], dp, partner).wait_send()


def per_device(videos, spatial_filter, temporal_filter, spatial_bias, temporal_bias):
    _, _, height, breadth, chans = videos.shape
    shard = spatial_filter.shape[1]
    pixels = height * breadth
    blocks = chans // BLOCK
    chunks = pixels // ROWS
    far_pixels = FAR_CHUNKS * ROWS + breadth
    bf = jnp.bfloat16
    anywhere = pl.BlockSpec(memory_space=pl.ANY)
    vmem = pl.BlockSpec(memory_space=pltpu.VMEM)
    dma = pltpu.SemaphoreType.DMA
    out = pl.pallas_call(
        functools.partial(kernel, (height, breadth, chans, shard)),
        out_shape=pltpu.VMEM((pixels, chans), bf),
        in_specs=[anywhere] * 5,
        out_specs=vmem,
        scratch_shapes=[
            pltpu.VMEM((pixels + 2 * breadth, 3 * chans), bf),
            pltpu.VMEM((far_pixels + breadth, 3 * chans), bf),
            pltpu.VMEM((far_pixels, chans), bf),
            pltpu.VMEM((FLOWS, RELAYED * breadth, chans), bf),
            pltpu.VMEM((2, blocks // 2, FAR_CHUNKS * ROWS, BLOCK), bf),
            pltpu.VMEM((blocks, 2, TAPS_S, chans // 2, BLOCK), bf),
            pltpu.VMEM((TAPS_T, chans, chans), bf),
            pltpu.VMEM((2, blocks // 2, pixels, BLOCK), bf),
            pltpu.VMEM((2, 2, blocks // 2, pixels, BLOCK), bf),
            pltpu.VMEM((pixels, chans), jnp.float32),
            pltpu.VMEM((blocks, 1, BLOCK), jnp.float32),
            pltpu.VMEM((1, chans), jnp.float32),
            dma((8,)),
            dma((4, 4)), dma((4, 5)),
            dma((2,)), dma((2, 4)),
            dma((2,)), dma((2,)),
            dma((2,)), dma((2, 2 * chunks)),
            dma((2, 4)),
            dma((2, FLOWS)),
            dma((1,)), dma((FAR_CHUNKS,)),
        ],
        compiler_params=pltpu.CompilerParams(
            collective_id=0, has_side_effects=True, vmem_limit_bytes=56 * 1024 * 1024
        ),
    )(
        videos.reshape(pixels, chans),
        spatial_filter,
        temporal_filter,
        spatial_bias.reshape(blocks, 1, BLOCK),
        temporal_bias.reshape(1, chans),
    )
    return out.reshape(videos.shape)


def solution(mesh):
    return jax.shard_map(
        per_device,
        mesh=mesh,
        in_specs=(
            P("dp", "tile", None, None, None),
            P(None, "dp", None),
            P(None, "dp", None),
            P(),
            P(),
        ),
        out_specs=P("dp", "tile", None, None, None),
        check_vma=False,
    )
```

```python
import functools

import jax
import jax.numpy as jnp
from jax import lax
from jax.experimental import pallas as pl
from jax.experimental.pallas import tpu as pltpu
from jax.sharding import PartitionSpec as P

BLOCK = 128
ROWS = 512
FAR_CHUNKS = 2
RELAYED = 4
FLOWS = 3
TAPS_S, TAPS_T = 9, 3
MESH = pl.DeviceIdType.MESH


def kernel(
    dims, vid_hbm, ws_hbm, wt_hbm, sb_hbm, tb_hbm, outv,
    xcat, xcat_far, vid_far, relayed, made, wb, wt, own, near, acc, sb_ref, tb_ref,
    local_sem, wsend, wrecv, xsend, xrecv, psend, precv, hsend, hrecv, vsem, rsem, csend, crecv,
):
    height, breadth, chans, shard = dims
    pixels = height * breadth
    chunks = pixels // ROWS
    blocks = chans // BLOCK
    group = chans // 2
    half = shard // 2

    dp, t = lax.axis_index("dp"), lax.axis_index("tile")
    tiles = lax.axis_size("tile")
    y, zh = dp // 2, dp % 2
    core, zl, x = t % 2, (t // 2) % 4, t // 8
    partner = t + 1 - 2 * core
    up, dn = ((y + 1) % 4) * 2 + zh, ((y + 3) % 4) * 2 + zh
    other = y * 2 + 1 - zh
    first, last = zl == 0, zl == 3
    edge = jnp.logical_or(first, last)
    base = t - zl * 2
    cross_edge = base + jnp.where(first, 6, 0)
    cross_inner = base + jnp.where(first, 4, 2)
    inner_source = base + jnp.where(zl == 1, 6, 0)
    x_next, x_prev = (t + 8) % tiles, (t + tiles - 8) % tiles
    has_before, has_after = t > 0, t < tiles - 1
    far_before = jnp.logical_and(t % 8 == 0, has_before)
    far_after = jnp.logical_and(t % 8 == 7, has_after)
    far_any = jnp.logical_or(far_before, far_after)
    aid_before = jnp.logical_and(t % 8 == 1, t > 1)
    aid_after = jnp.logical_and(t % 8 == 6, t < tiles - 2)
    aid_any = jnp.logical_or(aid_before, aid_after)
    team = jnp.logical_or(far_any, aid_any)
    far_side = jnp.where(jnp.logical_or(far_after, aid_after), 1, 0)
    two_off = jnp.where(far_side == 1, t + 2, t - 2)
    feeding_relay = jnp.where(aid_after, 0, tiles - 1)
    far_tile = jnp.where(far_after, t + 1, t - 1)
    is_relay = jnp.logical_or(t == 0, t == tiles - 1)
    my_relay = jnp.where(far_after, tiles - 1, 0)
    flow = jnp.where(far_after, x, x - 1)
    x_free = jnp.where(jnp.logical_or(first, zl == 2), FLOWS, 0)
    in_free = x == x_free
    x_across = (t + 16) % tiles
    is_one = core == 1
    is_zero = core == 0

    block_a, block_b, block_c, block_d = x, (x + 2) % 4, (x + 1) % 4, (x + 3) % 4
    block_e, cross_e = jnp.where(first, block_d, block_c), jnp.where(first, block_c, block_d)
    ring_blocks = {0: block_a, 1: block_b, 3: block_e}
    carried = jnp.where(is_zero, zh, 1 - zh)

    def remote(src, dst, ssem, rsem, to_dp, to_tile):
        return pltpu.make_async_remote_copy(
            src_ref=src, dst_ref=dst, send_sem=ssem, recv_sem=rsem,
            device_id={"dp": to_dp, "tile": to_tile}, device_id_type=MESH,
        )

    def columns(j):
        return pl.ds(pl.multiple_of(j * BLOCK, BLOCK), BLOCK)

    def block_piece(j, y_at, z_at, low=0, count=None):
        count = shard if count is None else count
        return wb.at[j, z_at, :, pl.ds(pl.multiple_of(y_at * shard + low, half), count), :]

    def piece(g, y_at, z_at, low=0, count=None):
        if g != 2:
            return block_piece(ring_blocks[g], y_at, z_at, low, count)
        count = shard if count is None else count
        return wt.at[:, pl.ds(pl.multiple_of((y_at * 2 + z_at) * shard + low, half), count), :]

    def source(g):
        return wt_hbm if g == 2 else ws_hbm.at[:, :, columns(ring_blocks[g])]

    vid_copy = pltpu.make_async_copy(vid_hbm, outv, local_sem.at[5])
    loads = [
        pltpu.make_async_copy(ws_hbm.at[:, :, columns(j)], block_piece(j, y, zh), local_sem.at[n])
        for n, j in enumerate((block_a, block_b, block_c, block_d))
    ]
    loads.append(pltpu.make_async_copy(wt_hbm, piece(2, y, zh), local_sem.at[4]))
    loads.append(pltpu.make_async_copy(sb_hbm, sb_ref, local_sem.at[6]))
    loads.append(pltpu.make_async_copy(tb_hbm, tb_ref, local_sem.at[7]))
    vid_copy.start()
    for load in loads:
        load.start()

    barrier = pltpu.get_barrier_semaphore()

    def greet(to_dp, to_tile):
        pl.semaphore_signal(barrier, inc=1, device_id={"dp": to_dp, "tile": to_tile}, device_id_type=MESH)

    greet(dp, partner)
    greet(up, t)
    greet(dn, t)
    greet(dp, x_next)
    greet(dp, x_prev)
    greet(dp, x_across)

    @pl.when(far_any)
    def _():
        greet(dp, my_relay)

    @pl.when(aid_any)
    def _():
        greet(dp, feeding_relay)

    @pl.when(team)
    def _():
        greet(dp, two_off)

    @pl.when(is_relay)
    def _():
        for n in range(FLOWS):
            greet(dp, jnp.where(t == 0, 8 * n + 8, 8 * n + 7))
            greet(dp, jnp.where(t == 0, 8 * n + 6, 8 * n + 9))

    @pl.when(edge)
    def _():
        greet(other, cross_edge)
        greet(other, cross_inner)

    @pl.when(jnp.logical_not(edge))
    def _():
        greet(other, inner_source)

    @pl.when(has_before)
    def _():
        greet(dp, t - 1)

    @pl.when(has_after)
    def _():
        greet(dp, t + 1)

    one = lambda flag: jnp.where(flag, 1, 0)
    pl.semaphore_wait(barrier, 7 + one(edge) + one(has_before) + one(has_after) + 2 * one(team) + 2 * FLOWS * one(is_relay))

    def ring(g, send, recv, y_at, z_at, to_dp, to_tile, low=0, count=None, src=None):
        ref = piece(g, y_at, z_at, low, count)
        return remote(ref if src is None else src, ref, wsend.at[g, send], wrecv.at[g, recv], to_dp, to_tile)

    def ring_many(g, send, recv, count):
        return ring(g, send, recv, 0, 0, dp, partner, 0, count * shard)

    def from_x(n, k, y_at, to_tile):
        ref = block_piece(block_a, y_at, carried)
        return remote(ref, ref, xsend.at[n], xrecv.at[n, k], dp, to_tile)

    by_x = jnp.logical_not(first), jnp.logical_not(last)

    def y_of(k):
        return (y + k) % 4

    def spread(g, k):
        ring(g, 3, 4, y_of(k), carried, dp, partner).start()
        if g == 0:
            pl.when(by_x[0])(lambda: from_x(0, k, y_of(k), x_next).start())
            pl.when(by_x[1])(lambda: from_x(1, k, y_of(k), x_prev).start())

    def cross_copy():
        return remote(
            ws_hbm.at[:, :, columns(cross_e)], block_piece(cross_e, y, zh), wsend.at[3, 0], wrecv.at[3, 0],
            other, cross_edge,
        )

    def start_z(g):
        if g == 3:
            cross_copy().start()
            return
        inner = lambda: ring(g, 1, 0, y, zh, other, cross_inner, src=source(g)).start()
        if g == 2:
            pl.when(in_free)(inner)
        else:
            inner()
        ring(g, 0, 0, y, zh, other, cross_edge, src=source(g)).start()

    def start_y(g, src=None):
        ring(g, 2, 1, y, carried, up, t, src=src).start()
        ring(g, 2, 2, y, carried, dn, t, src=src).start()

    inner_source_of_two = jnp.logical_and(jnp.logical_not(edge), in_free)

    def share(slot, to_tile):
        return ring(2, slot, 0, y, 1 - zh, dp, to_tile)

    def stage_share():
        ring(2, 0, 0, y, 1 - zh, dp, partner).wait_recv()
        for slot, to_tile in ((0, x_next), (0, x_prev), (0, x_across)):
            share(slot, to_tile).start()

    def stage_z(g):
        arrived = lambda: ring(g, 0, 0, y, 1 - zh, dp, partner).wait_recv()
        if g == 2:
            pl.when(jnp.logical_not(inner_source_of_two))(arrived)
        else:
            arrived()
        start_y(g)
        spread(g, 0)

    def stage_y(g):
        ring(g, 2, 1, y_of(3), carried, up, t).wait_recv()
        ring(g, 2, 3, y_of(3), carried, up, t, 0, half).start()
        ring(g, 2, 2, y_of(1), carried, dn, t).wait_recv()
        ring(g, 2, 3, y_of(1), carried, dn, t, half, half).start()
        spread(g, 3)
        spread(g, 1)

    def stage_far(g):
        ring(g, 2, 3, y_of(2), carried, up, t).wait_recv()
        spread(g, 2)

    def stage_done(g, ks):
        ring_many(g, 3, 4, len(ks)).wait_recv()

    def onward(n, k, z_at):
        ref = block_piece((block_d, block_c)[n], y_of(k), z_at)
        return remote(ref, ref, psend.at[n], precv.at[n], dp, partner)

    def many(n, count, send, recv):
        ref = block_piece(0, 0, 0, 0, count * shard)
        return remote(ref, ref, send.at[n], recv, dp, partner)

    def stage_x(k):
        for n in range(2):
            @pl.when(by_x[n])
            def _():
                ref = block_piece((block_d, block_c)[n], y_of(k), carried)
                remote(ref, ref, xsend.at[n], xrecv.at[n, k], dp, x_next).wait_recv()
                onward(n, k, carried).start()

    def stage_x_done(ks):
        for n in range(2):
            @pl.when(by_x[n])
            def _():
                many(n, len(ks), psend, precv.at[n]).wait_recv()

        pl.when(edge)(lambda: stage_done(3, ks))

    def by_core(wait):
        pl.when(is_zero)(lambda: wait(3))
        pl.when(is_one)(lambda: wait(4))

    def wait_ring(g):
        ring_many(g, 2, 0, 3).wait_send()
        by_core(lambda count: ring_many(g, 3, 0, count).wait_send())

    def wait_sends():
        for g in range(3):
            wait_ring(g)
        pl.when(edge)(lambda: wait_ring(3))

        @pl.when(jnp.logical_and(is_one, edge))
        def _():
            for g in range(3):
                ring(g, 0, 0, y, zh, other, cross_edge).wait_send()
            for g in range(2):
                ring(g, 1, 0, y, zh, other, cross_inner).wait_send()
            pl.when(in_free)(lambda: ring(2, 1, 0, y, zh, other, cross_inner).wait_send())
            cross_copy().wait_send()

        @pl.when(jnp.logical_and(is_one, inner_source_of_two))
        def _():
            ring_many(2, 0, 0, 3).wait_send()

        for n in range(2):
            @pl.when(by_x[n])
            def _():
                by_core(lambda count: many(n, count, xsend, xrecv.at[n, 0]).wait_send())
                by_core(lambda count: many(n, count, psend, precv.at[n]).wait_send())

    def rows_of(i):
        return pl.ds(pl.multiple_of(i * ROWS, ROWS), ROWS)

    def hcopy(q, i, side):
        slot = q * chunks + i
        return remote(
            own.at[q, :, rows_of(i), :], near.at[1 - side, q, :, rows_of(i), :],
            hsend.at[side], hrecv.at[side, slot], dp,
            jnp.maximum(t - 1, 0) if side == 0 else jnp.minimum(t + 1, tiles - 1),
        )

    def exchanged(side):
        there, far = ((has_before, far_before), (has_after, far_after))[side]
        return jnp.logical_and(there, jnp.logical_not(far))

    def send_hidden(p, i):
        for side in range(2):
            pl.when(exchanged(side))(lambda: hcopy((x + p) % 2, i, side).start())

    far_rows = (FAR_CHUNKS * ROWS // breadth + 1) * breadth
    half_rows = far_rows - breadth
    kept = half_rows - RELAYED * breadth
    passed = pl.ds(half_rows + kept, RELAYED * breadth)

    def far_upper():
        rows = pl.ds(0, half_rows)
        return remote(vid_hbm.at[rows], vid_far.at[rows], vsem.at[0, 0], vsem.at[1, 0], dp, far_tile)

    def far_lower():
        return remote(
            vid_hbm.at[pl.ds(half_rows, kept)], vid_far.at[pl.ds(breadth, kept)],
            vsem.at[0, 1], vsem.at[1, 1], dp, two_off,
        )

    def hand_row():
        src = pl.multiple_of(jnp.where(far_any, half_rows - breadth, breadth), breadth)
        dst = pl.multiple_of(jnp.where(far_any, 0, half_rows), breadth)
        return remote(
            vid_far.at[pl.ds(src, breadth)], vid_far.at[pl.ds(dst, breadth)], vsem.at[0, 3], vsem.at[1, 3], dp, partner
        )

    def to_relay():
        return remote(vid_hbm.at[passed], relayed.at[flow], vsem.at[0, 2], rsem.at[0, flow], dp, my_relay)

    def from_relay(n, to_tile):
        return remote(
            relayed.at[n], vid_far.at[pl.ds(breadth + kept, RELAYED * breadth)], rsem.at[1, n], vsem.at[1, 2], dp, to_tile
        )

    def relay_pass(distance):
        n = jnp.where(t == 0, distance - 1, FLOWS - distance)

        @pl.when(is_relay)
        def _():
            remote(vid_hbm.at[passed], relayed.at[n], vsem.at[0, 2], rsem.at[0, n], dp, partner).wait_recv()
            from_relay(n, jnp.where(t == 0, 8 * n + 6, 8 * n + 9)).start()

    def prepare(src, dst, lines, above=1):
        lanes = lax.broadcasted_iota(jnp.int32, (breadth, BLOCK), 1)
        at = lax.broadcasted_iota(jnp.int32, (breadth, group), 0)

        @pl.loop(0, lines)
        def _(r):
            line = src[pl.ds(pl.multiple_of(r * breadth, breadth), breadth), :].astype(jnp.float32)
            rows = pl.ds(pl.multiple_of((r + above) * breadth, breadth), breadth)
            parts = [line[:, n * BLOCK : (n + 1) * BLOCK] for n in range(blocks)]
            turned = [pltpu.roll(part, shard, 1) for part in parts]
            low = lanes < shard
            for z_at in range(2):
                left_of, right_of = (parts, turned) if z_at == 0 else (turned, parts)
                mid = jnp.concatenate(
                    [jnp.where(low, left_of[n], right_of[n + 1]) for n in range(0, blocks, 2)], axis=1
                )
                left = jnp.where(at == 0, 0.0, pltpu.roll(mid, 1, 0))
                right = jnp.where(at == breadth - 1, 0.0, pltpu.roll(mid, breadth - 1, 0))
                for dx, value in enumerate((left, mid, right)):
                    start = (3 * z_at + dx) * group
                    dst[rows, start : start + group] = value.astype(jnp.bfloat16)

    def half_dot(xs, z_at, pair, i):
        total = None
        for dy in range(3):
            start = pl.multiple_of(i * ROWS + dy * breadth, breadth)
            lhs = xs[pl.ds(start, ROWS), pl.ds(pl.multiple_of(z_at * (3 * group), 3 * group), 3 * group)]
            rhs = jnp.concatenate(
                [wb[j, z_at, 3 * dy : 3 * dy + 3].reshape(3 * group, BLOCK) for j in pair], axis=1
            )
            part = jnp.dot(lhs, rhs, preferred_element_type=jnp.float32)
            total = part if total is None else total + part
        return total

    def activate(total, pair):
        total = total + jnp.concatenate([sb_ref[j] for j in pair], axis=1)
        return (total / (1.0 + jnp.exp(-total))).astype(jnp.bfloat16)

    pairs = (block_a, block_b), (block_c, block_d)

    def spatial_first(p, i):
        acc[rows_of(i), 2 * BLOCK * p : 2 * BLOCK * (p + 1)] = half_dot(xcat, zh, pairs[p], i)

    def spatial_rest(p, i):
        total = acc[rows_of(i), 2 * BLOCK * p : 2 * BLOCK * (p + 1)] + half_dot(xcat, 1 - zh, pairs[p], i)
        hidden = activate(total, pairs[p])
        for n, j in enumerate(pairs[p]):
            own[j % 2, j // 2, rows_of(i), :] = hidden[:, n * BLOCK : (n + 1) * BLOCK]

    @pl.when(jnp.logical_and(is_one, edge))
    def _():
        for g in (0, 1, 3, 2):
            start_z(g)

    @pl.when(is_zero)
    def _():
        start_y(0, source(0))
        start_y(1, source(1))
        pl.when(edge)(lambda: start_y(3, source(3)))

    @pl.when(far_any)
    def _():
        to_relay().start()
        far_upper().start()
        far_lower().start()


    zeros = jnp.zeros((breadth, 6 * group), jnp.bfloat16)
    xcat[0:breadth, :] = zeros
    xcat[breadth + pixels :, :] = zeros
    vid_copy.wait()
    prepare(outv, xcat, height)
    for load in loads:
        load.wait()

    @pl.when(is_zero)
    def _():
        stage_y(0)
        stage_y(1)
        relay_pass(1)
        stage_far(0)
        stage_far(1)

    @pl.when(is_one)
    def _():
        stage_z(0)
        stage_z(1)
        relay_pass(1)
        stage_y(0)
        stage_y(1)
        pl.when(edge)(lambda: stage_z(3))
        stage_done(0, (1, 2, 3))
        stage_done(1, (1, 2, 3))

    relay_pass(2)
    relay_pass(3)
    edge_zero, edge_one = jnp.logical_and(edge, is_zero), jnp.logical_and(edge, is_one)
    sharing = jnp.logical_and(is_one, inner_source_of_two)

    def on(flag, n, at, *stages):
        @pl.when(jnp.logical_and(flag, n == at))
        def _():
            for stage in stages:
                stage()

    @pl.loop(0, chunks)
    def _(n):
        spatial_first(0, chunks - 1 - n)
        on(is_zero, n, 1, lambda: stage_x(3))
        on(is_zero, n, 2, lambda: stage_x(1))
        on(is_zero, n, 3, lambda: stage_x(2))
        on(is_one, n, 0, lambda: stage_far(0))
        on(is_one, n, 1, lambda: stage_far(1))
        on(edge_zero, n, 0, lambda: stage_y(3))
        on(edge_one, n, 2, lambda: stage_y(3))
        on(is_zero, n, 2, lambda: start_y(2, source(2)))
        on(edge_zero, n, 3, lambda: stage_far(3))
        on(sharing, n, 3, stage_share)

    @pl.when(is_zero)
    def _():
        stage_done(0, range(4))
        stage_done(1, range(4))

    @pl.loop(0, chunks)
    def _(n):
        spatial_rest(0, chunks - 1 - n)

        @pl.when(n > 0)
        def _():
            send_hidden(0, chunks - n)

        on(is_one, n, 0, lambda: stage_x(0))
        on(is_one, n, 1, lambda: stage_x(3))
        on(edge_one, n, 0, lambda: stage_far(3))
        on(is_one, n, 2, lambda: stage_x(1))
        on(is_one, n, 3, lambda: stage_z(2))

    pl.when(is_one)(lambda: stage_x_done((1, 2, 3)))

    @pl.loop(0, chunks)
    def _(n):
        spatial_first(1, chunks - 1 - n)

        @pl.when(n == 0)
        def _():
            send_hidden(0, 0)

        on(is_one, n, 0, lambda: stage_x(2))
        on(is_zero, n, 2, lambda: stage_y(2))

    pl.when(is_zero)(lambda: stage_x_done(range(4)))

    @pl.loop(0, chunks)
    def _(n):
        spatial_rest(1, chunks - 1 - n)

        @pl.when(n > 0)
        def _():
            send_hidden(1, chunks - n)

        on(far_any, n, 1, lambda: far_upper().wait_recv(), lambda: hand_row().start())
        on(aid_any, n, 0, lambda: far_lower().wait_recv(), lambda: hand_row().start())
        on(is_one, n, 0, lambda: stage_y(2))

    stage_far(2)
    send_hidden(1, 0)

    def made_copy(q, i):
        rows = rows_of(i + FAR_CHUNKS)
        return remote(
            made.at[q, :, rows_of(i), :], near.at[far_side, q, :, rows, :], csend.at[0], crecv.at[i], dp, partner
        )

    def far_step(n):
        p, i = n // FAR_CHUNKS, n % FAR_CHUNKS
        return (x + p) % 2, i

    @pl.when(far_any)
    def _():
        far_upper().wait_send()
        far_lower().wait_send()
        to_relay().wait_send()

    @pl.when(aid_any)
    def _():
        from_relay(0, partner).wait_recv()

    @pl.when(team)
    def _():
        hand_row().wait()
        blank = jnp.where(far_any, 0, far_rows)
        xcat_far[pl.ds(pl.multiple_of(blank, breadth), breadth), :] = zeros
        prepare(vid_far, xcat_far, far_rows // breadth, one(far_any))

        @pl.loop(0, 2 * FAR_CHUNKS)
        def _(n):
            p, i = n // FAR_CHUNKS, n % FAR_CHUNKS
            pair = ((x + p) % 4, (x + p + 2) % 4)
            hidden = activate(half_dot(xcat_far, 0, pair, i) + half_dot(xcat_far, 1, pair, i), pair)

            @pl.when(far_any)
            def _():
                for m, j in enumerate(pair):
                    near[far_side, j % 2, j // 2, rows_of(i), :] = hidden[:, m * BLOCK : (m + 1) * BLOCK]

            @pl.when(aid_any)
            def _():
                for m, j in enumerate(pair):
                    made[j % 2, j // 2, rows_of(i), :] = hidden[:, m * BLOCK : (m + 1) * BLOCK]

            pl.when(jnp.logical_and(aid_any, n > 0))(lambda: made_copy(*far_step(n - 1)).start())

    pl.when(is_zero)(lambda: stage_done(2, range(4)))
    pl.when(is_one)(lambda: stage_done(2, (1, 2, 3)))

    def taps(lag, j):
        return wt[lag, columns(j), :]

    def temporal(lag, ref, q, i):
        lhs = jnp.concatenate([ref[q, m, rows_of(i), :] for m in range(2)], axis=1)
        rhs = jnp.concatenate([taps(lag, q), taps(lag, q + 2)], axis=0)
        return jnp.dot(lhs, rhs, preferred_element_type=jnp.float32)

    @pl.when(jnp.logical_not(team))
    def _():
        @pl.loop(0, chunks)
        def _(n):
            acc[rows_of(n), :] = temporal(1, own, 0, n) + temporal(1, own, 1, n) + tb_ref[...]

    pl.when(aid_any)(lambda: made_copy(*far_step(2 * FAR_CHUNKS - 1)).start())
    wait_sends()

    @pl.when(is_relay)
    def _():
        for n in range(FLOWS):
            from_relay(n, partner).wait_send()

    there, x_there = (has_before, has_after), ((t + tiles - 1) % tiles // 8, (t + 1) % tiles // 8)

    def exchange_rest(chip, z):
        for p in range(2):
            @pl.loop(0, chunks)
            def _(n, p=p):
                i = chunks - 1 - n
                rows = rows_of(i)
                q = (x_there[chip] + p) % 2
                hcopy(q, i, 1 - chip).wait_recv()
                acc[rows, :] += temporal(2 * chip, near.at[chip], q, i)

                @pl.when(there[z])
                def _():
                    q = (x_there[z] + p) % 2
                    hcopy(q, i, 1 - z).wait_recv()
                    total = acc[rows, :] + temporal(2 * z, near.at[z], q, i)
                    if p == 0:
                        acc[rows, :] = total
                    else:
                        outv[rows, :] = total.astype(jnp.bfloat16)

                if p == 1:
                    @pl.when(jnp.logical_not(there[z]))
                    def _():
                        outv[rows, :] = acc[rows, :].astype(jnp.bfloat16)

    pl.when(jnp.logical_and(jnp.logical_not(team), is_zero))(lambda: exchange_rest(1, 0))
    pl.when(jnp.logical_and(jnp.logical_not(team), is_one))(lambda: exchange_rest(0, 1))

    @pl.when(aid_any)
    def _():
        z_side = jnp.where(aid_before, 1, 0)
        q_first = jnp.where(aid_before, x_there[1], x_there[0]) % 2

        @pl.loop(0, chunks)
        def _(n):
            i = chunks - 1 - n

            @pl.when(aid_before)
            def _():
                hcopy(q_first, i, 0).wait_recv()
                for q in range(2):
                    hcopy(q, i, 1).wait_recv()

            @pl.when(aid_after)
            def _():
                hcopy(q_first, i, 1).wait_recv()
                for q in range(2):
                    hcopy(q, i, 0).wait_recv()

            total = tb_ref[...] + temporal(2 * z_side, near.at[z_side], q_first, i)
            for q in range(2):
                total = total + temporal(1, own, q, i) + temporal(2 - 2 * z_side, near.at[1 - z_side], q, i)
            acc[rows_of(i), :] = total

        @pl.loop(0, chunks)
        def _(n):
            i = chunks - 1 - n
            pl.when(aid_before)(lambda: hcopy(1 - q_first, i, 0).wait_recv())
            pl.when(aid_after)(lambda: hcopy(1 - q_first, i, 1).wait_recv())
            rest = temporal(2 * z_side, near.at[z_side], 1 - q_first, i)
            outv[rows_of(i), :] = (acc[rows_of(i), :] + rest).astype(jnp.bfloat16)

    @pl.when(far_any)
    def _():
        @pl.loop(0, chunks)
        def _(i):
            pl.when(far_before)(lambda: [hcopy(q, i, 0).wait_recv() for q in range(2)] and None)
            pl.when(far_after)(lambda: [hcopy(q, i, 1).wait_recv() for q in range(2)] and None)

            @pl.when(i >= FAR_CHUNKS)
            def _():
                both = made.at[:, :, rows_of(i - FAR_CHUNKS), :]
                remote(both, both, csend.at[0], crecv.at[i - FAR_CHUNKS], dp, partner).wait_recv()

            total = tb_ref[...]
            for q in range(2):
                total = total + temporal(1, own, q, i)
                for side in range(2):
                    total = total + temporal(2 * side, near.at[side], q, i)
            outv[rows_of(i), :] = total.astype(jnp.bfloat16)

    for side in range(2):
        @pl.when(exchanged(side))
        def _():
            remote(own, near.at[1 - side], hsend.at[side], hrecv.at[side, 0], dp, partner).wait_send()

    @pl.when(aid_any)
    def _():
        remote(made, made, csend.at[0], crecv.at[0], dp, partner).wait_send()


def per_device(videos, spatial_filter, temporal_filter, spatial_bias, temporal_bias):
    _, _, height, breadth, chans = videos.shape
    shard = spatial_filter.shape[1]
    pixels = height * breadth
    blocks = chans // BLOCK
    chunks = pixels // ROWS
    far_pixels = FAR_CHUNKS * ROWS + breadth
    bf = jnp.bfloat16
    anywhere = pl.BlockSpec(memory_space=pl.ANY)
    vmem = pl.BlockSpec(memory_space=pltpu.VMEM)
    dma = pltpu.SemaphoreType.DMA
    out = pl.pallas_call(
        functools.partial(kernel, (height, breadth, chans, shard)),
        out_shape=pltpu.VMEM((pixels, chans), bf),
        in_specs=[anywhere] * 5,
        out_specs=vmem,
        scratch_shapes=[
            pltpu.VMEM((pixels + 2 * breadth, 3 * chans), bf),
            pltpu.VMEM((far_pixels + breadth, 3 * chans), bf),
            pltpu.VMEM((far_pixels, chans), bf),
            pltpu.VMEM((FLOWS, RELAYED * breadth, chans), bf),
            pltpu.VMEM((2, blocks // 2, FAR_CHUNKS * ROWS, BLOCK), bf),
            pltpu.VMEM((blocks, 2, TAPS_S, chans // 2, BLOCK), bf),
            pltpu.VMEM((TAPS_T, chans, chans), bf),
            pltpu.VMEM((2, blocks // 2, pixels, BLOCK), bf),
            pltpu.VMEM((2, 2, blocks // 2, pixels, BLOCK), bf),
            pltpu.VMEM((pixels, chans), jnp.float32),
            pltpu.VMEM((blocks, 1, BLOCK), jnp.float32),
            pltpu.VMEM((1, chans), jnp.float32),
            dma((8,)),
            dma((4, 4)), dma((4, 5)),
            dma((2,)), dma((2, 4)),
            dma((2,)), dma((2,)),
            dma((2,)), dma((2, 2 * chunks)),
            dma((2, 4)),
            dma((2, FLOWS)),
            dma((1,)), dma((FAR_CHUNKS,)),
        ],
        compiler_params=pltpu.CompilerParams(
            collective_id=0, has_side_effects=True, vmem_limit_bytes=56 * 1024 * 1024
        ),
    )(
        videos.reshape(pixels, chans),
        spatial_filter,
        temporal_filter,
        spatial_bias.reshape(blocks, 1, BLOCK),
        temporal_bias.reshape(1, chans),
    )
    return out.reshape(videos.shape)


def solution(mesh):
    return jax.shard_map(
        per_device,
        mesh=mesh,
        in_specs=(
            P("dp", "tile", None, None, None),
            P(None, "dp", None),
            P(None, "dp", None),
            P(),
            P(),
        ),
        out_specs=P("dp", "tile", None, None, None),
        check_vma=False,
    )
```

```python
import functools

import jax
import jax.numpy as jnp
from jax import lax
from jax.experimental import pallas as pl
from jax.experimental.pallas import tpu as pltpu
from jax.sharding import PartitionSpec as P

BLOCK = 128
ROWS = 512
FAR_CHUNKS = 2
RELAYED = 4
FLOWS = 3
TAPS_S, TAPS_T = 9, 3
MESH = pl.DeviceIdType.MESH


def kernel(
    dims, vid_hbm, ws_hbm, wt_hbm, sb_hbm, tb_hbm, outv,
    xcat, xcat_far, vid_far, relayed, made, wb, wt, own, near, acc, sb_ref, tb_ref,
    local_sem, wsend, wrecv, xsend, xrecv, psend, precv, hsend, hrecv, vsem, rsem, csend, crecv,
):
    height, breadth, chans, shard = dims
    pixels = height * breadth
    chunks = pixels // ROWS
    blocks = chans // BLOCK
    group = chans // 2
    half = shard // 2

    dp, t = lax.axis_index("dp"), lax.axis_index("tile")
    tiles = lax.axis_size("tile")
    y, zh = dp // 2, dp % 2
    core, zl, x = t % 2, (t // 2) % 4, t // 8
    partner = t + 1 - 2 * core
    up, dn = ((y + 1) % 4) * 2 + zh, ((y + 3) % 4) * 2 + zh
    other = y * 2 + 1 - zh
    first, last = zl == 0, zl == 3
    edge = jnp.logical_or(first, last)
    base = t - zl * 2
    cross_edge = base + jnp.where(first, 6, 0)
    cross_inner = base + jnp.where(first, 4, 2)
    inner_source = base + jnp.where(zl == 1, 6, 0)
    x_next, x_prev = (t + 8) % tiles, (t + tiles - 8) % tiles
    has_before, has_after = t > 0, t < tiles - 1
    far_before = jnp.logical_and(t % 8 == 0, has_before)
    far_after = jnp.logical_and(t % 8 == 7, has_after)
    far_any = jnp.logical_or(far_before, far_after)
    aid_before = jnp.logical_and(t % 8 == 1, t > 1)
    aid_after = jnp.logical_and(t % 8 == 6, t < tiles - 2)
    aid_any = jnp.logical_or(aid_before, aid_after)
    team = jnp.logical_or(far_any, aid_any)
    far_side = jnp.where(jnp.logical_or(far_after, aid_after), 1, 0)
    two_off = jnp.where(far_side == 1, t + 2, t - 2)
    feeding_relay = jnp.where(aid_after, 0, tiles - 1)
    far_tile = jnp.where(far_after, t + 1, t - 1)
    is_relay = jnp.logical_or(t == 0, t == tiles - 1)
    my_relay = jnp.where(far_after, tiles - 1, 0)
    flow = jnp.where(far_after, x, x - 1)
    x_free = jnp.where(jnp.logical_or(first, zl == 2), FLOWS, 0)
    in_free = x == x_free
    x_across = (t + 16) % tiles
    is_one = core == 1
    is_zero = core == 0

    block_a, block_b, block_c, block_d = x, (x + 2) % 4, (x + 1) % 4, (x + 3) % 4
    block_e, cross_e = jnp.where(first, block_d, block_c), jnp.where(first, block_c, block_d)
    ring_blocks = {0: block_a, 1: block_b, 3: block_e}
    carried = jnp.where(is_zero, zh, 1 - zh)

    def remote(src, dst, ssem, rsem, to_dp, to_tile):
        return pltpu.make_async_remote_copy(
            src_ref=src, dst_ref=dst, send_sem=ssem, recv_sem=rsem,
            device_id={"dp": to_dp, "tile": to_tile}, device_id_type=MESH,
        )

    def columns(j):
        return pl.ds(pl.multiple_of(j * BLOCK, BLOCK), BLOCK)

    def block_piece(j, y_at, z_at, low=0, count=None):
        count = shard if count is None else count
        return wb.at[j, z_at, :, pl.ds(pl.multiple_of(y_at * shard + low, half), count), :]

    def piece(g, y_at, z_at, low=0, count=None):
        if g != 2:
            return block_piece(ring_blocks[g], y_at, z_at, low, count)
        count = shard if count is None else count
        return wt.at[:, pl.ds(pl.multiple_of((y_at * 2 + z_at) * shard + low, half), count), :]

    def source(g):
        return wt_hbm if g == 2 else ws_hbm.at[:, :, columns(ring_blocks[g])]

    vid_copy = pltpu.make_async_copy(vid_hbm, outv, local_sem.at[5])
    loads = [
        pltpu.make_async_copy(ws_hbm.at[:, :, columns(j)], block_piece(j, y, zh), local_sem.at[n])
        for n, j in enumerate((block_a, block_b, block_c, block_d))
    ]
    loads.append(pltpu.make_async_copy(wt_hbm, piece(2, y, zh), local_sem.at[4]))
    loads.append(pltpu.make_async_copy(sb_hbm, sb_ref, local_sem.at[6]))
    loads.append(pltpu.make_async_copy(tb_hbm, tb_ref, local_sem.at[7]))

    barrier = pltpu.get_barrier_semaphore()

    def greet(to_dp, to_tile):
        pl.semaphore_signal(barrier, inc=1, device_id={"dp": to_dp, "tile": to_tile}, device_id_type=MESH)

    greet(dp, partner)
    greet(up, t)
    greet(dn, t)
    greet(dp, x_next)
    greet(dp, x_prev)
    greet(dp, x_across)

    @pl.when(far_any)
    def _():
        greet(dp, my_relay)

    @pl.when(aid_any)
    def _():
        greet(dp, feeding_relay)

    @pl.when(team)
    def _():
        greet(dp, two_off)

    @pl.when(is_relay)
    def _():
        for n in range(FLOWS):
            greet(dp, jnp.where(t == 0, 8 * n + 8, 8 * n + 7))
            greet(dp, jnp.where(t == 0, 8 * n + 6, 8 * n + 9))

    @pl.when(edge)
    def _():
        greet(other, cross_edge)
        greet(other, cross_inner)

    @pl.when(jnp.logical_not(edge))
    def _():
        greet(other, inner_source)

    @pl.when(has_before)
    def _():
        greet(dp, t - 1)

    @pl.when(has_after)
    def _():
        greet(dp, t + 1)

    vid_copy.start()
    for load in loads:
        load.start()

    one = lambda flag: jnp.where(flag, 1, 0)
    pl.semaphore_wait(barrier, 7 + one(edge) + one(has_before) + one(has_after) + 2 * one(team) + 2 * FLOWS * one(is_relay))

    def ring(g, send, recv, y_at, z_at, to_dp, to_tile, low=0, count=None, src=None):
        ref = piece(g, y_at, z_at, low, count)
        return remote(ref if src is None else src, ref, wsend.at[g, send], wrecv.at[g, recv], to_dp, to_tile)

    def ring_many(g, send, recv, count):
        return ring(g, send, recv, 0, 0, dp, partner, 0, count * shard)

    def from_x(n, k, y_at, to_tile):
        ref = block_piece(block_a, y_at, carried)
        return remote(ref, ref, xsend.at[n], xrecv.at[n, k], dp, to_tile)

    by_x = jnp.logical_not(first), jnp.logical_not(last)

    def y_of(k):
        return (y + k) % 4

    def spread(g, k):
        ring(g, 3, 4, y_of(k), carried, dp, partner).start()
        if g == 0:
            pl.when(by_x[0])(lambda: from_x(0, k, y_of(k), x_next).start())
            pl.when(by_x[1])(lambda: from_x(1, k, y_of(k), x_prev).start())

    def cross_copy():
        return remote(
            ws_hbm.at[:, :, columns(cross_e)], block_piece(cross_e, y, zh), wsend.at[3, 0], wrecv.at[3, 0],
            other, cross_edge,
        )

    def start_z(g):
        if g == 3:
            cross_copy().start()
            return
        inner = lambda: ring(g, 1, 0, y, zh, other, cross_inner, src=source(g)).start()
        if g == 2:
            pl.when(in_free)(inner)
        else:
            inner()
        ring(g, 0, 0, y, zh, other, cross_edge, src=source(g)).start()

    def start_y(g, src=None):
        ring(g, 2, 1, y, carried, up, t, src=src).start()
        ring(g, 2, 2, y, carried, dn, t, src=src).start()

    inner_source_of_two = jnp.logical_and(jnp.logical_not(edge), in_free)

    def share(slot, to_tile):
        return ring(2, slot, 0, y, 1 - zh, dp, to_tile)

    def stage_share():
        ring(2, 0, 0, y, 1 - zh, dp, partner).wait_recv()
        for slot, to_tile in ((0, x_next), (0, x_prev), (0, x_across)):
            share(slot, to_tile).start()

    def stage_z(g):
        arrived = lambda: ring(g, 0, 0, y, 1 - zh, dp, partner).wait_recv()
        if g == 2:
            pl.when(jnp.logical_not(inner_source_of_two))(arrived)
        else:
            arrived()
        start_y(g)
        spread(g, 0)

    def stage_y(g):
        ring(g, 2, 1, y_of(3), carried, up, t).wait_recv()
        ring(g, 2, 3, y_of(3), carried, up, t, 0, half).start()
        ring(g, 2, 2, y_of(1), carried, dn, t).wait_recv()
        ring(g, 2, 3, y_of(1), carried, dn, t, half, half).start()
        spread(g, 3)
        spread(g, 1)

    def stage_far(g):
        ring(g, 2, 3, y_of(2), carried, up, t).wait_recv()
        spread(g, 2)

    def stage_done(g, ks):
        ring_many(g, 3, 4, len(ks)).wait_recv()

    def onward(n, k, z_at):
        ref = block_piece((block_d, block_c)[n], y_of(k), z_at)
        return remote(ref, ref, psend.at[n], precv.at[n], dp, partner)

    def many(n, count, send, recv):
        ref = block_piece(0, 0, 0, 0, count * shard)
        return remote(ref, ref, send.at[n], recv, dp, partner)

    def stage_x(k):
        for n in range(2):
            @pl.when(by_x[n])
            def _():
                ref = block_piece((block_d, block_c)[n], y_of(k), carried)
                remote(ref, ref, xsend.at[n], xrecv.at[n, k], dp, x_next).wait_recv()
                onward(n, k, carried).start()

    def stage_x_done(ks):
        for n in range(2):
            @pl.when(by_x[n])
            def _():
                many(n, len(ks), psend, precv.at[n]).wait_recv()

        pl.when(edge)(lambda: stage_done(3, ks))

    def by_core(wait):
        pl.when(is_zero)(lambda: wait(3))
        pl.when(is_one)(lambda: wait(4))

    def wait_ring(g):
        ring_many(g, 2, 0, 3).wait_send()
        by_core(lambda count: ring_many(g, 3, 0, count).wait_send())

    def wait_sends():
        for g in range(3):
            wait_ring(g)
        pl.when(edge)(lambda: wait_ring(3))

        @pl.when(jnp.logical_and(is_one, edge))
        def _():
            for g in range(3):
                ring(g, 0, 0, y, zh, other, cross_edge).wait_send()
            for g in range(2):
                ring(g, 1, 0, y, zh, other, cross_inner).wait_send()
            pl.when(in_free)(lambda: ring(2, 1, 0, y, zh, other, cross_inner).wait_send())
            cross_copy().wait_send()

        @pl.when(jnp.logical_and(is_one, inner_source_of_two))
        def _():
            ring_many(2, 0, 0, 3).wait_send()

        for n in range(2):
            @pl.when(by_x[n])
            def _():
                by_core(lambda count: many(n, count, xsend, xrecv.at[n, 0]).wait_send())
                by_core(lambda count: many(n, count, psend, precv.at[n]).wait_send())

    def rows_of(i):
        return pl.ds(pl.multiple_of(i * ROWS, ROWS), ROWS)

    def hcopy(q, i, side):
        slot = q * chunks + i
        return remote(
            own.at[q, :, rows_of(i), :], near.at[1 - side, q, :, rows_of(i), :],
            hsend.at[side], hrecv.at[side, slot], dp,
            jnp.maximum(t - 1, 0) if side == 0 else jnp.minimum(t + 1, tiles - 1),
        )

    def exchanged(side):
        there, far = ((has_before, far_before), (has_after, far_after))[side]
        return jnp.logical_and(there, jnp.logical_not(far))

    def send_hidden(p, i):
        for side in range(2):
            pl.when(exchanged(side))(lambda: hcopy((x + p) % 2, i, side).start())

    far_rows = (FAR_CHUNKS * ROWS // breadth + 1) * breadth
    half_rows = far_rows - breadth
    kept = half_rows - RELAYED * breadth
    passed = pl.ds(half_rows + kept, RELAYED * breadth)

    def far_upper():
        rows = pl.ds(0, half_rows)
        return remote(vid_hbm.at[rows], vid_far.at[rows], vsem.at[0, 0], vsem.at[1, 0], dp, far_tile)

    def far_lower():
        return remote(
            vid_hbm.at[pl.ds(half_rows, kept)], vid_far.at[pl.ds(breadth, kept)],
            vsem.at[0, 1], vsem.at[1, 1], dp, two_off,
        )

    def hand_row():
        src = pl.multiple_of(jnp.where(far_any, half_rows - breadth, breadth), breadth)
        dst = pl.multiple_of(jnp.where(far_any, 0, half_rows), breadth)
        return remote(
            vid_far.at[pl.ds(src, breadth)], vid_far.at[pl.ds(dst, breadth)], vsem.at[0, 3], vsem.at[1, 3], dp, partner
        )

    def to_relay():
        return remote(vid_hbm.at[passed], relayed.at[flow], vsem.at[0, 2], rsem.at[0, flow], dp, my_relay)

    def from_relay(n, to_tile):
        return remote(
            relayed.at[n], vid_far.at[pl.ds(breadth + kept, RELAYED * breadth)], rsem.at[1, n], vsem.at[1, 2], dp, to_tile
        )

    def relay_pass(distance):
        n = jnp.where(t == 0, distance - 1, FLOWS - distance)

        @pl.when(is_relay)
        def _():
            remote(vid_hbm.at[passed], relayed.at[n], vsem.at[0, 2], rsem.at[0, n], dp, partner).wait_recv()
            from_relay(n, jnp.where(t == 0, 8 * n + 6, 8 * n + 9)).start()

    def prepare(src, dst, lines, above=1):
        lanes = lax.broadcasted_iota(jnp.int32, (breadth, BLOCK), 1)
        at = lax.broadcasted_iota(jnp.int32, (breadth, group), 0)

        @pl.loop(0, lines)
        def _(r):
            line = src[pl.ds(pl.multiple_of(r * breadth, breadth), breadth), :].astype(jnp.float32)
            rows = pl.ds(pl.multiple_of((r + above) * breadth, breadth), breadth)
            parts = [line[:, n * BLOCK : (n + 1) * BLOCK] for n in range(blocks)]
            turned = [pltpu.roll(part, shard, 1) for part in parts]
            low = lanes < shard
            for z_at in range(2):
                left_of, right_of = (parts, turned) if z_at == 0 else (turned, parts)
                mid = jnp.concatenate(
                    [jnp.where(low, left_of[n], right_of[n + 1]) for n in range(0, blocks, 2)], axis=1
                )
                left = jnp.where(at == 0, 0.0, pltpu.roll(mid, 1, 0))
                right = jnp.where(at == breadth - 1, 0.0, pltpu.roll(mid, breadth - 1, 0))
                for dx, value in enumerate((left, mid, right)):
                    start = (3 * z_at + dx) * group
                    dst[rows, start : start + group] = value.astype(jnp.bfloat16)

    def half_dot(xs, z_at, pair, i):
        total = None
        for dy in range(3):
            start = pl.multiple_of(i * ROWS + dy * breadth, breadth)
            lhs = xs[pl.ds(start, ROWS), pl.ds(pl.multiple_of(z_at * (3 * group), 3 * group), 3 * group)]
            rhs = jnp.concatenate(
                [wb[j, z_at, 3 * dy : 3 * dy + 3].reshape(3 * group, BLOCK) for j in pair], axis=1
            )
            part = jnp.dot(lhs, rhs, preferred_element_type=jnp.float32)
            total = part if total is None else total + part
        return total

    def activate(total, pair):
        total = total + jnp.concatenate([sb_ref[j] for j in pair], axis=1)
        return (total / (1.0 + jnp.exp(-total))).astype(jnp.bfloat16)

    pairs = (block_a, block_b), (block_c, block_d)

    def spatial_first(p, i):
        acc[rows_of(i), 2 * BLOCK * p : 2 * BLOCK * (p + 1)] = half_dot(xcat, zh, pairs[p], i)

    def spatial_rest(p, i):
        total = acc[rows_of(i), 2 * BLOCK * p : 2 * BLOCK * (p + 1)] + half_dot(xcat, 1 - zh, pairs[p], i)
        hidden = activate(total, pairs[p])
        for n, j in enumerate(pairs[p]):
            own[j % 2, j // 2, rows_of(i), :] = hidden[:, n * BLOCK : (n + 1) * BLOCK]

    @pl.when(jnp.logical_and(is_one, edge))
    def _():
        for g in (0, 1, 3, 2):
            start_z(g)

    @pl.when(is_zero)
    def _():
        start_y(0, source(0))
        start_y(1, source(1))
        pl.when(edge)(lambda: start_y(3, source(3)))

    @pl.when(far_any)
    def _():
        to_relay().start()
        far_upper().start()
        far_lower().start()


    zeros = jnp.zeros((breadth, 6 * group), jnp.bfloat16)
    xcat[0:breadth, :] = zeros
    xcat[breadth + pixels :, :] = zeros
    vid_copy.wait()
    prepare(outv, xcat, height)
    for load in loads:
        load.wait()

    @pl.when(is_zero)
    def _():
        stage_y(0)
        stage_y(1)
        relay_pass(1)
        stage_far(0)
        stage_far(1)

    @pl.when(is_one)
    def _():
        stage_z(0)
        stage_z(1)
        relay_pass(1)
        stage_y(0)
        stage_y(1)
        pl.when(edge)(lambda: stage_z(3))
        stage_done(0, (1, 2, 3))
        stage_done(1, (1, 2, 3))

    relay_pass(2)
    relay_pass(3)
    edge_zero, edge_one = jnp.logical_and(edge, is_zero), jnp.logical_and(edge, is_one)
    sharing = jnp.logical_and(is_one, inner_source_of_two)

    def on(flag, n, at, *stages):
        @pl.when(jnp.logical_and(flag, n == at))
        def _():
            for stage in stages:
                stage()

    @pl.loop(0, chunks)
    def _(n):
        spatial_first(0, chunks - 1 - n)
        on(is_zero, n, 1, lambda: stage_x(3))
        on(is_zero, n, 2, lambda: stage_x(1))
        on(is_zero, n, 3, lambda: stage_x(2))
        on(is_one, n, 0, lambda: stage_far(0))
        on(is_one, n, 1, lambda: stage_far(1))
        on(edge_zero, n, 0, lambda: stage_y(3))
        on(edge_one, n, 2, lambda: stage_y(3))
        on(is_zero, n, 2, lambda: start_y(2, source(2)))
        on(edge_zero, n, 3, lambda: stage_far(3))
        on(sharing, n, 3, stage_share)

    @pl.when(is_zero)
    def _():
        stage_done(0, range(4))
        stage_done(1, range(4))

    @pl.loop(0, chunks)
    def _(n):
        spatial_rest(0, chunks - 1 - n)

        @pl.when(n > 0)
        def _():
            send_hidden(0, chunks - n)

        on(is_one, n, 0, lambda: stage_x(0))
        on(is_one, n, 1, lambda: stage_x(3))
        on(edge_one, n, 0, lambda: stage_far(3))
        on(is_one, n, 2, lambda: stage_x(1))
        on(is_one, n, 3, lambda: stage_z(2))

    pl.when(is_one)(lambda: stage_x_done((1, 2, 3)))

    @pl.loop(0, chunks)
    def _(n):
        spatial_first(1, chunks - 1 - n)

        @pl.when(n == 0)
        def _():
            send_hidden(0, 0)

        on(is_one, n, 0, lambda: stage_x(2))
        on(is_zero, n, 2, lambda: stage_y(2))

    pl.when(is_zero)(lambda: stage_x_done(range(4)))

    @pl.loop(0, chunks)
    def _(n):
        spatial_rest(1, chunks - 1 - n)

        @pl.when(n > 0)
        def _():
            send_hidden(1, chunks - n)

        on(far_any, n, 1, lambda: far_upper().wait_recv(), lambda: hand_row().start())
        on(aid_any, n, 0, lambda: far_lower().wait_recv(), lambda: hand_row().start())
        on(is_one, n, 0, lambda: stage_y(2))

    stage_far(2)
    send_hidden(1, 0)

    def made_copy(q, i):
        rows = rows_of(i + FAR_CHUNKS)
        return remote(
            made.at[q, :, rows_of(i), :], near.at[far_side, q, :, rows, :], csend.at[0], crecv.at[i], dp, partner
        )

    def far_step(n):
        p, i = n // FAR_CHUNKS, n % FAR_CHUNKS
        return (x + p) % 2, i

    @pl.when(far_any)
    def _():
        far_upper().wait_send()
        far_lower().wait_send()
        to_relay().wait_send()

    @pl.when(aid_any)
    def _():
        from_relay(0, partner).wait_recv()

    @pl.when(team)
    def _():
        hand_row().wait()
        blank = jnp.where(far_any, 0, far_rows)
        xcat_far[pl.ds(pl.multiple_of(blank, breadth), breadth), :] = zeros
        prepare(vid_far, xcat_far, far_rows // breadth, one(far_any))

        @pl.loop(0, 2 * FAR_CHUNKS)
        def _(n):
            p, i = n // FAR_CHUNKS, n % FAR_CHUNKS
            pair = ((x + p) % 4, (x + p + 2) % 4)
            hidden = activate(half_dot(xcat_far, 0, pair, i) + half_dot(xcat_far, 1, pair, i), pair)

            @pl.when(far_any)
            def _():
                for m, j in enumerate(pair):
                    near[far_side, j % 2, j // 2, rows_of(i), :] = hidden[:, m * BLOCK : (m + 1) * BLOCK]

            @pl.when(aid_any)
            def _():
                for m, j in enumerate(pair):
                    made[j % 2, j // 2, rows_of(i), :] = hidden[:, m * BLOCK : (m + 1) * BLOCK]

            pl.when(jnp.logical_and(aid_any, n > 0))(lambda: made_copy(*far_step(n - 1)).start())

    pl.when(is_zero)(lambda: stage_done(2, range(4)))
    pl.when(is_one)(lambda: stage_done(2, (1, 2, 3)))

    def taps(lag, j):
        return wt[lag, columns(j), :]

    def temporal(lag, ref, q, i):
        lhs = jnp.concatenate([ref[q, m, rows_of(i), :] for m in range(2)], axis=1)
        rhs = jnp.concatenate([taps(lag, q), taps(lag, q + 2)], axis=0)
        return jnp.dot(lhs, rhs, preferred_element_type=jnp.float32)

    @pl.when(jnp.logical_not(team))
    def _():
        @pl.loop(0, chunks)
        def _(n):
            acc[rows_of(n), :] = temporal(1, own, 0, n) + temporal(1, own, 1, n) + tb_ref[...]

    pl.when(aid_any)(lambda: made_copy(*far_step(2 * FAR_CHUNKS - 1)).start())
    wait_sends()

    @pl.when(is_relay)
    def _():
        for n in range(FLOWS):
            from_relay(n, partner).wait_send()

    there, x_there = (has_before, has_after), ((t + tiles - 1) % tiles // 8, (t + 1) % tiles // 8)

    def exchange_rest(chip, z):
        for p in range(2):
            @pl.loop(0, chunks)
            def _(n, p=p):
                i = chunks - 1 - n
                rows = rows_of(i)
                q = (x_there[chip] + p) % 2
                hcopy(q, i, 1 - chip).wait_recv()
                acc[rows, :] += temporal(2 * chip, near.at[chip], q, i)

                @pl.when(there[z])
                def _():
                    q = (x_there[z] + p) % 2
                    hcopy(q, i, 1 - z).wait_recv()
                    total = acc[rows, :] + temporal(2 * z, near.at[z], q, i)
                    if p == 0:
                        acc[rows, :] = total
                    else:
                        outv[rows, :] = total.astype(jnp.bfloat16)

                if p == 1:
                    @pl.when(jnp.logical_not(there[z]))
                    def _():
                        outv[rows, :] = acc[rows, :].astype(jnp.bfloat16)

    pl.when(jnp.logical_and(jnp.logical_not(team), is_zero))(lambda: exchange_rest(1, 0))
    pl.when(jnp.logical_and(jnp.logical_not(team), is_one))(lambda: exchange_rest(0, 1))

    @pl.when(aid_any)
    def _():
        z_side = jnp.where(aid_before, 1, 0)
        q_first = jnp.where(aid_before, x_there[1], x_there[0]) % 2

        @pl.loop(0, chunks)
        def _(n):
            i = chunks - 1 - n

            @pl.when(aid_before)
            def _():
                hcopy(q_first, i, 0).wait_recv()
                for q in range(2):
                    hcopy(q, i, 1).wait_recv()

            @pl.when(aid_after)
            def _():
                hcopy(q_first, i, 1).wait_recv()
                for q in range(2):
                    hcopy(q, i, 0).wait_recv()

            total = tb_ref[...] + temporal(2 * z_side, near.at[z_side], q_first, i)
            for q in range(2):
                total = total + temporal(1, own, q, i) + temporal(2 - 2 * z_side, near.at[1 - z_side], q, i)
            acc[rows_of(i), :] = total

        @pl.loop(0, chunks)
        def _(n):
            i = chunks - 1 - n
            pl.when(aid_before)(lambda: hcopy(1 - q_first, i, 0).wait_recv())
            pl.when(aid_after)(lambda: hcopy(1 - q_first, i, 1).wait_recv())
            rest = temporal(2 * z_side, near.at[z_side], 1 - q_first, i)
            outv[rows_of(i), :] = (acc[rows_of(i), :] + rest).astype(jnp.bfloat16)

    @pl.when(far_any)
    def _():
        @pl.loop(0, chunks)
        def _(i):
            pl.when(far_before)(lambda: [hcopy(q, i, 0).wait_recv() for q in range(2)] and None)
            pl.when(far_after)(lambda: [hcopy(q, i, 1).wait_recv() for q in range(2)] and None)

            @pl.when(i >= FAR_CHUNKS)
            def _():
                both = made.at[:, :, rows_of(i - FAR_CHUNKS), :]
                remote(both, both, csend.at[0], crecv.at[i - FAR_CHUNKS], dp, partner).wait_recv()

            total = tb_ref[...]
            for q in range(2):
                total = total + temporal(1, own, q, i)
                for side in range(2):
                    total = total + temporal(2 * side, near.at[side], q, i)
            outv[rows_of(i), :] = total.astype(jnp.bfloat16)

    for side in range(2):
        @pl.when(exchanged(side))
        def _():
            remote(own, near.at[1 - side], hsend.at[side], hrecv.at[side, 0], dp, partner).wait_send()

    @pl.when(aid_any)
    def _():
        remote(made, made, csend.at[0], crecv.at[0], dp, partner).wait_send()


def per_device(videos, spatial_filter, temporal_filter, spatial_bias, temporal_bias):
    _, _, height, breadth, chans = videos.shape
    shard = spatial_filter.shape[1]
    pixels = height * breadth
    blocks = chans // BLOCK
    chunks = pixels // ROWS
    far_pixels = FAR_CHUNKS * ROWS + breadth
    bf = jnp.bfloat16
    anywhere = pl.BlockSpec(memory_space=pl.ANY)
    vmem = pl.BlockSpec(memory_space=pltpu.VMEM)
    dma = pltpu.SemaphoreType.DMA
    out = pl.pallas_call(
        functools.partial(kernel, (height, breadth, chans, shard)),
        out_shape=pltpu.VMEM((pixels, chans), bf),
        in_specs=[anywhere] * 5,
        out_specs=vmem,
        scratch_shapes=[
            pltpu.VMEM((pixels + 2 * breadth, 3 * chans), bf),
            pltpu.VMEM((far_pixels + breadth, 3 * chans), bf),
            pltpu.VMEM((far_pixels, chans), bf),
            pltpu.VMEM((FLOWS, RELAYED * breadth, chans), bf),
            pltpu.VMEM((2, blocks // 2, FAR_CHUNKS * ROWS, BLOCK), bf),
            pltpu.VMEM((blocks, 2, TAPS_S, chans // 2, BLOCK), bf),
            pltpu.VMEM((TAPS_T, chans, chans), bf),
            pltpu.VMEM((2, blocks // 2, pixels, BLOCK), bf),
            pltpu.VMEM((2, 2, blocks // 2, pixels, BLOCK), bf),
            pltpu.VMEM((pixels, chans), jnp.float32),
            pltpu.VMEM((blocks, 1, BLOCK), jnp.float32),
            pltpu.VMEM((1, chans), jnp.float32),
            dma((8,)),
            dma((4, 4)), dma((4, 5)),
            dma((2,)), dma((2, 4)),
            dma((2,)), dma((2,)),
            dma((2,)), dma((2, 2 * chunks)),
            dma((2, 4)),
            dma((2, FLOWS)),
            dma((1,)), dma((FAR_CHUNKS,)),
        ],
        compiler_params=pltpu.CompilerParams(
            collective_id=0, has_side_effects=True, vmem_limit_bytes=56 * 1024 * 1024
        ),
    )(
        videos.reshape(pixels, chans),
        spatial_filter,
        temporal_filter,
        spatial_bias.reshape(blocks, 1, BLOCK),
        temporal_bias.reshape(1, chans),
    )
    return out.reshape(videos.shape)


def solution(mesh):
    return jax.shard_map(
        per_device,
        mesh=mesh,
        in_specs=(
            P("dp", "tile", None, None, None),
            P(None, "dp", None),
            P(None, "dp", None),
            P(),
            P(),
        ),
        out_specs=P("dp", "tile", None, None, None),
        check_vma=False,
    )
```
